32 devices in a mesh: blk: 4 (over x, core), smp: 8 (over z, y).
Axes of the slice: x: 2, y: 2, z: 4, core: 2. Of those that a mesh axis runs over, the one named last changes fastest.
Arguments:
- scaled_genotype_counts: bfloat16 [16384, 2048], P('smp', 'blk'), may hold values from -6 to 6
- adjusted_trait_scores: bfloat16 [16384, 8], P('smp'), may hold values from -6 to 6
- subset_membership: int32 [16384], P('smp'), may hold values from 0 to 4, as said below
- regularizer_lambdas: float32 [2], replicated, may hold values from 0.01 to 0.1
- unseen_subset_guesses: bfloat16 [8, 2048, 8, 8], P('smp', 'blk'), may hold values from -6 to 6
Outputs:
- oof: bfloat16 [16384, 8, 8], P('smp', None, 'blk')
- cross: float32 [8, 8, 16], P(None, 'blk', 'smp')
The draws below stay inside these ranges and needn't reach their ends.
Inputs may be any that keep to these rules, and one draw needn't show every extreme that they name: `subset_membership`: every fold holds some samples.
All inputs are finite; a program needn't handle non-finite values.
Results may differ from the reference program's by a relative error of at most 0.0047.
Values may be sent and summed in bfloat16 or wider, within the bound.
No kernel may reach another device: no remote copies, remote signals or barrier semaphores. Data moves between devices by JAX's collectives and lax.ppermute only.
A program may use at most 128 MiB of HBM per device.

```python
import math
import jax
import jax.numpy as jnp
from jax import lax

BLOCK = 512
PHENOTYPIC_MEASURES = 8
FOLDS = 5
SHRINK_STRENGTH = 2
PER_DEVICE_CASES = 2048
SAMPLES = 16384
VARIANTS = 2048
PRIOR_ESTIMATES = 8


def shared_factor(key):
    anchor = jax.random.fold_in(key, 9001)
    ancestry = jax.random.normal(jax.random.fold_in(anchor, 1), (SAMPLES,), jnp.float32)
    trait_load = jax.random.uniform(jax.random.fold_in(anchor, 2), (PHENOTYPIC_MEASURES,), jnp.float32, 0.15, 0.35)
    return (ancestry, trait_load)


def draw_scaled_genotype_counts(key, part):
    nblocks = VARIANTS // BLOCK
    cohorts = SAMPLES // PER_DEVICE_CASES
    ancestry, trait_load = shared_factor(key)
    anchor = jax.random.fold_in(key, 4711)
    low_gap, high_gap = (math.log(0.02), math.log(0.5))
    low_scale, high_scale = (math.log(0.4), math.log(2.5))
    mixing = 0.1
    spacing = jnp.exp(jax.random.uniform(jax.random.fold_in(anchor, 1), (cohorts, nblocks), jnp.float32, low_gap, high_gap))
    retain = 1.0 - spacing
    renewal = jnp.sqrt(1.0 - retain * retain)
    row_cohort = jnp.arange(SAMPLES, dtype=jnp.int32) // PER_DEVICE_CASES
    retain_rows = retain[row_cohort]
    renewal_rows = renewal[row_cohort]
    noise_key = jax.random.fold_in(anchor, 2)

    def advance(carry, position):
        fresh = jax.random.normal(jax.random.fold_in(noise_key, position), (SAMPLES, nblocks), jnp.float32)
        value = jnp.where(position == 0, fresh, retain_rows * carry + renewal_rows * fresh)
        return (value, value)
    _, trajectory = lax.scan(advance, jnp.zeros((SAMPLES, nblocks), jnp.float32), jnp.arange(BLOCK, dtype=jnp.int32))
    chains = jnp.transpose(trajectory, (1, 2, 0))
    shuffles = jax.vmap(lambda subkey: jax.random.permutation(subkey, BLOCK))(jax.random.split(jax.random.fold_in(anchor, 3), nblocks))
    chains = jax.vmap(lambda block_values, columns: block_values[:, columns], in_axes=(1, 0), out_axes=1)(chains, shuffles)
    chains = chains.reshape(SAMPLES, VARIANTS)
    loading = jax.random.normal(jax.random.fold_in(anchor, 4), (VARIANTS,), jnp.float32)
    blended = math.sqrt(1.0 - mixing) * chains + math.sqrt(mixing) * ancestry[:, None] * loading[None, :]
    column_scale = jnp.exp(jax.random.uniform(jax.random.fold_in(anchor, 5), (cohorts, VARIANTS), jnp.float32, low_scale, high_scale))
    column_scale = column_scale / jnp.sqrt(jnp.mean(column_scale * column_scale, axis=0, keepdims=True))
    scaled = blended.reshape(cohorts, PER_DEVICE_CASES, VARIANTS) * column_scale[:, None, :]
    return jnp.clip(scaled.reshape(SAMPLES, VARIANTS), -6.0, 6.0).astype(jnp.bfloat16)


def draw_adjusted_trait_scores(key, part):
    ancestry, trait_load = shared_factor(key)
    noise_key = jax.random.fold_in(key, 5813)
    noise = jax.random.normal(noise_key, (SAMPLES, PHENOTYPIC_MEASURES), jnp.float32)
    shared_part = trait_load
    value = shared_part[None, :] * ancestry[:, None] + jnp.sqrt(1.0 - shared_part * shared_part)[None, :] * noise
    return jnp.clip(value, -6.0, 6.0).astype(jnp.bfloat16)


def draw_subset_membership(key, part):
    anchor = jax.random.fold_in(key, 3307)
    reach = SAMPLES // (4 * FOLDS)
    jitter = jax.random.randint(jax.random.fold_in(anchor, 1), (FOLDS - 1,), -reach, reach + 1, dtype=jnp.int32)
    bounds = jnp.arange(1, FOLDS, dtype=jnp.int32) * SAMPLES // FOLDS + jitter
    position = jnp.arange(SAMPLES, dtype=jnp.int32)
    contiguous = jnp.sum((position[:, None] >= bounds[None, :]).astype(jnp.int32), axis=1)
    stray = jax.random.randint(jax.random.fold_in(anchor, 2), (SAMPLES,), 0, 8, dtype=jnp.int32) == 0
    elsewhere = jax.random.randint(jax.random.fold_in(anchor, 3), (SAMPLES,), 0, FOLDS, dtype=jnp.int32)
    return jnp.where(stray, elsewhere, contiguous).astype(jnp.int32)


def draw_unseen_subset_guesses(key, part):
    ancestry, trait_load = shared_factor(key)
    anchor = jax.random.fold_in(key, 6151)
    feature_load = jax.random.uniform(jax.random.fold_in(anchor, 1), (PRIOR_ESTIMATES,), jnp.float32, 0.5, 1.5)
    noise_key = jax.random.fold_in(anchor, 2)
    noise = jax.random.normal(noise_key, (SAMPLES, PHENOTYPIC_MEASURES, PRIOR_ESTIMATES), jnp.float32)
    strength = 4.0
    value = strength * trait_load[None, :, None] * feature_load[None, None, :] * ancestry[:, None, None] + noise
    value = jnp.clip(value, -6.0, 6.0)
    cohorts = SAMPLES // PER_DEVICE_CASES
    return value.reshape(cohorts, PER_DEVICE_CASES, PHENOTYPIC_MEASURES, PRIOR_ESTIMATES).astype(jnp.bfloat16)


def setup_inputs(seed: int = 0) -> dict:
    keys = jax.random.split(jax.random.key(seed), 6)
    scaled_genotype_counts = draw_scaled_genotype_counts(jax.random.fold_in(keys[5], 71), 0)
    adjusted_trait_scores = draw_adjusted_trait_scores(jax.random.fold_in(keys[5], 71), 0)
    subset_membership = draw_subset_membership(jax.random.fold_in(keys[5], 71), 0)
    regularizer_lambdas = jnp.clip(jnp.exp(jax.random.uniform(keys[3], (SHRINK_STRENGTH,), jnp.float32, math.log(0.01), math.log(0.1))), 0.01, 0.1)
    unseen_subset_guesses = draw_unseen_subset_guesses(jax.random.fold_in(keys[5], 71), 0)
    return dict(scaled_genotype_counts=scaled_genotype_counts, adjusted_trait_scores=adjusted_trait_scores, subset_membership=subset_membership, regularizer_lambdas=regularizer_lambdas, unseen_subset_guesses=unseen_subset_guesses)


def train_locus_group(locus_group_span, adjusted_trait_scores, partition_indicator, regularizer_lambdas, person_entries):
    masked_values = locus_group_span.astype(jnp.float32)[:, None, :] * partition_indicator.astype(jnp.float32)[:, :, None]
    inner_covariance_stack = jnp.einsum('rpe,ro->peo', masked_values, locus_group_span.astype(jnp.float32), precision=lax.Precision.HIGHEST)
    pairwise_interaction_features = jnp.einsum('jdx,jr->dxr', masked_values, adjusted_trait_scores.astype(jnp.float32), precision=lax.Precision.HIGHEST)
    normal_equation_stack = lax.optimization_barrier(jnp.sum(inner_covariance_stack, axis=0))[None] - inner_covariance_stack
    equation_targets = lax.optimization_barrier(jnp.sum(pairwise_interaction_features, axis=0))[None] - pairwise_interaction_features
    unit_diagonal = jnp.eye(BLOCK, dtype=jnp.float32)
    solved = []
    for position_number in range(SHRINK_STRENGTH):
        regressor_array = normal_equation_stack + regularizer_lambdas[position_number] * person_entries * unit_diagonal
        factor = jnp.linalg.cholesky(regressor_array)
        solved.append(jax.vmap(lambda c, b: jax.scipy.linalg.cho_solve((c, True), b))(factor, equation_targets))
    weight_array = jnp.stack(solved, axis=-1)
    coeffs_half = jnp.transpose(weight_array, (1, 0, 2, 3)).astype(jnp.bfloat16)
    fitted = jnp.dot(locus_group_span.astype(jnp.float32), coeffs_half.reshape(BLOCK, -1).astype(jnp.float32), preferred_element_type=jnp.float32)
    fitted = fitted.reshape(locus_group_span.shape[0], FOLDS, PHENOTYPIC_MEASURES, SHRINK_STRENGTH)
    chosen = lax.optimization_barrier(jnp.sum(fitted * partition_indicator.astype(jnp.float32)[:, :, None, None], axis=1))
    return (chosen * math.sqrt(person_entries / BLOCK)).astype(jnp.bfloat16)

def reference(scaled_genotype_counts, adjusted_trait_scores, subset_membership, regularizer_lambdas, unseen_subset_guesses):
    person_entries = scaled_genotype_counts.shape[0]
    nblocks = scaled_genotype_counts.shape[1] // BLOCK
    partition_indicator = (subset_membership[:, None] == jnp.arange(FOLDS, dtype=jnp.int32)[None, :]).astype(jnp.bfloat16)

    def one_block(position_number):
        locus_group_span = lax.dynamic_slice_in_dim(scaled_genotype_counts, position_number * BLOCK, BLOCK, 1)
        return train_locus_group(locus_group_span, adjusted_trait_scores, partition_indicator, regularizer_lambdas, person_entries)
    fitted = lax.map(one_block, jnp.arange(nblocks, dtype=jnp.int32))
    oof = jnp.transpose(fitted, (1, 2, 0, 3)).reshape(person_entries, PHENOTYPIC_MEASURES, nblocks * SHRINK_STRENGTH)
    preceding = unseen_subset_guesses.reshape(person_entries, PHENOTYPIC_MEASURES, unseen_subset_guesses.shape[-1])
    joined = jnp.concatenate([preceding, oof], axis=2)
    cross = jnp.einsum('stf,stc->tfc', oof.astype(jnp.float32), joined.astype(jnp.float32), precision=lax.Precision.HIGHEST) / person_entries
    return (oof, cross)
```

```python
import math

import jax
import jax.numpy as jnp
from jax import lax
from jax.experimental import pallas as pl
from jax.experimental.pallas import tpu as pltpu
from jax.sharding import PartitionSpec as P

BLOCK = 512
PHENOTYPIC_MEASURES = 8
FOLDS = 5
SHRINK_STRENGTH = 2

LANES = 128
TILE = 8
HALF = 64
PACKED = 272
WIRE = 288
DIGIT = 32766.0
BOUND = 36.0
OWNERS = (0, 2, 3, 4, 6)

f32 = jnp.float32
bf16 = jnp.bfloat16
VMEM = pl.BlockSpec(memory_space=pltpu.VMEM)
SMEM = pl.BlockSpec(memory_space=pltpu.SMEM)
PARAMS = pltpu.CompilerParams(vmem_limit_bytes=60 * 1024 * 1024)


def mm(a, b, precision=lax.Precision.HIGHEST):
    return lax.dot_general(a, b, (((1,), (0,)), ((), ())), precision=precision, preferred_element_type=f32)


def nt(a, b, precision=None):
    return lax.dot_general(a, b, (((1,), (1,)), ((), ())), precision=precision, preferred_element_type=f32)


def iota(shape, dim):
    return lax.broadcasted_iota(jnp.int32, shape, dim)


def square_masks():
    row, col = iota((LANES, LANES), 0), iota((LANES, LANES), 1)
    return row == col, col < row


def column(row_vector, eye):
    return jnp.sum(jnp.where(eye, jnp.broadcast_to(row_vector, (LANES, LANES)), 0.0), axis=1, keepdims=True)


LAYOUT = (((0, 1), (1, 0), (2, 3), (3, 2)), ((2, 0), (2, 1), (3, 0), (3, 1)))


def place(r, c):
    return slice(r * LANES, (r + 1) * LANES), slice(c * LANES, (c + 1) * LANES)


def pair_scale(r, c, rows, cols, low):
    i, j = LAYOUT[r][c]
    if (r, c) in ((0, 0), (0, 2)):
        return jnp.where(low, cols[i] * rows[i], cols[j] * rows[j])
    return cols[i] * rows[j]


def split(vector):
    return [vector[:, i * LANES : (i + 1) * LANES] for i in range(BLOCK // LANES)]


def to_int(x):
    return jnp.floor(x + 0.5).astype(jnp.int32).astype(jnp.int16)


def digits(value, bound):
    u = value * (DIGIT / bound)
    high = jnp.floor(u)
    return high, (u - high) * DIGIT


def undigits(high, low, bound):
    return (high + low * (1.0 / DIGIT)) * (bound / DIGIT)


def encode(get, msg_ref, bound, eye, low):
    diag = get(slice(264, 265), slice(0, BLOCK))
    dh, dl = digits(diag, bound)
    dl = jnp.floor(dl + 0.5)
    scale = lax.rsqrt(undigits(dh, dl, bound) + 1e-3)
    rows = split(scale)
    cols = [column(r, eye) for r in rows]
    for r in range(2):
        for c in range(4):
            rs, cs = place(r, c)
            msg_ref[rs, cs] = to_int(get(rs, cs) * (pair_scale(r, c, rows, cols, low) * DIGIT))
    xh, xl = digits(get(slice(256, 264), slice(0, BLOCK)), bound)
    msg_ref[256:272, :] = to_int(jnp.concatenate([xh, xl], axis=0))
    spare = jnp.zeros((14, BLOCK), f32)
    msg_ref[272:288, :] = to_int(jnp.concatenate([dh, dl, spare], axis=0))


def decode(msg_ref, bound, eye, low):
    tail = msg_ref[272:288, :].astype(f32)
    diag = undigits(tail[0:1], tail[1:2], bound)
    scale = jnp.sqrt(diag + 1e-3)
    rows = split(scale)
    cols = [column(r, eye) for r in rows]

    def matrix(r, c):
        rs, cs = place(r, c)
        return msg_ref[rs, cs].astype(f32) * (pair_scale(r, c, rows, cols, low) * (1.0 / DIGIT))

    def rest():
        x = msg_ref[256:272, :].astype(f32)
        return undigits(x[0:8], x[8:16], bound), diag

    return matrix, rest


def add_message(dst_ref, src_ref, msg_ref, bound, eye, low):
    matrix, rest = decode(msg_ref, bound, eye, low)
    for r in range(2):
        for c in range(4):
            rs, cs = place(r, c)
            dst_ref[rs, cs] = src_ref[rs, cs] + matrix(r, c)
    xy, diag = rest()
    dst_ref[256:264, :] = src_ref[256:264, :] + xy
    dst_ref[264:272, :] = src_ref[264:272, :] + jnp.concatenate([diag, jnp.zeros((7, BLOCK), f32)], axis=0)


def reader(ref):
    return lambda rows, cols: ref[rows, cols]


def gram_one(fold, x_ref, xt_ref, f_ref, out_ref, eye, low):
    mask = jnp.where(f_ref[...] != fold, 1.0, 0.0).astype(bf16)
    g0 = jnp.dot(xt_ref[0:256, :] * mask, x_ref[:, 0:256], preferred_element_type=f32)
    g1 = jnp.dot(xt_ref[256:528, :] * mask, x_ref[...], preferred_element_type=f32)

    def block(i, j):
        rs, cs = place(i, j)
        return g0[rs, cs] if i < 2 else g1[(i - 2) * LANES : (i - 1) * LANES, cs]

    for r in range(2):
        for c in range(4):
            i, j = LAYOUT[r][c]
            rs, cs = place(r, c)
            if (r, c) in ((0, 0), (0, 2)):
                out_ref[rs, cs] = jnp.where(low, block(i, i), jnp.where(eye, 0.0, block(j, j)))
            else:
                out_ref[rs, cs] = block(i, j)
    diag = [jnp.sum(jnp.where(eye, block(i, i), 0.0), axis=0, keepdims=True) for i in range(4)]
    out_ref[256:264, :] = g1[256:264, :]
    out_ref[264:272, :] = jnp.concatenate([jnp.concatenate(diag, axis=1), jnp.zeros((7, BLOCK), f32)], axis=0)


def load_transposed(x_ref, yt_ref, xt_ref):
    xt_ref[0:BLOCK, :] = x_ref[...].T
    xt_ref[BLOCK : BLOCK + 16, :] = jnp.concatenate([yt_ref[...], jnp.zeros_like(yt_ref[...])], axis=0)


def gram_send_kernel(info_ref, x_ref, yt_ref, f_ref, msg_ref, keep_ref, xt_ref, work_ref, *, bound):
    eye, low = square_masks()
    load_transposed(x_ref, yt_ref, xt_ref)
    for slot, dst in ((0, work_ref), (1, keep_ref), (3, work_ref)):
        gram_one(info_ref[slot], x_ref, xt_ref, f_ref, dst, eye, low)
        encode(reader(dst), msg_ref.at[{0: 0, 1: 1, 3: 2}[slot]], bound, eye, low)


def gram_keep_kernel(info_ref, x_ref, yt_ref, f_ref, keep_ref, xt_ref):
    eye, low = square_masks()
    load_transposed(x_ref, yt_ref, xt_ref)
    for n, slot in enumerate((2, 4)):
        gram_one(info_ref[slot], x_ref, xt_ref, f_ref, keep_ref.at[n], eye, low)


def second_kernel(info_ref, k1_ref, k24_ref, p1_ref, p2_ref, p3_ref, msg_ref, keep_ref, s1_ref, s2_ref, *, bound):
    eye, low = square_masks()
    add_message(s2_ref, k24_ref.at[0], p1_ref, bound, eye, low)
    add_message(s1_ref, k1_ref, p2_ref, bound, eye, low)
    add_message(keep_ref.at[1], k24_ref.at[1], p3_ref, bound, eye, low)
    first = info_ref[5] == 1
    encode(lambda r, c: jnp.where(first, s1_ref[r, c], s2_ref[r, c]), msg_ref.at[0], bound, eye, low)
    encode(reader(keep_ref.at[1]), msg_ref.at[1], bound, eye, low)
    keep_ref[0] = jnp.where(first, s2_ref[...], s1_ref[...])


def third_kernel(info_ref, k_ref, p4_ref, p5_ref, msg_ref, keep_ref, sa_ref, sb_ref, *, bound):
    eye, low = square_masks()
    add_message(sa_ref, k_ref.at[0], p4_ref, bound, eye, low)
    add_message(sb_ref, k_ref.at[1], p5_ref, bound, eye, low)
    upper = info_ref[6] == 1
    encode(lambda r, c: jnp.where(upper, sa_ref[r, c], sb_ref[r, c]), msg_ref, bound, eye, low)
    keep_ref[...] = jnp.where(upper, sb_ref[...], sa_ref[...])


def sublane(x, p):
    return jnp.broadcast_to(x[p : p + 1, :], (TILE, LANES))


def tree(terms):
    terms = list(terms)
    while len(terms) > 1:
        terms = [terms[i] + terms[i + 1] if i + 1 < len(terms) else terms[i] for i in range(0, len(terms), 2)]
    return terms[0]


def invert_pair(tiles):
    lane, sub = iota((TILE, LANES), 1), iota((TILE, LANES), 0)
    col = lane % HALF
    half = lane - col
    here = [sub == p for p in range(TILE)]
    tiles = list(tiles)
    count = len(tiles)
    for g in range(count):
        inside = (col >= g * TILE) & (col < (g + 1) * TILE)
        index = [half + (g * TILE + q) for q in range(TILE)]

        def spread(t, q):
            return jnp.take_along_axis(t, index[q], axis=1)

        c = [spread(tiles[g], q) for q in range(TILE)]
        r = jnp.where(inside, jnp.where(col - g * TILE == sub, 1.0, 0.0), tiles[g])
        for p in range(0, TILE, 2):
            cp, cn = c[p], c[p + 1]
            a, b, d = sublane(cp, p), sublane(cp, p + 1), sublane(cn, p + 1)
            inv = 1.0 / (a * d - b * b)

            def eliminate(x):
                e0, e1 = sublane(x, p), sublane(x, p + 1)
                f0, f1 = d * e0 - b * e1, a * e1 - b * e0
                return jnp.where(here[p], f0 * inv, jnp.where(here[p + 1], f1 * inv, x - (cp * f0 + cn * f1) * inv))

            for q in range(p + 2, TILE):
                c[q] = eliminate(c[q])
            r = eliminate(r)
        rows = [sublane(r, p) for p in range(TILE)]
        for i in [(g + 1) % count] + [i for i in range(count) if i != g and i != (g + 1) % count]:
            t = tiles[i]
            tiles[i] = jnp.where(inside, 0.0, t) - tree([spread(t, p) * rows[p] for p in range(TILE)])
        tiles[g] = r
    return tiles


def block_diagonal(t):
    left = iota(t.shape, 1) < HALF
    return jnp.concatenate([jnp.where(left, t, 0.0), jnp.where(left, 0.0, t)], axis=0)


def solve_kernel(shift_ref, k_ref, p_ref, o_ref, m_ref, w_ref, x_ref, *, bound):
    eye, low = square_masks()
    matrix, rest = decode(p_ref, bound, eye, low)
    n = BLOCK

    def put(rows, t, c):
        u = pltpu.roll(t, HALF, 1)
        left = iota(t.shape, 1) < HALF
        m_ref[rows, 2 * c * LANES : (2 * c + 1) * LANES] = jnp.where(left, t, u)
        m_ref[rows, (2 * c + 1) * LANES : (2 * c + 2) * LANES] = jnp.where(left, u, t)

    xy, extra = rest()
    diag = split(k_ref[264:265, :] + extra)
    for r in range(2):
        for c in range(4):
            i, j = LAYOUT[r][c]
            t = k_ref[place(r, c)] + matrix(r, c)
            u = t.T
            if (r, c) in ((0, 0), (0, 2)):
                put(place(i, 0)[0], jnp.where(eye, diag[i], jnp.where(low, t, u)), i)
                put(place(j, 0)[0], jnp.where(eye, diag[j], jnp.where(low, u, t)), j)
            else:
                put(place(i, 0)[0], t, j)
                put(place(j, 0)[0], u, i)
    right = k_ref[256:264, :] + xy
    for c in range(4):
        put(slice(n, n + 8), right[:, c * LANES : (c + 1) * LANES], c)

    lane, sub = iota((HALF, LANES), 1), iota((HALF, LANES), 0)
    shift = jnp.where(lane % HALF == sub, jnp.where(lane < HALF, shift_ref[0], shift_ref[1]), 0.0)
    blocks = n // HALF
    for b in range(blocks):
        rs, cs = slice(b * HALF, (b + 1) * HALF), slice(b * LANES, (b + 1) * LANES)
        top = m_ref[rs, cs] + shift
        tiles = invert_pair([top[i * TILE : (i + 1) * TILE] for i in range(HALF // TILE)])
        inverse = block_diagonal(jnp.concatenate(tiles, axis=0))
        nx = (b + 1) * HALF
        w = mm(m_ref[nx:, cs], inverse)
        w_ref[nx:, cs] = w
        for j in range(b + 1, blocks):
            js = slice(j * LANES, (j + 1) * LANES)
            m_ref[nx:, js] = m_ref[nx:, js] - mm(w, block_diagonal(m_ref[rs, js]))
    for b in reversed(range(blocks)):
        cs = slice(b * LANES, (b + 1) * LANES)
        x = w_ref[n:, cs]
        if b + 1 < blocks:
            below = [block_diagonal(w_ref[i * HALF : (i + 1) * HALF, cs]) for i in range(b + 1, blocks)]
            x = x - mm(x_ref[:, (b + 1) * LANES :], jnp.concatenate(below, axis=0))
        x_ref[:, cs] = x
    left = iota((8, LANES), 1) < HALF
    for c in range(4):
        even, odd = x_ref[:, 2 * c * LANES : (2 * c + 1) * LANES], x_ref[:, (2 * c + 1) * LANES : (2 * c + 2) * LANES]
        first = jnp.where(left, even, pltpu.roll(odd, HALF, 1))
        second = jnp.where(left, pltpu.roll(even, HALF, 1), odd)
        o_ref[:, c * LANES : (c + 1) * LANES] = jnp.concatenate([first, second], axis=0).astype(bf16)


def predict_kernel(info_ref, x_ref, b_ref, f_ref, o_ref, *, scale):
    weights = jnp.concatenate([b_ref[info_ref[8 + k]] for k in range(FOLDS)], axis=0)
    fitted = nt(weights, x_ref[...])
    folds = f_ref[...]
    total = jnp.zeros((16, folds.shape[1]), f32)
    for k in range(FOLDS):
        total = jnp.where(folds == k, fitted[16 * k : 16 * (k + 1)], total)
    o_ref[...] = (total * scale).astype(bf16)


def cross_kernel(o_ref, j_ref, g_ref, c_ref, *, scale):
    own = o_ref[...]
    count, width = g_ref.shape[0], g_ref.shape[2]
    prior = g_ref.shape[1] // 8
    old = tree([nt(own[:, b * width : (b + 1) * width], g_ref[b]) for b in range(count)])
    new = nt(own, j_ref[...])
    t_row, t_old = iota(old.shape, 0) % 8, iota(old.shape, 1) // prior
    t_new = iota(new.shape, 1) % 8
    old = jnp.where(t_row == t_old, old, 0.0)
    new = jnp.where(iota(new.shape, 0) % 8 == t_new, new, 0.0)
    pick_old = jnp.where(iota((prior, old.shape[1]), 1) % prior == iota((prior, old.shape[1]), 0), 1.0, 0.0)
    features = new.shape[1] // 8
    pick_new = jnp.where(iota((features, new.shape[1]), 1) // 8 == iota((features, new.shape[1]), 0), 1.0, 0.0)
    high = lax.Precision.HIGHEST
    c_ref[0:prior, :] = nt(pick_old, old, high) * scale
    c_ref[prior : prior + features, :] = nt(pick_new, new, high) * scale


def make_local(mesh):
    n_blk, n_smp = mesh.shape["blk"], mesh.shape["smp"]
    if n_smp != 8:
        raise NotImplementedError(n_smp)

    def pairs(bit, sends):
        out = []
        for b in range(n_blk):
            for s in range(n_smp):
                role = s ^ (7 if b & 1 else 0)
                if sends(role & 1, role >> 1 & 1, role >> 2):
                    out.append((b * n_smp + s, b * n_smp + (s ^ bit)))
        return out

    def move(x, bit, sends):
        return lax.ppermute(x, ("blk", "smp"), pairs(bit, sends))

    def local(x, traits, folds, lambdas, guesses):
        rows = x.shape[0]
        total = rows * n_smp
        bound = BOUND * total
        mirror = 7 * (lax.axis_index("blk") & 1)
        role = lax.axis_index("smp") ^ mirror
        b0, b1, b2 = role & 1, role >> 1 & 1, role >> 2
        info = jnp.stack(
            [
                jnp.where(b0 == 0, 2, 0),
                jnp.int32(1) + 0 * b0,
                jnp.where(b0 == 0, 0, 2),
                jnp.where(b1 == 0, 4, 3),
                jnp.where(b1 == 0, 3, 4),
                jnp.where(b0 == b1, 1, 0),
                b2,
                b2,
            ]
            + [o ^ mirror for o in OWNERS]
            + [b2] * 3
        ).astype(jnp.int32)
        shift = lambdas * total
        yt = traits.T
        f_row = folds.reshape(1, rows)
        prior = jnp.transpose(guesses[0], (1, 2, 0)).reshape(-1, guesses.shape[1])

        def call(kernel, outs, specs, scratch, *args, **static):
            import functools

            return pl.pallas_call(
                functools.partial(kernel, **static),
                out_shape=outs,
                in_specs=specs,
                out_specs=jax.tree.map(lambda _: VMEM, outs),
                scratch_shapes=scratch,
                compiler_params=PARAMS,
            )(*args)

        def packed(*lead):
            return jax.ShapeDtypeStruct((*lead, PACKED, BLOCK), f32)

        def wire(*lead):
            return jax.ShapeDtypeStruct((*lead, WIRE, BLOCK), jnp.int16)

        xt = pltpu.VMEM((BLOCK + 16, rows), bf16)
        work = pltpu.VMEM((PACKED, BLOCK), f32)
        msg, k1 = call(
            gram_send_kernel, (wire(3), packed()), [SMEM, VMEM, VMEM, VMEM], [xt, work], info, x, yt, f_row, bound=bound
        )
        p1 = move(msg[0], 1, lambda u, v, w: True)
        p2 = move(msg[1], 1, lambda u, v, w: u == 1)
        p3 = move(msg[2], 2, lambda u, v, w: True)
        k24 = call(gram_keep_kernel, packed(2), [SMEM, VMEM, VMEM, VMEM], [xt], info, x, yt, f_row)
        msg, keep = call(
            second_kernel, (wire(2), packed(2)), [SMEM] + [VMEM] * 5, [work, work], info, k1, k24, p1, p2, p3, bound=bound
        )
        p4 = move(msg[0], 2, lambda u, v, w: (u, v) != (1, 1))
        p5 = move(msg[1], 1, lambda u, v, w: u == 1)
        msg, keep = call(
            third_kernel, (wire(), packed()), [SMEM] + [VMEM] * 3, [work, work], info, keep, p4, p5, bound=bound
        )
        p6 = move(msg, 4, lambda u, v, w: u == 0 or (u, v, w) == (1, 1, 1))
        beta = call(
            solve_kernel,
            jax.ShapeDtypeStruct((16, BLOCK), bf16),
            [SMEM, VMEM, VMEM],
            [pltpu.VMEM((BLOCK + 8, 2 * BLOCK), f32), pltpu.VMEM((BLOCK + 8, 2 * BLOCK), f32), pltpu.VMEM((8, 2 * BLOCK), f32)],
            shift,
            keep,
            p6,
            bound=bound,
        )
        betas = lax.all_to_all(jnp.broadcast_to(beta[None], (n_smp, 16, BLOCK)), "smp", 0, 0)
        oof = call(
            predict_kernel,
            jax.ShapeDtypeStruct((16, rows), bf16),
            [SMEM, VMEM, VMEM, VMEM],
            [],
            info,
            x,
            betas,
            f_row,
            scale=math.sqrt(total / BLOCK),
        )
        prior_all = lax.all_gather(prior, "blk", axis=0)
        oof_all = lax.all_gather(oof, "blk", axis=0, tiled=True)
        n_cross = prior.shape[0] // 8 + 2 * n_blk
        part = call(
            cross_kernel,
            jax.ShapeDtypeStruct((n_cross, 16), f32),
            [VMEM] * 3,
            [],
            oof,
            oof_all,
            prior_all,
            scale=1.0 / total,
        )
        part = lax.all_to_all(part.reshape(n_smp, n_cross // n_smp, 16), "smp", 0, 0)
        cross = jnp.sum(part, axis=0).reshape(n_cross // n_smp, 2, 8)
        return (
            jnp.transpose(oof.reshape(2, 8, rows), (2, 1, 0)),
            jnp.transpose(cross, (2, 1, 0)),
        )

    return local


def solution(mesh):
    return jax.shard_map(
        make_local(mesh),
        mesh=mesh,
        in_specs=(P("smp", "blk"), P("smp", None), P("smp"), P(), P("smp", "blk", None, None)),
        out_specs=(P("smp", None, "blk"), P(None, "blk", "smp")),
        check_vma=False,
    )
```

```python
import math

import jax
import jax.numpy as jnp
from jax import lax
from jax.experimental import pallas as pl
from jax.experimental.pallas import tpu as pltpu
from jax.sharding import PartitionSpec as P

BLOCK = 512
PHENOTYPIC_MEASURES = 8
FOLDS = 5
SHRINK_STRENGTH = 2

LANES = 128
TILE = 8
HALF = 64
PACKED = 272
WIRE = 288
DIGIT = 32766.0
BOUND = 36.0
OWNERS = (0, 2, 3, 4, 6)

f32 = jnp.float32
bf16 = jnp.bfloat16
VMEM = pl.BlockSpec(memory_space=pltpu.VMEM)
SMEM = pl.BlockSpec(memory_space=pltpu.SMEM)
PARAMS = pltpu.CompilerParams(vmem_limit_bytes=60 * 1024 * 1024)


def nt(a, b, precision=None):
    return lax.dot_general(a, b, (((1,), (1,)), ((), ())), precision=precision, preferred_element_type=f32)


def iota(shape, dim):
    return lax.broadcasted_iota(jnp.int32, shape, dim)


def square_masks():
    row, col = iota((LANES, LANES), 0), iota((LANES, LANES), 1)
    return row == col, col < row


def column(row_vector, eye):
    return jnp.sum(jnp.where(eye, jnp.broadcast_to(row_vector, (LANES, LANES)), 0.0), axis=1, keepdims=True)


LAYOUT = (((0, 1), (1, 0), (2, 3), (3, 2)), ((2, 0), (2, 1), (3, 0), (3, 1)))


def place(r, c):
    return slice(r * LANES, (r + 1) * LANES), slice(c * LANES, (c + 1) * LANES)


def pair_scale(r, c, rows, cols, low):
    i, j = LAYOUT[r][c]
    if (r, c) in ((0, 0), (0, 2)):
        return jnp.where(low, cols[i] * rows[i], cols[j] * rows[j])
    return cols[i] * rows[j]


def split(vector):
    return [vector[:, i * LANES : (i + 1) * LANES] for i in range(BLOCK // LANES)]


def to_int(x):
    return jnp.floor(x + 0.5).astype(jnp.int32).astype(jnp.int16)


def digits(value, bound):
    u = value * (DIGIT / bound)
    high = jnp.floor(u)
    return high, (u - high) * DIGIT


def undigits(high, low, bound):
    return (high + low * (1.0 / DIGIT)) * (bound / DIGIT)


def encode(get, msg_ref, bound, eye, low):
    diag = get(slice(264, 265), slice(0, BLOCK))
    dh, dl = digits(diag, bound)
    dl = jnp.floor(dl + 0.5)
    scale = lax.rsqrt(undigits(dh, dl, bound) + 1e-3)
    rows = split(scale)
    cols = [column(r, eye) for r in rows]
    for r in range(2):
        for c in range(4):
            rs, cs = place(r, c)
            msg_ref[rs, cs] = to_int(get(rs, cs) * (pair_scale(r, c, rows, cols, low) * DIGIT))
    xh, xl = digits(get(slice(256, 264), slice(0, BLOCK)), bound)
    msg_ref[256:272, :] = to_int(jnp.concatenate([xh, xl], axis=0))
    spare = jnp.zeros((14, BLOCK), f32)
    msg_ref[272:288, :] = to_int(jnp.concatenate([dh, dl, spare], axis=0))


def decode(msg_ref, bound, eye, low):
    tail = msg_ref[272:288, :].astype(f32)
    diag = undigits(tail[0:1], tail[1:2], bound)
    scale = jnp.sqrt(diag + 1e-3)
    rows = split(scale)
    cols = [column(r, eye) for r in rows]

    def matrix(r, c):
        rs, cs = place(r, c)
        return msg_ref[rs, cs].astype(f32) * (pair_scale(r, c, rows, cols, low) * (1.0 / DIGIT))

    def rest():
        x = msg_ref[256:272, :].astype(f32)
        return undigits(x[0:8], x[8:16], bound), diag

    return matrix, rest


def add_message(dst_ref, src_ref, msg_ref, bound, eye, low):
    matrix, rest = decode(msg_ref, bound, eye, low)
    for r in range(2):
        for c in range(4):
            rs, cs = place(r, c)
            dst_ref[rs, cs] = src_ref[rs, cs] + matrix(r, c)
    xy, diag = rest()
    dst_ref[256:264, :] = src_ref[256:264, :] + xy
    dst_ref[264:272, :] = src_ref[264:272, :] + jnp.concatenate([diag, jnp.zeros((7, BLOCK), f32)], axis=0)


def reader(ref):
    return lambda rows, cols: ref[rows, cols]


def gram_one(fold, x_ref, xt_ref, f_ref, out_ref, eye, low):
    mask = jnp.where(f_ref[...] != fold, 1.0, 0.0).astype(bf16)
    g0 = jnp.dot(xt_ref[0:256, :] * mask, x_ref[:, 0:256], preferred_element_type=f32)
    g1 = jnp.dot(xt_ref[256:528, :] * mask, x_ref[...], preferred_element_type=f32)

    def block(i, j):
        rs, cs = place(i, j)
        return g0[rs, cs] if i < 2 else g1[(i - 2) * LANES : (i - 1) * LANES, cs]

    for r in range(2):
        for c in range(4):
            i, j = LAYOUT[r][c]
            rs, cs = place(r, c)
            if (r, c) in ((0, 0), (0, 2)):
                out_ref[rs, cs] = jnp.where(low, block(i, i), jnp.where(eye, 0.0, block(j, j)))
            else:
                out_ref[rs, cs] = block(i, j)
    diag = [jnp.sum(jnp.where(eye, block(i, i), 0.0), axis=0, keepdims=True) for i in range(4)]
    out_ref[256:264, :] = g1[256:264, :]
    out_ref[264:272, :] = jnp.concatenate([jnp.concatenate(diag, axis=1), jnp.zeros((7, BLOCK), f32)], axis=0)


def load_transposed(x_ref, yt_ref, xt_ref):
    xt_ref[0:BLOCK, :] = x_ref[...].T
    xt_ref[BLOCK : BLOCK + 16, :] = jnp.concatenate([yt_ref[...], jnp.zeros_like(yt_ref[...])], axis=0)


def gram_send_kernel(info_ref, x_ref, yt_ref, f_ref, m0_ref, m1_ref, m3_ref, keep_ref, xt_ref, work_ref, *, bound):
    eye, low = square_masks()
    load_transposed(x_ref, yt_ref, xt_ref)
    for slot, dst, msg_ref in ((0, work_ref, m0_ref), (1, keep_ref, m1_ref), (3, work_ref, m3_ref)):
        gram_one(info_ref[slot], x_ref, xt_ref, f_ref, dst, eye, low)
        encode(reader(dst), msg_ref, bound, eye, low)


def gram_keep_kernel(info_ref, x_ref, yt_ref, f_ref, k2_ref, k4_ref, xt_ref):
    eye, low = square_masks()
    load_transposed(x_ref, yt_ref, xt_ref)
    for slot, dst in ((2, k2_ref), (4, k4_ref)):
        gram_one(info_ref[slot], x_ref, xt_ref, f_ref, dst, eye, low)


def second_kernel(
    info_ref, k1_ref, k2_ref, k4_ref, p1_ref, p2_ref, p3_ref, ma_ref, mb_ref, ka_ref, kb_ref, s1_ref, s2_ref, *, bound
):
    eye, low = square_masks()
    add_message(s2_ref, k2_ref, p1_ref, bound, eye, low)
    add_message(s1_ref, k1_ref, p2_ref, bound, eye, low)
    add_message(kb_ref, k4_ref, p3_ref, bound, eye, low)
    first = info_ref[5] == 1
    encode(lambda r, c: jnp.where(first, s1_ref[r, c], s2_ref[r, c]), ma_ref, bound, eye, low)
    encode(reader(kb_ref), mb_ref, bound, eye, low)
    ka_ref[...] = jnp.where(first, s2_ref[...], s1_ref[...])


def third_kernel(info_ref, ka_ref, kb_ref, p4_ref, p5_ref, msg_ref, keep_ref, sa_ref, sb_ref, *, bound):
    eye, low = square_masks()
    add_message(sa_ref, ka_ref, p4_ref, bound, eye, low)
    add_message(sb_ref, kb_ref, p5_ref, bound, eye, low)
    upper = info_ref[6] == 1
    encode(lambda r, c: jnp.where(upper, sa_ref[r, c], sb_ref[r, c]), msg_ref, bound, eye, low)
    keep_ref[...] = jnp.where(upper, sb_ref[...], sa_ref[...])


def sublane(x, p):
    return jnp.broadcast_to(x[p : p + 1, :], (TILE, LANES))


def tree(terms):
    terms = list(terms)
    while len(terms) > 1:
        terms = [terms[i] + terms[i + 1] if i + 1 < len(terms) else terms[i] for i in range(0, len(terms), 2)]
    return terms[0]


def invert_pair(tiles):
    lane, sub = iota((TILE, LANES), 1), iota((TILE, LANES), 0)
    col = lane % HALF
    half = lane - col
    here = [sub == p for p in range(TILE)]
    count = len(tiles)
    for g in range(count):
        inside = (col >= g * TILE) & (col < (g + 1) * TILE)
        index = [half + (g * TILE + q) for q in range(TILE)]

        def spread(t, q):
            return jnp.take_along_axis(t, index[q], axis=1)

        c = [spread(tiles[g], q) for q in range(TILE)]
        r = jnp.where(inside, jnp.where(col - g * TILE == sub, 1.0, 0.0), tiles[g])
        for p in range(0, TILE, 2):
            cp, cn = c[p], c[p + 1]
            a, b, d = sublane(cp, p), sublane(cp, p + 1), sublane(cn, p + 1)
            inv = 1.0 / (a * d - b * b)

            def eliminate(x):
                e0, e1 = sublane(x, p), sublane(x, p + 1)
                f0, f1 = d * e0 - b * e1, a * e1 - b * e0
                return jnp.where(here[p], f0 * inv, jnp.where(here[p + 1], f1 * inv, x - (cp * f0 + cn * f1) * inv))

            for q in range(p + 2, TILE):
                c[q] = eliminate(c[q])
            r = eliminate(r)
        rows = [sublane(r, p) for p in range(TILE)]
        for i in [(g + 1) % count] + [i for i in range(count) if i != g and i != (g + 1) % count]:
            t = tiles[i]
            tiles[i] = jnp.where(inside, 0.0, t) - tree([spread(t, p) * rows[p] for p in range(TILE)])
        tiles[g] = r
        yield


def block_diagonal(t):
    left = iota(t.shape, 1) < HALF
    zero = jnp.zeros_like(t)
    return jnp.concatenate([jnp.where(left, t, zero), jnp.where(left, zero, t)], axis=0)


def parts(x):
    high = x.astype(bf16)
    return high, (x - high.astype(f32)).astype(bf16)


def left4(p):
    return jnp.concatenate(p, axis=1)


def rows4(p):
    return jnp.concatenate([jnp.concatenate([q, q], axis=1) for q in p], axis=0)


def cols4(p):
    return jnp.concatenate([jnp.concatenate([q, q], axis=0) for q in p], axis=1)


def fold_halves(r):
    half = r.shape[1] // 2
    return r[:, :half] + r[:, half:]


def mm4(a, b):
    return fold_halves(lax.dot_general(a, b, (((1,), (0,)), ((), ())), preferred_element_type=f32))


def nt4(a, b):
    return fold_halves(nt(a, b))


def factor_solve(n, shift, m_ref, w_ref, x_ref):
    blocks, groups = n // HALF, HALF // TILE

    def begin(b):
        top = m_ref[b * HALF : (b + 1) * HALF, b * LANES : (b + 1) * LANES] + shift
        tiles = [top[i * TILE : (i + 1) * TILE] for i in range(groups)]
        return tiles, invert_pair(tiles)

    def run(steps, work):
        done = 0
        for g in range(groups):
            next(steps)
            todo = len(work) * (g + 1) // groups
            for k in range(done, todo):
                work[k]()
            done = todo
        for _ in steps:
            pass

    tiles, steps = begin(0)
    run(steps, [])
    for b in range(blocks):
        cs, nx = slice(b * LANES, (b + 1) * LANES), (b + 1) * HALF
        inverse = cols4(parts(block_diagonal(jnp.concatenate(tiles, axis=0))))
        panel = parts(m_ref[nx:, cs])
        left = left4(panel)
        first = HALF if nx < n else 8
        w0 = mm4(left[:first], inverse)
        w_ref[nx : nx + first, cs] = w0
        if nx >= n:
            break

        def right(j):
            lo = (j - b - 1) * HALF
            return rows4([block_diagonal(p[lo : lo + HALF]) for p in panel])

        js = slice((b + 1) * LANES, (b + 2) * LANES)
        m_ref[nx : nx + HALF, js] = m_ref[nx : nx + HALF, js] - nt4(left4(parts(w0)), right(b + 1))
        tiles, steps = begin(b + 1)
        kept = {}

        def rest():
            w = mm4(left[HALF:], inverse)
            w_ref[nx + HALF :, cs] = w
            kept["w"] = left4(parts(w))

        def trail(j):
            def go():
                jc, r0 = slice(j * LANES, (j + 1) * LANES), max(j * HALF, nx + HALF)
                m_ref[r0:, jc] = m_ref[r0:, jc] - nt4(kept["w"][r0 - nx - HALF :], right(j))

            return go

        run(steps, [rest] + [trail(j) for j in range(b + 1, blocks)])
    for b in reversed(range(blocks)):
        cs = slice(b * LANES, (b + 1) * LANES)
        x = w_ref[n:, cs]
        if b + 1 < blocks:
            below = [
                jnp.concatenate([block_diagonal(p[i * HALF : (i + 1) * HALF]) for i in range(blocks - b - 1)], axis=0)
                for p in parts(w_ref[(b + 1) * HALF : n, cs])
            ]
            x = x - mm4(left4(parts(x_ref[:, (b + 1) * LANES :])), cols4(below))
        x_ref[:, cs] = x


def solve_kernel(shift_ref, k_ref, p_ref, o_ref, m_ref, w_ref, x_ref, *, bound):
    eye, low = square_masks()
    matrix, rest = decode(p_ref, bound, eye, low)
    n = BLOCK

    def put(rows, t, c):
        u = pltpu.roll(t, HALF, 1)
        left = iota(t.shape, 1) < HALF
        m_ref[rows, 2 * c * LANES : (2 * c + 1) * LANES] = jnp.where(left, t, u)
        m_ref[rows, (2 * c + 1) * LANES : (2 * c + 2) * LANES] = jnp.where(left, u, t)

    xy, extra = rest()
    diag = split(k_ref[264:265, :] + extra)
    for r in range(2):
        for c in range(4):
            i, j = LAYOUT[r][c]
            t = k_ref[place(r, c)] + matrix(r, c)
            if (r, c) in ((0, 0), (0, 2)):
                u = t.T
                put(place(i, 0)[0], jnp.where(eye, diag[i], jnp.where(low, t, u)), i)
                put(place(j, 0)[0], jnp.where(eye, diag[j], jnp.where(low, u, t)), j)
            else:
                put(place(i, 0)[0], t, j)
    right = k_ref[256:264, :] + xy
    for c in range(4):
        put(slice(n, n + 8), right[:, c * LANES : (c + 1) * LANES], c)

    lane, sub = iota((HALF, LANES), 1), iota((HALF, LANES), 0)
    shift = jnp.where(lane % HALF == sub, jnp.where(lane < HALF, shift_ref[0], shift_ref[1]), 0.0)
    factor_solve(n, shift, m_ref, w_ref, x_ref)
    left = iota((8, LANES), 1) < HALF
    for c in range(4):
        even, odd = x_ref[:, 2 * c * LANES : (2 * c + 1) * LANES], x_ref[:, (2 * c + 1) * LANES : (2 * c + 2) * LANES]
        first = jnp.where(left, even, pltpu.roll(odd, HALF, 1))
        second = jnp.where(left, pltpu.roll(even, HALF, 1), odd)
        o_ref[:, c * LANES : (c + 1) * LANES] = jnp.concatenate([first, second], axis=0).astype(bf16)


def predict_kernel(info_ref, x_ref, b_ref, f_ref, o_ref, *, scale):
    weights = jnp.concatenate([b_ref[info_ref[8 + k]] for k in range(FOLDS)], axis=0)
    fitted = nt(weights, x_ref[...])
    folds = f_ref[...]
    total = jnp.zeros((16, folds.shape[1]), f32)
    for k in range(FOLDS):
        total = jnp.where(folds == k, fitted[16 * k : 16 * (k + 1)], total)
    o_ref[...] = (total * scale).astype(bf16)


def cross_kernel(o_ref, j_ref, g_ref, c_ref, *, scale):
    own = o_ref[...]
    count, width = g_ref.shape[0], g_ref.shape[2]
    prior = g_ref.shape[1] // 8
    old = tree([nt(own[:, b * width : (b + 1) * width], g_ref[b]) for b in range(count)])
    new = nt(own, j_ref[...])
    t_row, t_old = iota(old.shape, 0) % 8, iota(old.shape, 1) // prior
    t_new = iota(new.shape, 1) % 8
    old = jnp.where(t_row == t_old, old, 0.0)
    new = jnp.where(iota(new.shape, 0) % 8 == t_new, new, 0.0)
    pick_old = jnp.where(iota((prior, old.shape[1]), 1) % prior == iota((prior, old.shape[1]), 0), 1.0, 0.0)
    features = new.shape[1] // 8
    pick_new = jnp.where(iota((features, new.shape[1]), 1) // 8 == iota((features, new.shape[1]), 0), 1.0, 0.0)
    high = lax.Precision.HIGHEST
    c_ref[0:prior, :] = nt(pick_old, old, high) * scale
    c_ref[prior : prior + features, :] = nt(pick_new, new, high) * scale


def make_local(mesh):
    n_blk, n_smp = mesh.shape["blk"], mesh.shape["smp"]
    if n_smp != 8:
        raise NotImplementedError(n_smp)

    def pairs(bit, sends):
        out = []
        for b in range(n_blk):
            for s in range(n_smp):
                role = s ^ (7 if b & 1 else 0)
                if sends(role & 1, role >> 1 & 1, role >> 2):
                    out.append((b * n_smp + s, b * n_smp + (s ^ bit)))
        return out

    def move(x, bit, sends):
        return lax.ppermute(x, ("blk", "smp"), pairs(bit, sends))

    def local(x, traits, folds, lambdas, guesses):
        rows = x.shape[0]
        total = rows * n_smp
        bound = BOUND * total
        mirror = 7 * (lax.axis_index("blk") & 1)
        role = lax.axis_index("smp") ^ mirror
        b0, b1, b2 = role & 1, role >> 1 & 1, role >> 2
        info = jnp.stack(
            [
                jnp.where(b0 == 0, 2, 0),
                jnp.int32(1) + 0 * b0,
                jnp.where(b0 == 0, 0, 2),
                jnp.where(b1 == 0, 4, 3),
                jnp.where(b1 == 0, 3, 4),
                jnp.where(b0 == b1, 1, 0),
                b2,
                b2,
            ]
            + [o ^ mirror for o in OWNERS]
            + [b2] * 3
        ).astype(jnp.int32)
        shift = lambdas * total
        yt = traits.T
        f_row = folds.reshape(1, rows)
        prior = jnp.transpose(guesses[0], (1, 2, 0)).reshape(-1, guesses.shape[1])

        def call(kernel, outs, specs, scratch, *args, **static):
            import functools

            return pl.pallas_call(
                functools.partial(kernel, **static),
                out_shape=outs,
                in_specs=specs,
                out_specs=jax.tree.map(lambda _: VMEM, outs),
                scratch_shapes=scratch,
                compiler_params=PARAMS,
            )(*args)

        def packed(*lead):
            return jax.ShapeDtypeStruct((*lead, PACKED, BLOCK), f32)

        def wire(*lead):
            return jax.ShapeDtypeStruct((*lead, WIRE, BLOCK), jnp.int16)

        xt = pltpu.VMEM((BLOCK + 16, rows), bf16)
        work = pltpu.VMEM((PACKED, BLOCK), f32)
        m0, m1, m3, k1 = call(
            gram_send_kernel,
            (wire(), wire(), wire(), packed()),
            [SMEM, VMEM, VMEM, VMEM],
            [xt, work],
            info,
            x,
            yt,
            f_row,
            bound=bound,
        )
        p1 = move(m0, 1, lambda u, v, w: True)
        p2 = move(m1, 1, lambda u, v, w: u == 1)
        p3 = move(m3, 2, lambda u, v, w: True)
        k2, k4 = call(gram_keep_kernel, (packed(), packed()), [SMEM, VMEM, VMEM, VMEM], [xt], info, x, yt, f_row)
        ma, mb, ka, kb = call(
            second_kernel,
            (wire(), wire(), packed(), packed()),
            [SMEM] + [VMEM] * 6,
            [work, work],
            info,
            k1,
            k2,
            k4,
            p1,
            p2,
            p3,
            bound=bound,
        )
        p4 = move(ma, 2, lambda u, v, w: (u, v) != (1, 1))
        p5 = move(mb, 1, lambda u, v, w: u == 1)
        msg, keep = call(
            third_kernel, (wire(), packed()), [SMEM] + [VMEM] * 4, [work, work], info, ka, kb, p4, p5, bound=bound
        )
        p6 = move(msg, 4, lambda u, v, w: u == 0 or (u, v, w) == (1, 1, 1))
        beta = call(
            solve_kernel,
            jax.ShapeDtypeStruct((16, BLOCK), bf16),
            [SMEM, VMEM, VMEM],
            [pltpu.VMEM((BLOCK + 8, 2 * BLOCK), f32), pltpu.VMEM((BLOCK + 8, 2 * BLOCK), f32), pltpu.VMEM((8, 2 * BLOCK), f32)],
            shift,
            keep,
            p6,
            bound=bound,
        )
        betas = lax.all_to_all(jnp.broadcast_to(beta[None], (n_smp, 16, BLOCK)), "smp", 0, 0)
        oof = call(
            predict_kernel,
            jax.ShapeDtypeStruct((16, rows), bf16),
            [SMEM, VMEM, VMEM, VMEM],
            [],
            info,
            x,
            betas,
            f_row,
            scale=math.sqrt(total / BLOCK),
        )
        prior_all = lax.all_gather(prior, "blk", axis=0)
        oof_all = lax.all_gather(oof, "blk", axis=0, tiled=True)
        n_cross = prior.shape[0] // 8 + 2 * n_blk
        part = call(
            cross_kernel,
            jax.ShapeDtypeStruct((n_cross, 16), f32),
            [VMEM] * 3,
            [],
            oof,
            oof_all,
            prior_all,
            scale=1.0 / total,
        )
        part = lax.all_to_all(part.reshape(n_smp, n_cross // n_smp, 16), "smp", 0, 0)
        cross = jnp.sum(part, axis=0).reshape(n_cross // n_smp, 2, 8)
        return (
            jnp.transpose(oof.reshape(2, 8, rows), (2, 1, 0)),
            jnp.transpose(cross, (2, 1, 0)),
        )

    return local


def solution(mesh):
    return jax.shard_map(
        make_local(mesh),
        mesh=mesh,
        in_specs=(P("smp", "blk"), P("smp", None), P("smp"), P(), P("smp", "blk", None, None)),
        out_specs=(P("smp", None, "blk"), P(None, "blk", "smp")),
        check_vma=False,
    )
```

```python
import math

import jax
import jax.numpy as jnp
from jax import lax
from jax.experimental import pallas as pl
from jax.experimental.pallas import tpu as pltpu
from jax.sharding import PartitionSpec as P

BLOCK = 512
PHENOTYPIC_MEASURES = 8
FOLDS = 5
SHRINK_STRENGTH = 2

LANES = 128
TILE = 8
HALF = 64
PACKED = 272
WIRE = 288
DIGIT = 32766.0
BOUND = 36.0
OWNERS = (0, 2, 3, 4, 6)

f32 = jnp.float32
bf16 = jnp.bfloat16
VMEM = pl.BlockSpec(memory_space=pltpu.VMEM)
SMEM = pl.BlockSpec(memory_space=pltpu.SMEM)
MIB = 1024 * 1024


def nt(a, b, precision=None):
    return lax.dot_general(a, b, (((1,), (1,)), ((), ())), precision=precision, preferred_element_type=f32)


def iota(shape, dim):
    return lax.broadcasted_iota(jnp.int32, shape, dim)


def square_masks():
    row, col = iota((LANES, LANES), 0), iota((LANES, LANES), 1)
    return row == col, col < row


def column(row_vector, eye):
    return jnp.sum(jnp.where(eye, jnp.broadcast_to(row_vector, (LANES, LANES)), 0.0), axis=1, keepdims=True)


LAYOUT = (((0, 1), (1, 0), (2, 3), (3, 2)), ((2, 0), (2, 1), (3, 0), (3, 1)))


def place(r, c):
    return slice(r * LANES, (r + 1) * LANES), slice(c * LANES, (c + 1) * LANES)


def pair_scale(r, c, rows, cols, low):
    i, j = LAYOUT[r][c]
    if (r, c) in ((0, 0), (0, 2)):
        return jnp.where(low, cols[i] * rows[i], cols[j] * rows[j])
    return cols[i] * rows[j]


def split(vector):
    return [vector[:, i * LANES : (i + 1) * LANES] for i in range(BLOCK // LANES)]


def to_int(x):
    return jnp.floor(x + 0.5).astype(jnp.int32).astype(jnp.int16)


def digits(value, bound):
    u = value * (DIGIT / bound)
    high = jnp.floor(u)
    return high, (u - high) * DIGIT


def undigits(high, low, bound):
    return (high + low * (1.0 / DIGIT)) * (bound / DIGIT)


def encode(get, msg_ref, bound, eye, low):
    diag = get(slice(264, 265), slice(0, BLOCK))
    dh, dl = digits(diag, bound)
    dl = jnp.floor(dl + 0.5)
    scale = lax.rsqrt(undigits(dh, dl, bound) + 1e-3)
    rows = split(scale)
    cols = [column(r, eye) for r in rows]
    for r in range(2):
        for c in range(4):
            rs, cs = place(r, c)
            msg_ref[rs, cs] = to_int(get(rs, cs) * (pair_scale(r, c, rows, cols, low) * DIGIT))
    xh, xl = digits(get(slice(256, 264), slice(0, BLOCK)), bound)
    msg_ref[256:272, :] = to_int(jnp.concatenate([xh, xl], axis=0))
    spare = jnp.zeros((14, BLOCK), f32)
    msg_ref[272:288, :] = to_int(jnp.concatenate([dh, dl, spare], axis=0))


def decode(msg_ref, bound, eye, low):
    tail = msg_ref[272:288, :].astype(f32)
    diag = undigits(tail[0:1], tail[1:2], bound)
    scale = jnp.sqrt(diag + 1e-3)
    rows = split(scale)
    cols = [column(r, eye) for r in rows]

    def matrix(r, c):
        rs, cs = place(r, c)
        return msg_ref[rs, cs].astype(f32) * (pair_scale(r, c, rows, cols, low) * (1.0 / DIGIT))

    def rest():
        x = msg_ref[256:272, :].astype(f32)
        return undigits(x[0:8], x[8:16], bound), diag

    return matrix, rest


def add_message(dst_ref, src_ref, msg_ref, bound, eye, low):
    matrix, rest = decode(msg_ref, bound, eye, low)
    for r in range(2):
        for c in range(4):
            rs, cs = place(r, c)
            dst_ref[rs, cs] = src_ref[rs, cs] + matrix(r, c)
    xy, diag = rest()
    dst_ref[256:264, :] = src_ref[256:264, :] + xy
    dst_ref[264:272, :] = src_ref[264:272, :] + jnp.concatenate([diag, jnp.zeros((7, BLOCK), f32)], axis=0)


def reader(ref):
    return lambda rows, cols: ref[rows, cols]


def gram_one(fold, x_ref, xt_ref, f_ref, out_ref, eye, low):
    mask = jnp.where(f_ref[...] != fold, 1.0, 0.0).astype(bf16)
    g0 = jnp.dot(xt_ref[0:256, :] * mask, x_ref[:, 0:256], preferred_element_type=f32)
    g1 = jnp.dot(xt_ref[256:528, :] * mask, x_ref[...], preferred_element_type=f32)

    def block(i, j):
        rs, cs = place(i, j)
        return g0[rs, cs] if i < 2 else g1[(i - 2) * LANES : (i - 1) * LANES, cs]

    for r in range(2):
        for c in range(4):
            i, j = LAYOUT[r][c]
            rs, cs = place(r, c)
            if (r, c) in ((0, 0), (0, 2)):
                out_ref[rs, cs] = jnp.where(low, block(i, i), jnp.where(eye, 0.0, block(j, j)))
            else:
                out_ref[rs, cs] = block(i, j)
    diag = [jnp.sum(jnp.where(eye, block(i, i), 0.0), axis=0, keepdims=True) for i in range(4)]
    out_ref[256:264, :] = g1[256:264, :]
    out_ref[264:272, :] = jnp.concatenate([jnp.concatenate(diag, axis=1), jnp.zeros((7, BLOCK), f32)], axis=0)


def load_transposed(x_ref, yt_ref, xt_ref):
    xt_ref[0:BLOCK, :] = x_ref[...].T
    xt_ref[BLOCK : BLOCK + 16, :] = jnp.concatenate([yt_ref[...], jnp.zeros_like(yt_ref[...])], axis=0)


def gram_send_kernel(info_ref, x_ref, yt_ref, f_ref, m0_ref, m1_ref, m3_ref, keep_ref, xt_ref, work_ref, *, bound):
    eye, low = square_masks()
    load_transposed(x_ref, yt_ref, xt_ref)
    for slot, dst, msg_ref in ((0, work_ref, m0_ref), (1, keep_ref, m1_ref), (3, work_ref, m3_ref)):
        gram_one(info_ref[slot], x_ref, xt_ref, f_ref, dst, eye, low)
        encode(reader(dst), msg_ref, bound, eye, low)


def gram_keep_kernel(info_ref, x_ref, yt_ref, f_ref, k2_ref, k4_ref, xt_ref):
    eye, low = square_masks()
    load_transposed(x_ref, yt_ref, xt_ref)
    for slot, dst in ((2, k2_ref), (4, k4_ref)):
        gram_one(info_ref[slot], x_ref, xt_ref, f_ref, dst, eye, low)


def second_kernel(
    info_ref, k1_ref, k2_ref, k4_ref, p1_ref, p2_ref, p3_ref, ma_ref, mb_ref, ka_ref, kb_ref, s1_ref, s2_ref, *, bound
):
    eye, low = square_masks()
    add_message(s2_ref, k2_ref, p1_ref, bound, eye, low)
    add_message(s1_ref, k1_ref, p2_ref, bound, eye, low)
    add_message(kb_ref, k4_ref, p3_ref, bound, eye, low)
    first = info_ref[5] == 1
    encode(lambda r, c: jnp.where(first, s1_ref[r, c], s2_ref[r, c]), ma_ref, bound, eye, low)
    encode(reader(kb_ref), mb_ref, bound, eye, low)
    ka_ref[...] = jnp.where(first, s2_ref[...], s1_ref[...])


def third_kernel(info_ref, ka_ref, kb_ref, p4_ref, p5_ref, msg_ref, keep_ref, sa_ref, sb_ref, *, bound):
    eye, low = square_masks()
    add_message(sa_ref, ka_ref, p4_ref, bound, eye, low)
    add_message(sb_ref, kb_ref, p5_ref, bound, eye, low)
    upper = info_ref[6] == 1
    encode(lambda r, c: jnp.where(upper, sa_ref[r, c], sb_ref[r, c]), msg_ref, bound, eye, low)
    keep_ref[...] = jnp.where(upper, sb_ref[...], sa_ref[...])


def sublane(x, p):
    return jnp.broadcast_to(x[p : p + 1, :], (TILE, LANES))


def tree(terms):
    terms = list(terms)
    while len(terms) > 1:
        terms = [terms[i] + terms[i + 1] if i + 1 < len(terms) else terms[i] for i in range(0, len(terms), 2)]
    return terms[0]


def invert_pair(tiles):
    lane, sub = iota((TILE, LANES), 1), iota((TILE, LANES), 0)
    col = lane % HALF
    half = lane - col
    here = [sub == p for p in range(TILE)]
    count = len(tiles)
    for g in range(count):
        inside = (col >= g * TILE) & (col < (g + 1) * TILE)
        index = [half + (g * TILE + q) for q in range(TILE)]

        def spread(t, q):
            return jnp.take_along_axis(t, index[q], axis=1)

        c = [spread(tiles[g], q) for q in range(TILE)]
        r = jnp.where(inside, jnp.where(col - g * TILE == sub, 1.0, 0.0), tiles[g])
        for p in range(0, TILE, 2):
            cp, cn = c[p], c[p + 1]
            a, b, d = sublane(cp, p), sublane(cp, p + 1), sublane(cn, p + 1)
            inv = 1.0 / (a * d - b * b)

            def eliminate(x):
                e0, e1 = sublane(x, p), sublane(x, p + 1)
                f0, f1 = d * e0 - b * e1, a * e1 - b * e0
                return jnp.where(here[p], f0 * inv, jnp.where(here[p + 1], f1 * inv, x - (cp * f0 + cn * f1) * inv))

            for q in range(p + 2, TILE):
                c[q] = eliminate(c[q])
            r = eliminate(r)
        rows = [sublane(r, p) for p in range(TILE)]
        for i in [(g + 1) % count] + [i for i in range(count) if i != g and i != (g + 1) % count]:
            t = tiles[i]
            tiles[i] = jnp.where(inside, 0.0, t) - tree([spread(t, p) * rows[p] for p in range(TILE)])
        tiles[g] = r
        yield


def block_diagonal(t):
    left = iota(t.shape, 1) < HALF
    zero = jnp.zeros_like(t)
    return jnp.concatenate([jnp.where(left, t, zero), jnp.where(left, zero, t)], axis=0)


def parts(x):
    high = x.astype(bf16)
    return high, (x - high.astype(f32)).astype(bf16)


def left4(p):
    return jnp.concatenate(p, axis=1)


def rows4(p):
    return jnp.concatenate([jnp.concatenate([q, q], axis=1) for q in p], axis=0)


def cols4(p):
    return jnp.concatenate([jnp.concatenate([q, q], axis=0) for q in p], axis=1)


def fold_halves(r):
    half = r.shape[1] // 2
    return r[:, :half] + r[:, half:]


def mm4(a, b):
    return fold_halves(lax.dot_general(a, b, (((1,), (0,)), ((), ())), preferred_element_type=f32))


def nt4(a, b):
    return fold_halves(nt(a, b))


def factor_solve(n, shift, m_ref, w_ref, x_ref):
    blocks, groups = n // HALF, HALF // TILE

    def begin(b):
        top = m_ref[b * HALF : (b + 1) * HALF, b * LANES : (b + 1) * LANES] + shift
        tiles = [top[i * TILE : (i + 1) * TILE] for i in range(groups)]
        return tiles, invert_pair(tiles)

    def run(steps, work):
        done = 0
        for g in range(groups):
            next(steps)
            todo = len(work) * (g + 1) // groups
            for k in range(done, todo):
                work[k]()
            done = todo
        for _ in steps:
            pass

    tiles, steps = begin(0)
    run(steps, [])
    for b in range(blocks):
        cs, nx = slice(b * LANES, (b + 1) * LANES), (b + 1) * HALF
        inverse = cols4(parts(block_diagonal(jnp.concatenate(tiles, axis=0))))
        panel = parts(m_ref[nx:, cs])
        left = left4(panel)
        first = HALF if nx < n else 8
        w0 = mm4(left[:first], inverse)
        w_ref[nx : nx + first, cs] = w0
        if nx >= n:
            break

        def right(j):
            lo = (j - b - 1) * HALF
            return rows4([block_diagonal(p[lo : lo + HALF]) for p in panel])

        js = slice((b + 1) * LANES, (b + 2) * LANES)
        m_ref[nx : nx + HALF, js] = m_ref[nx : nx + HALF, js] - nt4(left4(parts(w0)), right(b + 1))
        tiles, steps = begin(b + 1)
        kept = {}

        def rest():
            w = mm4(left[HALF:], inverse)
            w_ref[nx + HALF :, cs] = w
            kept["w"] = left4(parts(w))

        def trail(j):
            def go():
                jc, r0 = slice(j * LANES, (j + 1) * LANES), max(j * HALF, nx + HALF)
                m_ref[r0:, jc] = m_ref[r0:, jc] - nt4(kept["w"][r0 - nx - HALF :], right(j))

            return go

        run(steps, [rest] + [trail(j) for j in range(b + 1, blocks)])
    for b in reversed(range(blocks)):
        cs = slice(b * LANES, (b + 1) * LANES)
        x = w_ref[n:, cs]
        if b + 1 < blocks:
            below = [
                jnp.concatenate([block_diagonal(p[i * HALF : (i + 1) * HALF]) for i in range(blocks - b - 1)], axis=0)
                for p in parts(w_ref[(b + 1) * HALF : n, cs])
            ]
            x = x - mm4(left4(parts(x_ref[:, (b + 1) * LANES :])), cols4(below))
        x_ref[:, cs] = x


def solve_kernel(shift_ref, k_ref, p_ref, o_ref, m_ref, w_ref, x_ref, *, bound):
    eye, low = square_masks()
    matrix, rest = decode(p_ref, bound, eye, low)
    n = BLOCK

    def put(rows, t, c):
        u = pltpu.roll(t, HALF, 1)
        left = iota(t.shape, 1) < HALF
        m_ref[rows, 2 * c * LANES : (2 * c + 1) * LANES] = jnp.where(left, t, u)
        m_ref[rows, (2 * c + 1) * LANES : (2 * c + 2) * LANES] = jnp.where(left, u, t)

    xy, extra = rest()
    diag = split(k_ref[264:265, :] + extra)
    for r in range(2):
        for c in range(4):
            i, j = LAYOUT[r][c]
            t = k_ref[place(r, c)] + matrix(r, c)
            if (r, c) in ((0, 0), (0, 2)):
                u = t.T
                put(place(i, 0)[0], jnp.where(eye, diag[i], jnp.where(low, t, u)), i)
                put(place(j, 0)[0], jnp.where(eye, diag[j], jnp.where(low, u, t)), j)
            else:
                put(place(i, 0)[0], t, j)
    right = k_ref[256:264, :] + xy
    for c in range(4):
        put(slice(n, n + 8), right[:, c * LANES : (c + 1) * LANES], c)

    lane, sub = iota((HALF, LANES), 1), iota((HALF, LANES), 0)
    shift = jnp.where(lane % HALF == sub, jnp.where(lane < HALF, shift_ref[0], shift_ref[1]), 0.0)
    factor_solve(n, shift, m_ref, w_ref, x_ref)
    left = iota((8, LANES), 1) < HALF
    for c in range(4):
        even, odd = x_ref[:, 2 * c * LANES : (2 * c + 1) * LANES], x_ref[:, (2 * c + 1) * LANES : (2 * c + 2) * LANES]
        first = jnp.where(left, even, pltpu.roll(odd, HALF, 1))
        second = jnp.where(left, pltpu.roll(even, HALF, 1), odd)
        both = jnp.concatenate([first, second], axis=0).astype(bf16)
        for d in range(o_ref.shape[0]):
            o_ref[d, :, c * LANES : (c + 1) * LANES] = both


def predict_kernel(info_ref, x_ref, b_ref, f_ref, o_ref, *, scale):
    weights = jnp.concatenate([b_ref[info_ref[8 + k]] for k in range(FOLDS)], axis=0)
    fitted = nt(weights, x_ref[...])
    folds = f_ref[...]
    total = jnp.zeros((16, folds.shape[1]), f32)
    for k in range(FOLDS):
        total = jnp.where(folds == k, fitted[16 * k : 16 * (k + 1)], total)
    o_ref[...] = (total * scale).astype(bf16)


def cross_kernel(o_ref, j_ref, g_ref, c_ref, *, scale):
    own = o_ref[...]
    count, width = g_ref.shape[0], g_ref.shape[2]
    prior = g_ref.shape[1] // 8
    old = tree([nt(own[:, b * width : (b + 1) * width], g_ref[b]) for b in range(count)])
    new = nt(own, j_ref[...])
    t_row, t_old = iota(old.shape, 0) % 8, iota(old.shape, 1) // prior
    t_new = iota(new.shape, 1) % 8
    old = jnp.where(t_row == t_old, old, 0.0)
    new = jnp.where(iota(new.shape, 0) % 8 == t_new, new, 0.0)
    pick_old = jnp.where(iota((prior, old.shape[1]), 1) % prior == iota((prior, old.shape[1]), 0), 1.0, 0.0)
    features = new.shape[1] // 8
    pick_new = jnp.where(iota((features, new.shape[1]), 1) // 8 == iota((features, new.shape[1]), 0), 1.0, 0.0)
    high = lax.Precision.HIGHEST
    c_ref[0:prior, :] = nt(pick_old, old, high) * scale
    c_ref[prior : prior + features, :] = nt(pick_new, new, high) * scale


def make_local(mesh):
    n_blk, n_smp = mesh.shape["blk"], mesh.shape["smp"]
    if n_smp != 8:
        raise NotImplementedError(n_smp)

    def pairs(bit, sends):
        out = []
        for b in range(n_blk):
            for s in range(n_smp):
                role = s ^ (7 if b & 1 else 0)
                if sends(role & 1, role >> 1 & 1, role >> 2):
                    out.append((b * n_smp + s, b * n_smp + (s ^ bit)))
        return out

    def move(x, bit, sends):
        return lax.ppermute(x, ("blk", "smp"), pairs(bit, sends))

    def local(x, traits, folds, lambdas, guesses):
        rows = x.shape[0]
        total = rows * n_smp
        bound = BOUND * total
        mirror = 7 * (lax.axis_index("blk") & 1)
        role = lax.axis_index("smp") ^ mirror
        b0, b1, b2 = role & 1, role >> 1 & 1, role >> 2
        info = jnp.stack(
            [
                jnp.where(b0 == 0, 2, 0),
                jnp.int32(1) + 0 * b0,
                jnp.where(b0 == 0, 0, 2),
                jnp.where(b1 == 0, 4, 3),
                jnp.where(b1 == 0, 3, 4),
                jnp.where(b0 == b1, 1, 0),
                b2,
                b2,
            ]
            + [o ^ mirror for o in OWNERS]
            + [b2] * 3
        ).astype(jnp.int32)
        shift = lambdas * total
        yt = traits.T
        f_row = folds.reshape(1, rows)
        prior = jnp.transpose(guesses[0], (1, 2, 0)).reshape(-1, guesses.shape[1])

        def call(kernel, outs, specs, scratch, *args, mib=12, **static):
            import functools

            return pl.pallas_call(
                functools.partial(kernel, **static),
                out_shape=outs,
                in_specs=specs,
                out_specs=jax.tree.map(lambda _: VMEM, outs),
                scratch_shapes=scratch,
                compiler_params=pltpu.CompilerParams(vmem_limit_bytes=mib * MIB),
            )(*args)

        def packed(*lead):
            return jax.ShapeDtypeStruct((*lead, PACKED, BLOCK), f32)

        def wire(*lead):
            return jax.ShapeDtypeStruct((*lead, WIRE, BLOCK), jnp.int16)

        xt = pltpu.VMEM((BLOCK + 16, rows), bf16)
        work = pltpu.VMEM((PACKED, BLOCK), f32)
        m0, m1, m3, k1 = call(
            gram_send_kernel,
            (wire(), wire(), wire(), packed()),
            [SMEM, VMEM, VMEM, VMEM],
            [xt, work],
            info,
            x,
            yt,
            f_row,
            bound=bound,
            mib=16,
        )
        p1 = move(m0, 1, lambda u, v, w: True)
        p2 = move(m1, 1, lambda u, v, w: u == 1)
        p3 = move(m3, 2, lambda u, v, w: True)
        k2, k4 = call(gram_keep_kernel, (packed(), packed()), [SMEM, VMEM, VMEM, VMEM], [xt], info, x, yt, f_row, mib=16)
        ma, mb, ka, kb = call(
            second_kernel,
            (wire(), wire(), packed(), packed()),
            [SMEM] + [VMEM] * 6,
            [work, work],
            info,
            k1,
            k2,
            k4,
            p1,
            p2,
            p3,
            bound=bound,
        )
        p4 = move(ma, 2, lambda u, v, w: (u, v) != (1, 1))
        p5 = move(mb, 1, lambda u, v, w: u == 1)
        msg, keep = call(
            third_kernel, (wire(), packed()), [SMEM] + [VMEM] * 4, [work, work], info, ka, kb, p4, p5, bound=bound
        )
        p6 = move(msg, 4, lambda u, v, w: u == 0 or (u, v, w) == (1, 1, 1))
        beta = call(
            solve_kernel,
            jax.ShapeDtypeStruct((n_smp, 16, BLOCK), bf16),
            [SMEM, VMEM, VMEM],
            [pltpu.VMEM((BLOCK + 8, 2 * BLOCK), f32), pltpu.VMEM((BLOCK + 8, 2 * BLOCK), f32), pltpu.VMEM((8, 2 * BLOCK), f32)],
            shift,
            keep,
            p6,
            bound=bound,
        )
        betas = lax.all_to_all(beta, "smp", 0, 0)
        oof = call(
            predict_kernel,
            jax.ShapeDtypeStruct((16, rows), bf16),
            [SMEM, VMEM, VMEM, VMEM],
            [],
            info,
            x,
            betas,
            f_row,
            scale=math.sqrt(total / BLOCK),
        )
        prior_all = lax.all_gather(prior, "blk", axis=0)
        oof_all = lax.all_gather(oof, "blk", axis=0, tiled=True)
        n_cross = prior.shape[0] // 8 + 2 * n_blk
        part = call(
            cross_kernel,
            jax.ShapeDtypeStruct((n_cross, 16), f32),
            [VMEM] * 3,
            [],
            oof,
            oof_all,
            prior_all,
            scale=1.0 / total,
        )
        part = lax.all_to_all(part.reshape(n_smp, n_cross // n_smp, 16), "smp", 0, 0)
        cross = jnp.sum(part, axis=0).reshape(n_cross // n_smp, 2, 8)
        return (
            jnp.transpose(oof.reshape(2, 8, rows), (2, 1, 0)),
            jnp.transpose(cross, (2, 1, 0)),
        )

    return local


def solution(mesh):
    return jax.shard_map(
        make_local(mesh),
        mesh=mesh,
        in_specs=(P("smp", "blk"), P("smp", None), P("smp"), P(), P("smp", "blk", None, None)),
        out_specs=(P("smp", None, "blk"), P(None, "blk", "smp")),
        check_vma=False,
    )
```

```python
import math

import jax
import jax.numpy as jnp
from jax import lax
from jax.experimental import pallas as pl
from jax.experimental.pallas import tpu as pltpu
from jax.sharding import PartitionSpec as P

BLOCK = 512
FOLDS = 5

LANES = 128
TILE = 8
HALF = 64
PACKED = 272
WIRE = 288
DIGIT = 32766.0
BOUND = 36.0
OWNERS = (0, 2, 3, 4, 6)

f32 = jnp.float32
bf16 = jnp.bfloat16
VMEM = pl.BlockSpec(memory_space=pltpu.VMEM)
SMEM = pl.BlockSpec(memory_space=pltpu.SMEM)
HBM = pl.BlockSpec(memory_space=pltpu.HBM)
MIB = 1024 * 1024


def nt(a, b, precision=None):
    return lax.dot_general(a, b, (((1,), (1,)), ((), ())), precision=precision, preferred_element_type=f32)


def iota(shape, dim):
    return lax.broadcasted_iota(jnp.int32, shape, dim)


def square_masks():
    row, col = iota((LANES, LANES), 0), iota((LANES, LANES), 1)
    return row == col, col < row


def column(row_vector, eye):
    return jnp.sum(jnp.where(eye, jnp.broadcast_to(row_vector, (LANES, LANES)), 0.0), axis=1, keepdims=True)


LAYOUT = (((0, 1), (1, 0), (2, 3), (3, 2)), ((2, 0), (2, 1), (3, 0), (3, 1)))


def place(r, c):
    return slice(r * LANES, (r + 1) * LANES), slice(c * LANES, (c + 1) * LANES)


def pair_scale(r, c, rows, cols, low):
    i, j = LAYOUT[r][c]
    if (r, c) in ((0, 0), (0, 2)):
        return jnp.where(low, cols[i] * rows[i], cols[j] * rows[j])
    return cols[i] * rows[j]


def split(vector):
    return [vector[:, i * LANES : (i + 1) * LANES] for i in range(BLOCK // LANES)]


def to_int(x):
    return jnp.floor(x + 0.5).astype(jnp.int32).astype(jnp.int16)


def digits(value, bound):
    u = value * (DIGIT / bound)
    high = jnp.floor(u)
    return high, (u - high) * DIGIT


def undigits(high, low, bound):
    return (high + low * (1.0 / DIGIT)) * (bound / DIGIT)


def encode(get, msg_ref, bound, eye, low):
    diag = get(slice(264, 265), slice(0, BLOCK))
    dh, dl = digits(diag, bound)
    dl = jnp.floor(dl + 0.5)
    scale = lax.rsqrt(undigits(dh, dl, bound) + 1e-3)
    rows = split(scale)
    cols = [column(r, eye) for r in rows]
    for r in range(2):
        for c in range(4):
            rs, cs = place(r, c)
            msg_ref[rs, cs] = to_int(get(rs, cs) * (pair_scale(r, c, rows, cols, low) * DIGIT))
    xh, xl = digits(get(slice(256, 264), slice(0, BLOCK)), bound)
    msg_ref[256:272, :] = to_int(jnp.concatenate([xh, xl], axis=0))
    spare = jnp.zeros((14, BLOCK), f32)
    msg_ref[272:288, :] = to_int(jnp.concatenate([dh, dl, spare], axis=0))


def decode(msg_ref, bound, eye, low):
    tail = msg_ref[272:288, :].astype(f32)
    diag = undigits(tail[0:1], tail[1:2], bound)
    scale = jnp.sqrt(diag + 1e-3)
    rows = split(scale)
    cols = [column(r, eye) for r in rows]

    def matrix(r, c):
        rs, cs = place(r, c)
        return msg_ref[rs, cs].astype(f32) * (pair_scale(r, c, rows, cols, low) * (1.0 / DIGIT))

    def rest():
        x = msg_ref[256:272, :].astype(f32)
        return undigits(x[0:8], x[8:16], bound), diag

    return matrix, rest


def add_message(dst_ref, src_ref, msg_ref, bound, eye, low):
    matrix, rest = decode(msg_ref, bound, eye, low)
    for r in range(2):
        for c in range(4):
            rs, cs = place(r, c)
            dst_ref[rs, cs] = src_ref[rs, cs] + matrix(r, c)
    xy, diag = rest()
    dst_ref[256:264, :] = src_ref[256:264, :] + xy
    dst_ref[264:272, :] = src_ref[264:272, :] + jnp.concatenate([diag, jnp.zeros((7, BLOCK), f32)], axis=0)


def reader(ref):
    return lambda rows, cols: ref[rows, cols]


def gram_one(fold, x_ref, xt_ref, yt_ref, f_ref, out_ref, eye, low):
    mask = jnp.where(f_ref[...] != fold, 1.0, 0.0).astype(bf16)
    g0 = jnp.dot(xt_ref[0:256, :] * mask, x_ref[:, 0:256], preferred_element_type=f32)
    lower = jnp.concatenate([xt_ref[256:BLOCK, :], yt_ref[...]], axis=0)
    g1 = jnp.dot(lower * mask, x_ref[...], preferred_element_type=f32)

    def block(i, j):
        rs, cs = place(i, j)
        return g0[rs, cs] if i < 2 else g1[(i - 2) * LANES : (i - 1) * LANES, cs]

    for r in range(2):
        for c in range(4):
            i, j = LAYOUT[r][c]
            rs, cs = place(r, c)
            if (r, c) in ((0, 0), (0, 2)):
                out_ref[rs, cs] = jnp.where(low, block(i, i), jnp.where(eye, 0.0, block(j, j)))
            else:
                out_ref[rs, cs] = block(i, j)
    diag = [jnp.sum(jnp.where(eye, block(i, i), 0.0), axis=0, keepdims=True) for i in range(4)]
    out_ref[256:264, :] = g1[256:264, :]
    out_ref[264:272, :] = jnp.concatenate([jnp.concatenate(diag, axis=1), jnp.zeros((7, BLOCK), f32)], axis=0)


def gram_first_kernel(
    x_hbm, yt_hbm, f_hbm, msg_ref, x_ref, yt_ref, f_ref, work_ref, xt_ref, in_ref, sems, *, bound, fold_of, chunks
):
    rows = x_ref.shape[0] // chunks
    small = [pltpu.make_async_copy(yt_hbm, in_ref, sems.at[chunks]), pltpu.make_async_copy(f_hbm, f_ref, sems.at[chunks + 1])]
    loads = []
    for c in range(chunks):
        part = pl.ds(c * rows, rows)
        loads.append(pltpu.make_async_copy(x_hbm.at[part], x_ref.at[part], sems.at[c]))
    for copy in loads + small:
        copy.start()
    eye, low = square_masks()
    for c, copy in enumerate(loads):
        copy.wait()
        part = slice(c * rows, (c + 1) * rows)
        xt_ref[:, part] = x_ref[part, :].T
    for copy in small:
        copy.wait()
    yt_ref[...] = jnp.concatenate([in_ref[...], jnp.zeros_like(in_ref[...])], axis=0)
    gram_one(fold_of(), x_ref, xt_ref, yt_ref, f_ref, work_ref, eye, low)
    encode(reader(work_ref), msg_ref, bound, eye, low)


def gram_send_kernel(info_ref, x_ref, yt_ref, f_ref, m1_ref, m3_ref, keep_ref, work_ref, xt_ref, *, bound):
    eye, low = square_masks()
    xt_ref[...] = x_ref[...].T
    for slot, dst, msg_ref in ((1, keep_ref, m1_ref), (3, work_ref, m3_ref)):
        gram_one(info_ref[slot], x_ref, xt_ref, yt_ref, f_ref, dst, eye, low)
        encode(reader(dst), msg_ref, bound, eye, low)


def gram_keep_kernel(info_ref, x_ref, yt_ref, f_ref, k2_ref, k4_ref, xt_ref):
    eye, low = square_masks()
    xt_ref[...] = x_ref[...].T
    for slot, dst in ((2, k2_ref), (4, k4_ref)):
        gram_one(info_ref[slot], x_ref, xt_ref, yt_ref, f_ref, dst, eye, low)


def second_kernel(
    info_ref, k1_ref, k2_ref, k4_ref, p1_ref, p2_ref, p3_ref, ma_ref, mb_ref, ka_ref, kb_ref, s1_ref, s2_ref, *, bound
):
    eye, low = square_masks()
    add_message(s2_ref, k2_ref, p1_ref, bound, eye, low)
    add_message(s1_ref, k1_ref, p2_ref, bound, eye, low)
    add_message(kb_ref, k4_ref, p3_ref, bound, eye, low)
    first = info_ref[5] == 1
    encode(lambda r, c: jnp.where(first, s1_ref[r, c], s2_ref[r, c]), ma_ref, bound, eye, low)
    encode(reader(kb_ref), mb_ref, bound, eye, low)
    ka_ref[...] = jnp.where(first, s2_ref[...], s1_ref[...])


def third_kernel(info_ref, ka_ref, kb_ref, p4_ref, p5_ref, msg_ref, keep_ref, sa_ref, sb_ref, *, bound):
    eye, low = square_masks()
    add_message(sa_ref, ka_ref, p4_ref, bound, eye, low)
    add_message(sb_ref, kb_ref, p5_ref, bound, eye, low)
    upper = info_ref[6] == 1
    encode(lambda r, c: jnp.where(upper, sa_ref[r, c], sb_ref[r, c]), msg_ref, bound, eye, low)
    keep_ref[...] = jnp.where(upper, sb_ref[...], sa_ref[...])


def sublane(x, p):
    return jnp.broadcast_to(x[p : p + 1, :], (TILE, LANES))


def tree(terms):
    terms = list(terms)
    while len(terms) > 1:
        terms = [terms[i] + terms[i + 1] if i + 1 < len(terms) else terms[i] for i in range(0, len(terms), 2)]
    return terms[0]


def invert_pair(tiles):
    lane, sub = iota((TILE, LANES), 1), iota((TILE, LANES), 0)
    col = lane % HALF
    half = lane - col
    here = [sub == p for p in range(TILE)]
    count = len(tiles)
    for g in range(count):
        inside = (col >= g * TILE) & (col < (g + 1) * TILE)
        index = [half + (g * TILE + q) for q in range(TILE)]

        def spread(t, q):
            return jnp.take_along_axis(t, index[q], axis=1)

        c = [spread(tiles[g], q) for q in range(TILE)]
        r = jnp.where(inside, jnp.where(col - g * TILE == sub, 1.0, 0.0), tiles[g])
        for p in range(0, TILE, 2):
            cp, cn = c[p], c[p + 1]
            a, b, d = sublane(cp, p), sublane(cp, p + 1), sublane(cn, p + 1)
            inv = 1.0 / (a * d - b * b)

            def eliminate(x):
                e0, e1 = sublane(x, p), sublane(x, p + 1)
                f0, f1 = d * e0 - b * e1, a * e1 - b * e0
                return jnp.where(here[p], f0 * inv, jnp.where(here[p + 1], f1 * inv, x - (cp * f0 + cn * f1) * inv))

            for q in range(p + 2, TILE):
                c[q] = eliminate(c[q])
            r = eliminate(r)
        rows = [sublane(r, p) for p in range(TILE)]
        for i in [(g + 1) % count] + [i for i in range(count) if i != g and i != (g + 1) % count]:
            t = tiles[i]
            tiles[i] = jnp.where(inside, 0.0, t) - tree([spread(t, p) * rows[p] for p in range(TILE)])
        tiles[g] = r
        yield


def block_diagonal(t):
    left = iota(t.shape, 1) < HALF
    zero = jnp.zeros_like(t)
    return jnp.concatenate([jnp.where(left, t, zero), jnp.where(left, zero, t)], axis=0)


def parts(x):
    high = x.astype(bf16)
    return high, (x - high.astype(f32)).astype(bf16)


def left4(p):
    return jnp.concatenate(p, axis=1)


def rows4(p):
    return jnp.concatenate([jnp.concatenate([q, q], axis=1) for q in p], axis=0)


def cols4(p):
    return jnp.concatenate([jnp.concatenate([q, q], axis=0) for q in p], axis=1)


def fold_halves(r):
    half = r.shape[1] // 2
    return r[:, :half] + r[:, half:]


def mm4(a, b):
    return fold_halves(lax.dot_general(a, b, (((1,), (0,)), ((), ())), preferred_element_type=f32))


def nt4(a, b):
    return fold_halves(nt(a, b))


def factor_solve(n, shift, m_ref, w_ref, x_ref):
    blocks, groups = n // HALF, HALF // TILE

    def begin(b):
        top = m_ref[b * HALF : (b + 1) * HALF, b * LANES : (b + 1) * LANES] + shift
        tiles = [top[i * TILE : (i + 1) * TILE] for i in range(groups)]
        return tiles, invert_pair(tiles)

    def run(steps, work):
        done = 0
        for g in range(groups):
            next(steps)
            todo = len(work) * (g + 1) // groups
            for k in range(done, todo):
                work[k]()
            done = todo
        for _ in steps:
            pass

    tiles, steps = begin(0)
    run(steps, [])
    for b in range(blocks):
        cs, nx = slice(b * LANES, (b + 1) * LANES), (b + 1) * HALF
        inverse = cols4(parts(block_diagonal(jnp.concatenate(tiles, axis=0))))
        panel = parts(m_ref[nx:, cs])
        left = left4(panel)
        first = HALF if nx < n else 8
        w0 = mm4(left[:first], inverse)
        w_ref[nx : nx + first, cs] = w0
        if nx >= n:
            break

        def right(j):
            lo = (j - b - 1) * HALF
            return rows4([block_diagonal(p[lo : lo + HALF]) for p in panel])

        js = slice((b + 1) * LANES, (b + 2) * LANES)
        m_ref[nx : nx + HALF, js] = m_ref[nx : nx + HALF, js] - nt4(left4(parts(w0)), right(b + 1))
        tiles, steps = begin(b + 1)
        kept = {}

        def rest():
            w = mm4(left[HALF:], inverse)
            w_ref[nx + HALF :, cs] = w
            kept["w"] = left4(parts(w))

        def trail(j):
            def go():
                jc, r0 = slice(j * LANES, (j + 1) * LANES), max(j * HALF, nx + HALF)
                m_ref[r0:, jc] = m_ref[r0:, jc] - nt4(kept["w"][r0 - nx - HALF :], right(j))

            return go

        run(steps, [rest] + [trail(j) for j in range(b + 1, blocks)])
    for b in reversed(range(blocks)):
        cs = slice(b * LANES, (b + 1) * LANES)
        x = w_ref[n:, cs]
        if b + 1 < blocks:
            below = [
                jnp.concatenate([block_diagonal(p[i * HALF : (i + 1) * HALF]) for i in range(blocks - b - 1)], axis=0)
                for p in parts(w_ref[(b + 1) * HALF : n, cs])
            ]
            x = x - mm4(left4(parts(x_ref[:, (b + 1) * LANES :])), cols4(below))
        x_ref[:, cs] = x


def solve_kernel(shift_ref, k_ref, p_ref, o_ref, m_ref, w_ref, x_ref, *, bound):
    eye, low = square_masks()
    matrix, rest = decode(p_ref, bound, eye, low)
    n = BLOCK

    def put(rows, t, c):
        u = pltpu.roll(t, HALF, 1)
        left = iota(t.shape, 1) < HALF
        m_ref[rows, 2 * c * LANES : (2 * c + 1) * LANES] = jnp.where(left, t, u)
        m_ref[rows, (2 * c + 1) * LANES : (2 * c + 2) * LANES] = jnp.where(left, u, t)

    xy, extra = rest()
    diag = split(k_ref[264:265, :] + extra)
    for r in range(2):
        for c in range(4):
            i, j = LAYOUT[r][c]
            t = k_ref[place(r, c)] + matrix(r, c)
            if (r, c) in ((0, 0), (0, 2)):
                u = t.T
                put(place(i, 0)[0], jnp.where(eye, diag[i], jnp.where(low, t, u)), i)
                put(place(j, 0)[0], jnp.where(eye, diag[j], jnp.where(low, u, t)), j)
            else:
                put(place(i, 0)[0], t, j)
    right = k_ref[256:264, :] + xy
    for c in range(4):
        put(slice(n, n + 8), right[:, c * LANES : (c + 1) * LANES], c)

    lane, sub = iota((HALF, LANES), 1), iota((HALF, LANES), 0)
    shift = jnp.where(lane % HALF == sub, jnp.where(lane < HALF, shift_ref[0], shift_ref[1]), 0.0)
    factor_solve(n, shift, m_ref, w_ref, x_ref)
    left = iota((8, LANES), 1) < HALF
    for c in range(4):
        even, odd = x_ref[:, 2 * c * LANES : (2 * c + 1) * LANES], x_ref[:, (2 * c + 1) * LANES : (2 * c + 2) * LANES]
        first = jnp.where(left, even, pltpu.roll(odd, HALF, 1))
        second = jnp.where(left, pltpu.roll(even, HALF, 1), odd)
        both = jnp.concatenate([first, second], axis=0).astype(bf16)
        for d in range(o_ref.shape[0]):
            o_ref[d, :, c * LANES : (c + 1) * LANES] = both


def predict_kernel(info_ref, x_ref, b_ref, f_ref, o_ref, *, scale):
    weights = jnp.concatenate([b_ref[info_ref[8 + k]] for k in range(FOLDS)], axis=0)
    fitted = nt(weights, x_ref[...])
    folds = f_ref[...]
    total = jnp.zeros((16, folds.shape[1]), f32)
    for k in range(FOLDS):
        total = jnp.where(folds == k, fitted[16 * k : 16 * (k + 1)], total)
    o_ref[...] = (total * scale).astype(bf16)


def cross_kernel(o_ref, j_ref, g_ref, c_ref, *, scale):
    own = o_ref[...]
    count, width = g_ref.shape[0], g_ref.shape[2]
    prior = g_ref.shape[1] // 8
    old = tree([nt(own[:, b * width : (b + 1) * width], g_ref[b]) for b in range(count)])
    new = nt(own, j_ref[...])
    t_row, t_old = iota(old.shape, 0) % 8, iota(old.shape, 1) // prior
    t_new = iota(new.shape, 1) % 8
    old = jnp.where(t_row == t_old, old, 0.0)
    new = jnp.where(iota(new.shape, 0) % 8 == t_new, new, 0.0)
    pick_old = jnp.where(iota((prior, old.shape[1]), 1) % prior == iota((prior, old.shape[1]), 0), 1.0, 0.0)
    features = new.shape[1] // 8
    pick_new = jnp.where(iota((features, new.shape[1]), 1) // 8 == iota((features, new.shape[1]), 0), 1.0, 0.0)
    high = lax.Precision.HIGHEST
    c_ref[0:prior, :] = nt(pick_old, old, high) * scale
    c_ref[prior : prior + features, :] = nt(pick_new, new, high) * scale


def make_local(mesh):
    n_blk, n_smp = mesh.shape["blk"], mesh.shape["smp"]
    if n_smp != 8:
        raise NotImplementedError(n_smp)

    def pairs(bit, sends):
        out = []
        for b in range(n_blk):
            for s in range(n_smp):
                role = s ^ (7 if b & 1 else 0)
                if sends(role & 1, role >> 1 & 1, role >> 2):
                    out.append((b * n_smp + s, b * n_smp + (s ^ bit)))
        return out

    def move(x, bit, sends):
        return lax.ppermute(x, ("blk", "smp"), pairs(bit, sends))

    def local(x, traits, folds, lambdas, guesses):
        rows = x.shape[0]
        total = rows * n_smp
        bound = BOUND * total
        mirror = 7 * (lax.axis_index("blk") & 1)
        role = lax.axis_index("smp") ^ mirror
        b0, b1, b2 = role & 1, role >> 1 & 1, role >> 2
        info = jnp.stack(
            [
                jnp.where(b0 == 0, 2, 0),
                jnp.int32(1) + 0 * b0,
                jnp.where(b0 == 0, 0, 2),
                jnp.where(b1 == 0, 4, 3),
                jnp.where(b1 == 0, 3, 4),
                jnp.where(b0 == b1, 1, 0),
                b2,
                b2,
            ]
            + [o ^ mirror for o in OWNERS]
            + [b2] * 3
        ).astype(jnp.int32)
        shift = lambdas * total
        yt = traits.T
        f_row = folds.reshape(1, rows)
        prior = jnp.transpose(guesses[0], (1, 2, 0)).reshape(-1, guesses.shape[1])

        def call(kernel, outs, specs, scratch, *args, mib=12, flops=0, **static):
            import functools

            return pl.pallas_call(
                functools.partial(kernel, **static),
                out_shape=outs,
                in_specs=specs,
                out_specs=jax.tree.map(lambda _: VMEM, outs),
                scratch_shapes=scratch,
                compiler_params=pltpu.CompilerParams(vmem_limit_bytes=mib * MIB),
                cost_estimate=pl.CostEstimate(flops=flops, bytes_accessed=4 * MIB, transcendentals=0),
            )(*args)

        def packed(*lead):
            return jax.ShapeDtypeStruct((*lead, PACKED, BLOCK), f32)

        def wire(*lead):
            return jax.ShapeDtypeStruct((*lead, WIRE, BLOCK), jnp.int16)

        def first_fold():
            s = lax.axis_index("smp") ^ (lax.axis_index("blk") & 1)
            return jnp.where(s & 1 == 0, 2, 0)

        work = pltpu.VMEM((PACKED, BLOCK), f32)
        xt = pltpu.VMEM((BLOCK, rows), bf16)
        chunks = 4
        gram_flops = 2 * rows * BLOCK * BLOCK
        m0, x_near, yt_near, f_near = call(
            gram_first_kernel,
            (
                wire(),
                jax.ShapeDtypeStruct(x.shape, bf16),
                jax.ShapeDtypeStruct((16, rows), bf16),
                jax.ShapeDtypeStruct((1, rows), jnp.int32),
            ),
            [HBM] * 3,
            [work, xt, pltpu.VMEM(yt.shape, bf16), pltpu.SemaphoreType.DMA((chunks + 2,))],
            *(pltpu.with_memory_space_constraint(v, pltpu.HBM) for v in (x, yt, f_row)),
            bound=bound,
            fold_of=first_fold,
            chunks=chunks,
            mib=14,
            flops=gram_flops,
        )
        p1 = move(m0, 1, lambda u, v, w: True)
        m1, m3, k1 = call(
            gram_send_kernel,
            (wire(), wire(), packed()),
            [SMEM, VMEM, VMEM, VMEM],
            [work, xt],
            info,
            x_near,
            yt_near,
            f_near,
            bound=bound,
            mib=14,
            flops=2 * gram_flops,
        )
        p2 = move(m1, 1, lambda u, v, w: u == 1)
        p3 = move(m3, 2, lambda u, v, w: True)
        k2, k4 = call(
            gram_keep_kernel, (packed(), packed()), [SMEM] + [VMEM] * 3, [xt], info, x_near, yt_near, f_near, mib=14, flops=2 * gram_flops
        )
        ma, mb, ka, kb = call(
            second_kernel,
            (wire(), wire(), packed(), packed()),
            [SMEM] + [VMEM] * 6,
            [work, work],
            info,
            k1,
            k2,
            k4,
            p1,
            p2,
            p3,
            bound=bound,
        )
        p4 = move(ma, 2, lambda u, v, w: (u, v) != (1, 1))
        p5 = move(mb, 1, lambda u, v, w: u == 1)
        msg, keep = call(
            third_kernel, (wire(), packed()), [SMEM] + [VMEM] * 4, [work, work], info, ka, kb, p4, p5, bound=bound
        )
        p6 = move(msg, 4, lambda u, v, w: u == 0 or (u, v, w) == (1, 1, 1))
        beta = call(
            solve_kernel,
            jax.ShapeDtypeStruct((n_smp, 16, BLOCK), bf16),
            [SMEM, VMEM, VMEM],
            [pltpu.VMEM((BLOCK + 8, 2 * BLOCK), f32), pltpu.VMEM((BLOCK + 8, 2 * BLOCK), f32), pltpu.VMEM((8, 2 * BLOCK), f32)],
            shift,
            keep,
            p6,
            bound=bound,
        )
        betas = lax.all_to_all(beta, "smp", 0, 0)
        oof = call(
            predict_kernel,
            jax.ShapeDtypeStruct((16, rows), bf16),
            [SMEM, VMEM, VMEM, VMEM],
            [],
            info,
            x_near,
            betas,
            f_near,
            scale=math.sqrt(total / BLOCK),
        )
        prior_all = lax.all_gather(prior, "blk", axis=0)
        oof_all = lax.all_gather(oof, "blk", axis=0, tiled=True)
        n_cross = prior.shape[0] // 8 + 2 * n_blk
        part = call(
            cross_kernel,
            jax.ShapeDtypeStruct((n_cross, 16), f32),
            [VMEM] * 3,
            [],
            oof,
            oof_all,
            prior_all,
            scale=1.0 / total,
        )
        part = lax.all_to_all(part.reshape(n_smp, n_cross // n_smp, 16), "smp", 0, 0)
        cross = jnp.sum(part, axis=0).reshape(n_cross // n_smp, 2, 8)
        return (
            jnp.transpose(oof.reshape(2, 8, rows), (2, 1, 0)),
            jnp.transpose(cross, (2, 1, 0)),
        )

    return local


def solution(mesh):
    return jax.shard_map(
        make_local(mesh),
        mesh=mesh,
        in_specs=(P("smp", "blk"), P("smp", None), P("smp"), P(), P("smp", "blk", None, None)),
        out_specs=(P("smp", None, "blk"), P(None, "blk", "smp")),
        check_vma=False,
    )
```

```python
import math

import jax
import jax.numpy as jnp
from jax import lax
from jax.experimental import pallas as pl
from jax.experimental.pallas import tpu as pltpu
from jax.sharding import PartitionSpec as P

BLOCK = 512
FOLDS = 5

LANES = 128
TILE = 8
HALF = 64
PACKED = 272
WIRE = 288
DIGIT = 32766.0
BOUND = 36.0
OWNERS = (0, 2, 3, 4, 6)

f32 = jnp.float32
bf16 = jnp.bfloat16
VMEM = pl.BlockSpec(memory_space=pltpu.VMEM)
SMEM = pl.BlockSpec(memory_space=pltpu.SMEM)
HBM = pl.BlockSpec(memory_space=pltpu.HBM)
MIB = 1024 * 1024


def nt(a, b, precision=None):
    return lax.dot_general(a, b, (((1,), (1,)), ((), ())), precision=precision, preferred_element_type=f32)


def iota(shape, dim):
    return lax.broadcasted_iota(jnp.int32, shape, dim)


def square_masks():
    row, col = iota((LANES, LANES), 0), iota((LANES, LANES), 1)
    return row == col, col < row


def column(row_vector, eye):
    return jnp.sum(jnp.where(eye, jnp.broadcast_to(row_vector, (LANES, LANES)), 0.0), axis=1, keepdims=True)


LAYOUT = (((0, 1), (1, 0), (2, 3), (3, 2)), ((2, 0), (2, 1), (3, 0), (3, 1)))


def place(r, c):
    return slice(r * LANES, (r + 1) * LANES), slice(c * LANES, (c + 1) * LANES)


def pair_scale(r, c, rows, cols, low):
    i, j = LAYOUT[r][c]
    if (r, c) in ((0, 0), (0, 2)):
        return jnp.where(low, cols[i] * rows[i], cols[j] * rows[j])
    return cols[i] * rows[j]


def split(vector):
    return [vector[:, i * LANES : (i + 1) * LANES] for i in range(BLOCK // LANES)]


def to_int(x):
    return jnp.floor(x + 0.5).astype(jnp.int32).astype(jnp.int16)


def digits(value, bound):
    u = value * (DIGIT / bound)
    high = jnp.floor(u)
    return high, (u - high) * DIGIT


def undigits(high, low, bound):
    return (high + low * (1.0 / DIGIT)) * (bound / DIGIT)


def encode(get, msg_ref, bound, eye, low):
    diag = get(slice(264, 265), slice(0, BLOCK))
    dh, dl = digits(diag, bound)
    dl = jnp.floor(dl + 0.5)
    scale = lax.rsqrt(undigits(dh, dl, bound) + 1e-3)
    rows = split(scale)
    cols = [column(r, eye) for r in rows]
    for r in range(2):
        for c in range(4):
            rs, cs = place(r, c)
            msg_ref[rs, cs] = to_int(get(rs, cs) * (pair_scale(r, c, rows, cols, low) * DIGIT))
    xh, xl = digits(get(slice(256, 264), slice(0, BLOCK)), bound)
    msg_ref[256:272, :] = to_int(jnp.concatenate([xh, xl], axis=0))
    spare = jnp.zeros((14, BLOCK), f32)
    msg_ref[272:288, :] = to_int(jnp.concatenate([dh, dl, spare], axis=0))


def decode(msg_ref, bound, eye, low):
    tail = msg_ref[272:288, :].astype(f32)
    diag = undigits(tail[0:1], tail[1:2], bound)
    scale = jnp.sqrt(diag + 1e-3)
    rows = split(scale)
    cols = [column(r, eye) for r in rows]

    def matrix(r, c):
        rs, cs = place(r, c)
        return msg_ref[rs, cs].astype(f32) * (pair_scale(r, c, rows, cols, low) * (1.0 / DIGIT))

    def rest():
        x = msg_ref[256:272, :].astype(f32)
        return undigits(x[0:8], x[8:16], bound), diag

    return matrix, rest


def add_message(dst_ref, src_ref, msg_ref, bound, eye, low):
    matrix, rest = decode(msg_ref, bound, eye, low)
    for r in range(2):
        for c in range(4):
            rs, cs = place(r, c)
            dst_ref[rs, cs] = src_ref[rs, cs] + matrix(r, c)
    xy, diag = rest()
    dst_ref[256:264, :] = src_ref[256:264, :] + xy
    dst_ref[264:272, :] = src_ref[264:272, :] + jnp.concatenate([diag, jnp.zeros((7, BLOCK), f32)], axis=0)


def reader(ref):
    return lambda rows, cols: ref[rows, cols]


def gram_one(fold, x_ref, xt_ref, yt_ref, f_ref, out_ref, eye, low):
    mask = jnp.where(f_ref[...] != fold, 1.0, 0.0).astype(bf16)
    g0 = jnp.dot(xt_ref[0:256, :] * mask, x_ref[:, 0:256], preferred_element_type=f32)
    lower = jnp.concatenate([xt_ref[256:BLOCK, :], yt_ref[...]], axis=0)
    g1 = jnp.dot(lower * mask, x_ref[...], preferred_element_type=f32)

    def block(i, j):
        rs, cs = place(i, j)
        return g0[rs, cs] if i < 2 else g1[(i - 2) * LANES : (i - 1) * LANES, cs]

    for r in range(2):
        for c in range(4):
            i, j = LAYOUT[r][c]
            rs, cs = place(r, c)
            if (r, c) in ((0, 0), (0, 2)):
                out_ref[rs, cs] = jnp.where(low, block(i, i), jnp.where(eye, 0.0, block(j, j)))
            else:
                out_ref[rs, cs] = block(i, j)
    diag = [jnp.sum(jnp.where(eye, block(i, i), 0.0), axis=0, keepdims=True) for i in range(4)]
    out_ref[256:264, :] = g1[256:264, :]
    out_ref[264:272, :] = jnp.concatenate([jnp.concatenate(diag, axis=1), jnp.zeros((7, BLOCK), f32)], axis=0)


def gram_first_kernel(
    x_hbm, yt_hbm, f_hbm, msg_ref, x_ref, yt_ref, f_ref, work_ref, xt_ref, in_ref, sems, *, bound, fold_of, chunks
):
    rows = x_ref.shape[0] // chunks
    small = [pltpu.make_async_copy(yt_hbm, in_ref, sems.at[chunks]), pltpu.make_async_copy(f_hbm, f_ref, sems.at[chunks + 1])]
    loads = []
    for c in range(chunks):
        part = pl.ds(c * rows, rows)
        loads.append(pltpu.make_async_copy(x_hbm.at[part], x_ref.at[part], sems.at[c]))
    for copy in loads + small:
        copy.start()
    eye, low = square_masks()
    for c, copy in enumerate(loads):
        copy.wait()
        part = slice(c * rows, (c + 1) * rows)
        xt_ref[:, part] = x_ref[part, :].T
    for copy in small:
        copy.wait()
    yt_ref[...] = jnp.concatenate([in_ref[...], jnp.zeros_like(in_ref[...])], axis=0)
    gram_one(fold_of(), x_ref, xt_ref, yt_ref, f_ref, work_ref, eye, low)
    encode(reader(work_ref), msg_ref, bound, eye, low)


def gram_send_kernel(info_ref, x_ref, yt_ref, f_ref, m1_ref, m3_ref, keep_ref, work_ref, xt_ref, *, bound):
    eye, low = square_masks()
    xt_ref[...] = x_ref[...].T
    for slot, dst, msg_ref in ((3, work_ref, m3_ref), (1, keep_ref, m1_ref)):
        gram_one(info_ref[slot], x_ref, xt_ref, yt_ref, f_ref, dst, eye, low)
        encode(reader(dst), msg_ref, bound, eye, low)


def gram_keep_kernel(info_ref, x_ref, yt_ref, f_ref, k2_ref, k4_ref, xt_ref):
    eye, low = square_masks()
    xt_ref[...] = x_ref[...].T
    for slot, dst in ((2, k2_ref), (4, k4_ref)):
        gram_one(info_ref[slot], x_ref, xt_ref, yt_ref, f_ref, dst, eye, low)


def second_kernel(
    info_ref, k1_ref, k2_ref, k4_ref, p1_ref, p2_ref, p3_ref, ma_ref, mb_ref, ka_ref, kb_ref, s1_ref, s2_ref, *, bound
):
    eye, low = square_masks()
    add_message(s2_ref, k2_ref, p1_ref, bound, eye, low)
    add_message(s1_ref, k1_ref, p2_ref, bound, eye, low)
    add_message(kb_ref, k4_ref, p3_ref, bound, eye, low)
    first = info_ref[5] == 1
    encode(lambda r, c: jnp.where(first, s1_ref[r, c], s2_ref[r, c]), ma_ref, bound, eye, low)
    encode(reader(kb_ref), mb_ref, bound, eye, low)
    ka_ref[...] = jnp.where(first, s2_ref[...], s1_ref[...])


def third_kernel(info_ref, ka_ref, kb_ref, p4_ref, p5_ref, msg_ref, keep_ref, sa_ref, sb_ref, *, bound):
    eye, low = square_masks()
    add_message(sa_ref, ka_ref, p4_ref, bound, eye, low)
    add_message(sb_ref, kb_ref, p5_ref, bound, eye, low)
    upper = info_ref[6] == 1
    encode(lambda r, c: jnp.where(upper, sa_ref[r, c], sb_ref[r, c]), msg_ref, bound, eye, low)
    keep_ref[...] = jnp.where(upper, sb_ref[...], sa_ref[...])


def sublane(x, p):
    return jnp.broadcast_to(x[p : p + 1, :], (TILE, LANES))


def tree(terms):
    terms = list(terms)
    while len(terms) > 1:
        terms = [terms[i] + terms[i + 1] if i + 1 < len(terms) else terms[i] for i in range(0, len(terms), 2)]
    return terms[0]


def invert_pair(tiles):
    lane, sub = iota((TILE, LANES), 1), iota((TILE, LANES), 0)
    col = lane % HALF
    half = lane - col
    here = [sub == p for p in range(TILE)]
    count = len(tiles)
    for g in range(count):
        inside = (col >= g * TILE) & (col < (g + 1) * TILE)
        index = [half + (g * TILE + q) for q in range(TILE)]

        def spread(t, q):
            return jnp.take_along_axis(t, index[q], axis=1)

        c = [spread(tiles[g], q) for q in range(TILE)]
        r = jnp.where(inside, jnp.where(col - g * TILE == sub, 1.0, 0.0), tiles[g])
        for p in range(0, TILE, 2):
            cp, cn = c[p], c[p + 1]
            a, b, d = sublane(cp, p), sublane(cp, p + 1), sublane(cn, p + 1)
            inv = 1.0 / (a * d - b * b)

            def eliminate(x):
                e0, e1 = sublane(x, p), sublane(x, p + 1)
                f0, f1 = d * e0 - b * e1, a * e1 - b * e0
                return jnp.where(here[p], f0 * inv, jnp.where(here[p + 1], f1 * inv, x - (cp * f0 + cn * f1) * inv))

            for q in range(p + 2, TILE):
                c[q] = eliminate(c[q])
            r = eliminate(r)
        rows = [sublane(r, p) for p in range(TILE)]
        for i in [(g + 1) % count] + [i for i in range(count) if i != g and i != (g + 1) % count]:
            t = tiles[i]
            tiles[i] = jnp.where(inside, 0.0, t) - tree([spread(t, p) * rows[p] for p in range(TILE)])
        tiles[g] = r
        yield


def block_diagonal(t):
    left = iota(t.shape, 1) < HALF
    zero = jnp.zeros_like(t)
    return jnp.concatenate([jnp.where(left, t, zero), jnp.where(left, zero, t)], axis=0)


def parts(x):
    high = x.astype(bf16)
    return high, (x - high.astype(f32)).astype(bf16)


def left4(p):
    return jnp.concatenate(p, axis=1)


def rows4(p):
    return jnp.concatenate([jnp.concatenate([q, q], axis=1) for q in p], axis=0)


def cols4(p):
    return jnp.concatenate([jnp.concatenate([q, q], axis=0) for q in p], axis=1)


def fold_halves(r):
    half = r.shape[1] // 2
    return r[:, :half] + r[:, half:]


def mm4(a, b):
    return fold_halves(lax.dot_general(a, b, (((1,), (0,)), ((), ())), preferred_element_type=f32))


def nt4(a, b):
    return fold_halves(nt(a, b))


def factor_solve(n, shift, m_ref, w_ref, x_ref):
    blocks, groups = n // HALF, HALF // TILE

    def begin(b):
        top = m_ref[b * HALF : (b + 1) * HALF, b * LANES : (b + 1) * LANES] + shift
        tiles = [top[i * TILE : (i + 1) * TILE] for i in range(groups)]
        return tiles, invert_pair(tiles)

    def run(steps, work):
        done = 0
        for g in range(groups):
            next(steps)
            todo = len(work) * (g + 1) // groups
            for k in range(done, todo):
                work[k]()
            done = todo
        for _ in steps:
            pass

    tiles, steps = begin(0)
    run(steps, [])
    for b in range(blocks):
        cs, nx = slice(b * LANES, (b + 1) * LANES), (b + 1) * HALF
        inverse = cols4(parts(block_diagonal(jnp.concatenate(tiles, axis=0))))
        panel = parts(m_ref[nx:, cs])
        left = left4(panel)
        first = HALF if nx < n else 8
        w0 = mm4(left[:first], inverse)
        w_ref[nx : nx + first, cs] = w0
        if nx >= n:
            break

        def right(j):
            lo = (j - b - 1) * HALF
            return rows4([block_diagonal(p[lo : lo + HALF]) for p in panel])

        js = slice((b + 1) * LANES, (b + 2) * LANES)
        m_ref[nx : nx + HALF, js] = m_ref[nx : nx + HALF, js] - nt4(left4(parts(w0)), right(b + 1))
        tiles, steps = begin(b + 1)
        kept = {}

        def rest():
            w = mm4(left[HALF:], inverse)
            w_ref[nx + HALF :, cs] = w
            kept["w"] = left4(parts(w))

        def trail(j):
            def go():
                jc, r0 = slice(j * LANES, (j + 1) * LANES), max(j * HALF, nx + HALF)
                m_ref[r0:, jc] = m_ref[r0:, jc] - nt4(kept["w"][r0 - nx - HALF :], right(j))

            return go

        run(steps, [rest] + [trail(j) for j in range(b + 1, blocks)])
    for b in reversed(range(blocks)):
        cs = slice(b * LANES, (b + 1) * LANES)
        x = w_ref[n:, cs]
        if b + 1 < blocks:
            below = [
                jnp.concatenate([block_diagonal(p[i * HALF : (i + 1) * HALF]) for i in range(blocks - b - 1)], axis=0)
                for p in parts(w_ref[(b + 1) * HALF : n, cs])
            ]
            x = x - mm4(left4(parts(x_ref[:, (b + 1) * LANES :])), cols4(below))
        x_ref[:, cs] = x


def solve_kernel(shift_ref, k_ref, p_ref, o_ref, m_ref, w_ref, x_ref, *, bound):
    eye, low = square_masks()
    matrix, rest = decode(p_ref, bound, eye, low)
    n = BLOCK

    def put(rows, t, c):
        u = pltpu.roll(t, HALF, 1)
        left = iota(t.shape, 1) < HALF
        m_ref[rows, 2 * c * LANES : (2 * c + 1) * LANES] = jnp.where(left, t, u)
        m_ref[rows, (2 * c + 1) * LANES : (2 * c + 2) * LANES] = jnp.where(left, u, t)

    xy, extra = rest()
    diag = split(k_ref[264:265, :] + extra)
    for r in range(2):
        for c in range(4):
            i, j = LAYOUT[r][c]
            t = k_ref[place(r, c)] + matrix(r, c)
            if (r, c) in ((0, 0), (0, 2)):
                u = t.T
                put(place(i, 0)[0], jnp.where(eye, diag[i], jnp.where(low, t, u)), i)
                put(place(j, 0)[0], jnp.where(eye, diag[j], jnp.where(low, u, t)), j)
            else:
                put(place(i, 0)[0], t, j)
    right = k_ref[256:264, :] + xy
    for c in range(4):
        put(slice(n, n + 8), right[:, c * LANES : (c + 1) * LANES], c)

    lane, sub = iota((HALF, LANES), 1), iota((HALF, LANES), 0)
    shift = jnp.where(lane % HALF == sub, jnp.where(lane < HALF, shift_ref[0], shift_ref[1]), 0.0)
    factor_solve(n, shift, m_ref, w_ref, x_ref)
    left = iota((8, LANES), 1) < HALF
    for c in range(4):
        even, odd = x_ref[:, 2 * c * LANES : (2 * c + 1) * LANES], x_ref[:, (2 * c + 1) * LANES : (2 * c + 2) * LANES]
        first = jnp.where(left, even, pltpu.roll(odd, HALF, 1))
        second = jnp.where(left, pltpu.roll(even, HALF, 1), odd)
        both = jnp.concatenate([first, second], axis=0).astype(bf16)
        for d in range(o_ref.shape[0]):
            o_ref[d, :, c * LANES : (c + 1) * LANES] = both


def predict_kernel(info_ref, x_ref, b_ref, f_ref, o_ref, *, scale):
    weights = jnp.concatenate([b_ref[info_ref[8 + k]] for k in range(FOLDS)], axis=0)
    fitted = nt(weights, x_ref[...])
    folds = f_ref[...]
    total = jnp.zeros((16, folds.shape[1]), f32)
    for k in range(FOLDS):
        total = jnp.where(folds == k, fitted[16 * k : 16 * (k + 1)], total)
    o_ref[...] = (total * scale).astype(bf16)


def cross_kernel(o_ref, j_ref, g_ref, c_ref, *, scale):
    own = o_ref[...]
    count, width = g_ref.shape[0], g_ref.shape[2]
    prior = g_ref.shape[1] // 8
    old = tree([nt(own[:, b * width : (b + 1) * width], g_ref[b]) for b in range(count)])
    new = nt(own, j_ref[...])
    t_row, t_old = iota(old.shape, 0) % 8, iota(old.shape, 1) // prior
    t_new = iota(new.shape, 1) % 8
    old = jnp.where(t_row == t_old, old, 0.0)
    new = jnp.where(iota(new.shape, 0) % 8 == t_new, new, 0.0)
    pick_old = jnp.where(iota((prior, old.shape[1]), 1) % prior == iota((prior, old.shape[1]), 0), 1.0, 0.0)
    features = new.shape[1] // 8
    pick_new = jnp.where(iota((features, new.shape[1]), 1) // 8 == iota((features, new.shape[1]), 0), 1.0, 0.0)
    high = lax.Precision.HIGHEST
    both = jnp.concatenate([nt(pick_old, old, high), nt(pick_new, new, high)], axis=0) * scale
    share = (prior + features) // c_ref.shape[0]
    for j in range(2):
        for d in range(c_ref.shape[0]):
            c_ref[d, j] = both[d * share : (d + 1) * share, 8 * j : 8 * (j + 1)]


def make_local(mesh):
    n_blk, n_smp = mesh.shape["blk"], mesh.shape["smp"]
    if n_smp != 8:
        raise NotImplementedError(n_smp)

    def pairs(bit, sends):
        out = []
        for b in range(n_blk):
            for s in range(n_smp):
                role = s ^ (7 if b & 1 else 0)
                if sends(role & 1, role >> 1 & 1, role >> 2):
                    out.append((b * n_smp + s, b * n_smp + (s ^ bit)))
        return out

    def move(x, bit, sends):
        return lax.ppermute(x, ("blk", "smp"), pairs(bit, sends))

    def local(x, traits, folds, lambdas, guesses):
        rows = x.shape[0]
        total = rows * n_smp
        bound = BOUND * total
        mirror = 7 * (lax.axis_index("blk") & 1)
        role = lax.axis_index("smp") ^ mirror
        b0, b1, b2 = role & 1, role >> 1 & 1, role >> 2
        info = jnp.stack(
            [
                jnp.where(b0 == 0, 2, 0),
                jnp.int32(1) + 0 * b0,
                jnp.where(b0 == 0, 0, 2),
                jnp.where(b1 == 0, 4, 3),
                jnp.where(b1 == 0, 3, 4),
                jnp.where(b0 == b1, 1, 0),
                b2,
                b2,
            ]
            + [o ^ mirror for o in OWNERS]
            + [b2] * 3
        ).astype(jnp.int32)
        shift = lambdas * total
        yt = traits.T
        f_row = folds.reshape(1, rows)
        prior = jnp.transpose(guesses[0], (1, 2, 0)).reshape(-1, guesses.shape[1])

        def call(kernel, outs, specs, scratch, *args, mib=12, flops=0, **static):
            import functools

            return pl.pallas_call(
                functools.partial(kernel, **static),
                out_shape=outs,
                in_specs=specs,
                out_specs=jax.tree.map(lambda _: VMEM, outs),
                scratch_shapes=scratch,
                compiler_params=pltpu.CompilerParams(vmem_limit_bytes=mib * MIB),
                cost_estimate=pl.CostEstimate(flops=flops, bytes_accessed=4 * MIB, transcendentals=0),
            )(*args)

        def packed(*lead):
            return jax.ShapeDtypeStruct((*lead, PACKED, BLOCK), f32)

        def wire(*lead):
            return jax.ShapeDtypeStruct((*lead, WIRE, BLOCK), jnp.int16)

        def first_fold():
            s = lax.axis_index("smp") ^ (lax.axis_index("blk") & 1)
            return jnp.where(s & 1 == 0, 2, 0)

        work = pltpu.VMEM((PACKED, BLOCK), f32)
        xt = pltpu.VMEM((BLOCK, rows), bf16)
        chunks = 4
        gram_flops = 2 * rows * BLOCK * BLOCK
        m0, x_near, yt_near, f_near = call(
            gram_first_kernel,
            (
                wire(),
                jax.ShapeDtypeStruct(x.shape, bf16),
                jax.ShapeDtypeStruct((16, rows), bf16),
                jax.ShapeDtypeStruct((1, rows), jnp.int32),
            ),
            [HBM] * 3,
            [work, xt, pltpu.VMEM(yt.shape, bf16), pltpu.SemaphoreType.DMA((chunks + 2,))],
            *(pltpu.with_memory_space_constraint(v, pltpu.HBM) for v in (x, yt, f_row)),
            bound=bound,
            fold_of=first_fold,
            chunks=chunks,
            mib=14,
            flops=gram_flops,
        )
        p1 = move(m0, 1, lambda u, v, w: True)
        m1, m3, k1 = call(
            gram_send_kernel,
            (wire(), wire(), packed()),
            [SMEM, VMEM, VMEM, VMEM],
            [work, xt],
            info,
            x_near,
            yt_near,
            f_near,
            bound=bound,
            mib=14,
            flops=2 * gram_flops,
        )
        p3 = move(m3, 2, lambda u, v, w: True)
        p2 = move(m1, 1, lambda u, v, w: u == 1)
        k2, k4 = call(
            gram_keep_kernel, (packed(), packed()), [SMEM] + [VMEM] * 3, [xt], info, x_near, yt_near, f_near, mib=14, flops=2 * gram_flops
        )
        ma, mb, ka, kb = call(
            second_kernel,
            (wire(), wire(), packed(), packed()),
            [SMEM] + [VMEM] * 6,
            [work, work],
            info,
            k1,
            k2,
            k4,
            p1,
            p2,
            p3,
            bound=bound,
        )
        early, ma, mb = lax.optimization_barrier((prior, ma, mb))
        p4 = move(ma, 2, lambda u, v, w: (u, v) != (1, 1))
        p5 = move(mb, 1, lambda u, v, w: u == 1)
        prior_all = lax.all_gather(early, "blk", axis=0)
        prior_all, p4 = lax.optimization_barrier((prior_all, p4))
        msg, keep = call(
            third_kernel, (wire(), packed()), [SMEM] + [VMEM] * 4, [work, work], info, ka, kb, p4, p5, bound=bound
        )
        p6 = move(msg, 4, lambda u, v, w: u == 0 or (u, v, w) == (1, 1, 1))
        beta = call(
            solve_kernel,
            jax.ShapeDtypeStruct((n_smp, 16, BLOCK), bf16),
            [SMEM, VMEM, VMEM],
            [pltpu.VMEM((BLOCK + 8, 2 * BLOCK), f32), pltpu.VMEM((BLOCK + 8, 2 * BLOCK), f32), pltpu.VMEM((8, 2 * BLOCK), f32)],
            shift,
            keep,
            p6,
            bound=bound,
        )
        betas = lax.all_to_all(beta, "smp", 0, 0)
        oof = call(
            predict_kernel,
            jax.ShapeDtypeStruct((16, rows), bf16),
            [SMEM, VMEM, VMEM, VMEM],
            [],
            info,
            x_near,
            betas,
            f_near,
            scale=math.sqrt(total / BLOCK),
        )
        oof_all = lax.all_gather(oof, "blk", axis=0, tiled=True)
        n_cross = prior.shape[0] // 8 + 2 * n_blk
        part = call(
            cross_kernel,
            jax.ShapeDtypeStruct((n_smp, 2, n_cross // n_smp, 8), f32),
            [VMEM] * 3,
            [],
            oof,
            oof_all,
            prior_all,
            scale=1.0 / total,
        )
        cross = jnp.sum(lax.all_to_all(part, "smp", 0, 0), axis=0)
        return (
            jnp.transpose(oof.reshape(2, 8, rows), (2, 1, 0)),
            jnp.transpose(cross, (2, 0, 1)),
        )

    return local


def solution(mesh):
    return jax.shard_map(
        make_local(mesh),
        mesh=mesh,
        in_specs=(P("smp", "blk"), P("smp", None), P("smp"), P(), P("smp", "blk", None, None)),
        out_specs=(P("smp", None, "blk"), P(None, "blk", "smp")),
        check_vma=False,
    )
```

```python
import math

import jax
import jax.numpy as jnp
from jax import lax
from jax.experimental import pallas as pl
from jax.experimental.pallas import tpu as pltpu
from jax.sharding import PartitionSpec as P

BLOCK = 512
FOLDS = 5

LANES = 128
TILE = 8
HALF = 64
PACKED = 272
WIRE = 288
DIGIT = 32766.0
BOUND = 36.0
OWNERS = (0, 2, 3, 4, 6)

f32 = jnp.float32
bf16 = jnp.bfloat16
VMEM = pl.BlockSpec(memory_space=pltpu.VMEM)
SMEM = pl.BlockSpec(memory_space=pltpu.SMEM)
HBM = pl.BlockSpec(memory_space=pltpu.HBM)
MIB = 1024 * 1024


def nt(a, b, precision=None):
    return lax.dot_general(a, b, (((1,), (1,)), ((), ())), precision=precision, preferred_element_type=f32)


def iota(shape, dim):
    return lax.broadcasted_iota(jnp.int32, shape, dim)


def square_masks():
    row, col = iota((LANES, LANES), 0), iota((LANES, LANES), 1)
    return row == col, col < row


def column(row_vector, eye):
    return jnp.sum(jnp.where(eye, jnp.broadcast_to(row_vector, (LANES, LANES)), 0.0), axis=1, keepdims=True)


LAYOUT = (((0, 1), (1, 0), (2, 3), (3, 2)), ((2, 0), (2, 1), (3, 0), (3, 1)))


def place(r, c):
    return slice(r * LANES, (r + 1) * LANES), slice(c * LANES, (c + 1) * LANES)


def pair_scale(r, c, rows, cols, low):
    i, j = LAYOUT[r][c]
    if (r, c) in ((0, 0), (0, 2)):
        return jnp.where(low, cols[i] * rows[i], cols[j] * rows[j])
    return cols[i] * rows[j]


def split(vector):
    return [vector[:, i * LANES : (i + 1) * LANES] for i in range(BLOCK // LANES)]


def to_int(x):
    return jnp.floor(x + 0.5).astype(jnp.int32).astype(jnp.int16)


def digits(value, bound):
    u = value * (DIGIT / bound)
    high = jnp.floor(u)
    return high, (u - high) * DIGIT


def undigits(high, low, bound):
    return (high + low * (1.0 / DIGIT)) * (bound / DIGIT)


def encode(get, msg_ref, bound, eye, low):
    diag = get(slice(264, 265), slice(0, BLOCK))
    dh, dl = digits(diag, bound)
    dl = jnp.floor(dl + 0.5)
    scale = lax.rsqrt(undigits(dh, dl, bound) + 1e-3)
    rows = split(scale)
    cols = [column(r, eye) for r in rows]
    for r in range(2):
        for c in range(4):
            rs, cs = place(r, c)
            msg_ref[rs, cs] = to_int(get(rs, cs) * (pair_scale(r, c, rows, cols, low) * DIGIT))
    xh, xl = digits(get(slice(256, 264), slice(0, BLOCK)), bound)
    msg_ref[256:272, :] = to_int(jnp.concatenate([xh, xl], axis=0))
    spare = jnp.zeros((14, BLOCK), f32)
    msg_ref[272:288, :] = to_int(jnp.concatenate([dh, dl, spare], axis=0))


def decode(msg_ref, bound, eye, low):
    tail = msg_ref[272:288, :].astype(f32)
    diag = undigits(tail[0:1], tail[1:2], bound)
    scale = jnp.sqrt(diag + 1e-3)
    rows = split(scale)
    cols = [column(r, eye) for r in rows]

    def matrix(r, c):
        rs, cs = place(r, c)
        return msg_ref[rs, cs].astype(f32) * (pair_scale(r, c, rows, cols, low) * (1.0 / DIGIT))

    def rest():
        x = msg_ref[256:272, :].astype(f32)
        return undigits(x[0:8], x[8:16], bound), diag

    return matrix, rest


def add_message(dst_ref, src_ref, msg_ref, bound, eye, low):
    matrix, rest = decode(msg_ref, bound, eye, low)
    for r in range(2):
        for c in range(4):
            rs, cs = place(r, c)
            dst_ref[rs, cs] = src_ref[rs, cs] + matrix(r, c)
    xy, diag = rest()
    dst_ref[256:264, :] = src_ref[256:264, :] + xy
    dst_ref[264:272, :] = src_ref[264:272, :] + jnp.concatenate([diag, jnp.zeros((7, BLOCK), f32)], axis=0)


def reader(ref):
    return lambda rows, cols: ref[rows, cols]


def gram_one(fold, x_ref, xt_ref, yt_ref, f_ref, out_ref, eye, low):
    mask = jnp.where(f_ref[...] != fold, 1.0, 0.0).astype(bf16)
    g0 = jnp.dot(xt_ref[0:256, :] * mask, x_ref[:, 0:256], preferred_element_type=f32)
    lower = jnp.concatenate([xt_ref[256:BLOCK, :], yt_ref[...]], axis=0)
    g1 = jnp.dot(lower * mask, x_ref[...], preferred_element_type=f32)

    def block(i, j):
        rs, cs = place(i, j)
        return g0[rs, cs] if i < 2 else g1[(i - 2) * LANES : (i - 1) * LANES, cs]

    for r in range(2):
        for c in range(4):
            i, j = LAYOUT[r][c]
            rs, cs = place(r, c)
            if (r, c) in ((0, 0), (0, 2)):
                out_ref[rs, cs] = jnp.where(low, block(i, i), jnp.where(eye, 0.0, block(j, j)))
            else:
                out_ref[rs, cs] = block(i, j)
    diag = [jnp.sum(jnp.where(eye, block(i, i), 0.0), axis=0, keepdims=True) for i in range(4)]
    out_ref[256:264, :] = g1[256:264, :]
    out_ref[264:272, :] = jnp.concatenate([jnp.concatenate(diag, axis=1), jnp.zeros((7, BLOCK), f32)], axis=0)


def gram_first_kernel(
    x_hbm, yt_hbm, f_hbm, msg_ref, x_ref, yt_ref, f_ref, work_ref, xt_ref, in_ref, sems, *, bound, roles, chunks
):
    rows = x_ref.shape[0] // chunks
    small = [pltpu.make_async_copy(yt_hbm, in_ref, sems.at[chunks]), pltpu.make_async_copy(f_hbm, f_ref, sems.at[chunks + 1])]
    loads = []
    for c in range(chunks):
        part = pl.ds(c * rows, rows)
        loads.append(pltpu.make_async_copy(x_hbm.at[part], x_ref.at[part], sems.at[c]))
    for copy in loads + small:
        copy.start()
    eye, low = square_masks()
    for c, copy in enumerate(loads):
        copy.wait()
        part = slice(c * rows, (c + 1) * rows)
        xt_ref[:, part] = x_ref[part, :].T
    for copy in small:
        copy.wait()
    yt_ref[...] = jnp.concatenate([in_ref[...], jnp.zeros_like(in_ref[...])], axis=0)
    gram_one(roles()[0], x_ref, xt_ref, yt_ref, f_ref, work_ref, eye, low)
    encode(reader(work_ref), msg_ref, bound, eye, low)


def gram_send_kernel(x_ref, yt_ref, f_ref, m1_ref, m3_ref, keep_ref, work_ref, xt_ref, *, bound, roles):
    eye, low = square_masks()
    info = roles()
    xt_ref[...] = x_ref[...].T
    for slot, dst, msg_ref in ((3, work_ref, m3_ref), (1, keep_ref, m1_ref)):
        gram_one(info[slot], x_ref, xt_ref, yt_ref, f_ref, dst, eye, low)
        encode(reader(dst), msg_ref, bound, eye, low)


def gram_keep_kernel(x_ref, yt_ref, f_ref, k2_ref, k4_ref, xt_ref, *, roles):
    eye, low = square_masks()
    info = roles()
    xt_ref[...] = x_ref[...].T
    for slot, dst in ((2, k2_ref), (4, k4_ref)):
        gram_one(info[slot], x_ref, xt_ref, yt_ref, f_ref, dst, eye, low)


def second_kernel(
    k1_ref, k2_ref, k4_ref, p1_ref, p2_ref, p3_ref, ma_ref, mb_ref, ka_ref, kb_ref, s1_ref, s2_ref, *, bound, roles
):
    eye, low = square_masks()
    add_message(s2_ref, k2_ref, p1_ref, bound, eye, low)
    add_message(s1_ref, k1_ref, p2_ref, bound, eye, low)
    add_message(kb_ref, k4_ref, p3_ref, bound, eye, low)
    first = roles()[5] == 1
    encode(lambda r, c: jnp.where(first, s1_ref[r, c], s2_ref[r, c]), ma_ref, bound, eye, low)
    encode(reader(kb_ref), mb_ref, bound, eye, low)
    ka_ref[...] = jnp.where(first, s2_ref[...], s1_ref[...])


def third_kernel(ka_ref, kb_ref, p4_ref, p5_ref, msg_ref, keep_ref, sa_ref, sb_ref, *, bound, roles):
    eye, low = square_masks()
    add_message(sa_ref, ka_ref, p4_ref, bound, eye, low)
    add_message(sb_ref, kb_ref, p5_ref, bound, eye, low)
    upper = roles()[6] == 1
    encode(lambda r, c: jnp.where(upper, sa_ref[r, c], sb_ref[r, c]), msg_ref, bound, eye, low)
    keep_ref[...] = jnp.where(upper, sb_ref[...], sa_ref[...])


def sublane(x, p):
    return jnp.broadcast_to(x[p : p + 1, :], (TILE, LANES))


def tree(terms):
    terms = list(terms)
    while len(terms) > 1:
        terms = [terms[i] + terms[i + 1] if i + 1 < len(terms) else terms[i] for i in range(0, len(terms), 2)]
    return terms[0]


def invert_pair(tiles):
    lane, sub = iota((TILE, LANES), 1), iota((TILE, LANES), 0)
    col = lane % HALF
    half = lane - col
    here = [sub == p for p in range(TILE)]
    count = len(tiles)
    for g in range(count):
        inside = (col >= g * TILE) & (col < (g + 1) * TILE)
        index = [half + (g * TILE + q) for q in range(TILE)]

        def spread(t, q):
            return jnp.take_along_axis(t, index[q], axis=1)

        others = [(g + 1) % count] + [i for i in range(count) if i != g and i != (g + 1) % count]
        lanes = [[None] * TILE for _ in range(count)]
        for q in range(TILE):
            for i in [g] + others:
                lanes[i][q] = spread(tiles[i], q)
        c = list(lanes[g])
        r = jnp.where(inside, jnp.where(col - g * TILE == sub, 1.0, 0.0), tiles[g])
        for p in range(0, TILE, 2):
            cp, cn = c[p], c[p + 1]
            a, b, d = sublane(cp, p), sublane(cp, p + 1), sublane(cn, p + 1)
            inv = 1.0 / (a * d - b * b)

            def eliminate(x):
                e0, e1 = sublane(x, p), sublane(x, p + 1)
                f0, f1 = d * e0 - b * e1, a * e1 - b * e0
                return jnp.where(here[p], f0 * inv, jnp.where(here[p + 1], f1 * inv, x - (cp * f0 + cn * f1) * inv))

            for q in range(p + 2, TILE):
                c[q] = eliminate(c[q])
            r = eliminate(r)
        rows = [sublane(r, p) for p in range(TILE)]
        for i in others:
            tiles[i] = jnp.where(inside, 0.0, tiles[i]) - tree([lanes[i][p] * rows[p] for p in range(TILE)])
        tiles[g] = r
        yield


def block_diagonal(t):
    left = iota(t.shape, 1) < HALF
    zero = jnp.zeros_like(t)
    return jnp.concatenate([jnp.where(left, t, zero), jnp.where(left, zero, t)], axis=0)


def parts(x):
    high = x.astype(bf16)
    return high, (x - high.astype(f32)).astype(bf16)


def left4(p):
    return jnp.concatenate(p, axis=1)


def rows4(p):
    return jnp.concatenate([jnp.concatenate([q, q], axis=1) for q in p], axis=0)


def cols4(p):
    return jnp.concatenate([jnp.concatenate([q, q], axis=0) for q in p], axis=1)


def fold_halves(r):
    half = r.shape[1] // 2
    return r[:, :half] + r[:, half:]


def mm4(a, b):
    return fold_halves(lax.dot_general(a, b, (((1,), (0,)), ((), ())), preferred_element_type=f32))


def nt4(a, b):
    return fold_halves(nt(a, b))


def factor_solve(n, shift, m_ref, w_ref, x_ref):
    blocks, groups = n // HALF, HALF // TILE

    def begin(b):
        top = m_ref[b * HALF : (b + 1) * HALF, b * LANES : (b + 1) * LANES] + shift
        tiles = [top[i * TILE : (i + 1) * TILE] for i in range(groups)]
        return tiles, invert_pair(tiles)

    def run(steps, work):
        done = 0
        for g in range(groups):
            next(steps)
            todo = len(work) * (g + 1) // groups
            for k in range(done, todo):
                work[k]()
            done = todo
        for _ in steps:
            pass

    tiles, steps = begin(0)
    run(steps, [])
    for b in range(blocks):
        cs, nx = slice(b * LANES, (b + 1) * LANES), (b + 1) * HALF
        inverse = cols4(parts(block_diagonal(jnp.concatenate(tiles, axis=0))))
        panel = parts(m_ref[nx:, cs])
        left = left4(panel)
        first = HALF if nx < n else 8
        w0 = mm4(left[:first], inverse)
        w_ref[nx : nx + first, cs] = w0
        if nx >= n:
            break

        def right(j):
            lo = (j - b - 1) * HALF
            return rows4([block_diagonal(p[lo : lo + HALF]) for p in panel])

        js = slice((b + 1) * LANES, (b + 2) * LANES)
        m_ref[nx : nx + HALF, js] = m_ref[nx : nx + HALF, js] - nt4(left4(parts(w0)), right(b + 1))
        tiles, steps = begin(b + 1)
        kept = {}

        def rest():
            w = mm4(left[HALF:], inverse)
            w_ref[nx + HALF :, cs] = w
            kept["w"] = left4(parts(w))

        def trail(j):
            def go():
                jc, r0 = slice(j * LANES, (j + 1) * LANES), max(j * HALF, nx + HALF)
                m_ref[r0:, jc] = m_ref[r0:, jc] - nt4(kept["w"][r0 - nx - HALF :], right(j))

            return go

        run(steps, [rest] + [trail(j) for j in range(b + 1, blocks)])
    for b in reversed(range(blocks)):
        cs = slice(b * LANES, (b + 1) * LANES)
        x = w_ref[n:, cs]
        if b + 1 < blocks:
            below = [
                jnp.concatenate([block_diagonal(p[i * HALF : (i + 1) * HALF]) for i in range(blocks - b - 1)], axis=0)
                for p in parts(w_ref[(b + 1) * HALF : n, cs])
            ]
            x = x - mm4(left4(parts(x_ref[:, (b + 1) * LANES :])), cols4(below))
        x_ref[:, cs] = x


def solve_kernel(lambda_ref, k_ref, p_ref, o_ref, m_ref, w_ref, x_ref, *, bound, total):
    eye, low = square_masks()
    matrix, rest = decode(p_ref, bound, eye, low)
    n = BLOCK

    def put(rows, t, c):
        u = pltpu.roll(t, HALF, 1)
        left = iota(t.shape, 1) < HALF
        m_ref[rows, 2 * c * LANES : (2 * c + 1) * LANES] = jnp.where(left, t, u)
        m_ref[rows, (2 * c + 1) * LANES : (2 * c + 2) * LANES] = jnp.where(left, u, t)

    xy, extra = rest()
    diag = split(k_ref[264:265, :] + extra)
    for r in range(2):
        for c in range(4):
            i, j = LAYOUT[r][c]
            t = k_ref[place(r, c)] + matrix(r, c)
            if (r, c) in ((0, 0), (0, 2)):
                u = t.T
                put(place(i, 0)[0], jnp.where(eye, diag[i], jnp.where(low, t, u)), i)
                put(place(j, 0)[0], jnp.where(eye, diag[j], jnp.where(low, u, t)), j)
            else:
                put(place(i, 0)[0], t, j)
    right = k_ref[256:264, :] + xy
    for c in range(4):
        put(slice(n, n + 8), right[:, c * LANES : (c + 1) * LANES], c)

    lane, sub = iota((HALF, LANES), 1), iota((HALF, LANES), 0)
    shift = jnp.where(lane % HALF == sub, jnp.where(lane < HALF, lambda_ref[0] * total, lambda_ref[1] * total), 0.0)
    factor_solve(n, shift, m_ref, w_ref, x_ref)
    left = iota((8, LANES), 1) < HALF
    for c in range(4):
        even, odd = x_ref[:, 2 * c * LANES : (2 * c + 1) * LANES], x_ref[:, (2 * c + 1) * LANES : (2 * c + 2) * LANES]
        first = jnp.where(left, even, pltpu.roll(odd, HALF, 1))
        second = jnp.where(left, pltpu.roll(even, HALF, 1), odd)
        both = jnp.concatenate([first, second], axis=0).astype(bf16)
        for d in range(o_ref.shape[0]):
            o_ref[d, :, c * LANES : (c + 1) * LANES] = both


def predict_kernel(x_ref, b_ref, f_ref, o_ref, *, scale, roles):
    info = roles()
    weights = jnp.concatenate([b_ref[info[7 + k]] for k in range(FOLDS)], axis=0)
    fitted = nt(weights, x_ref[...])
    folds = f_ref[...]
    total = jnp.zeros((16, folds.shape[1]), f32)
    for k in range(FOLDS):
        total = jnp.where(folds == k, fitted[16 * k : 16 * (k + 1)], total)
    o_ref[...] = (total * scale).astype(bf16)


def cross_kernel(o_ref, j_ref, g_ref, c_ref, *, scale):
    own = o_ref[...]
    count, width = g_ref.shape[0], g_ref.shape[2]
    prior = g_ref.shape[1] // 8
    old = tree([nt(own[:, b * width : (b + 1) * width], g_ref[b]) for b in range(count)])
    new = nt(own, j_ref[...])
    t_row, t_old = iota(old.shape, 0) % 8, iota(old.shape, 1) // prior
    t_new = iota(new.shape, 1) % 8
    old = jnp.where(t_row == t_old, old, 0.0)
    new = jnp.where(iota(new.shape, 0) % 8 == t_new, new, 0.0)
    pick_old = jnp.where(iota((prior, old.shape[1]), 1) % prior == iota((prior, old.shape[1]), 0), 1.0, 0.0)
    features = new.shape[1] // 8
    pick_new = jnp.where(iota((features, new.shape[1]), 1) // 8 == iota((features, new.shape[1]), 0), 1.0, 0.0)
    high = lax.Precision.HIGHEST
    both = jnp.concatenate([nt(pick_old, old, high), nt(pick_new, new, high)], axis=0) * scale
    share = (prior + features) // c_ref.shape[0]
    for j in range(2):
        for d in range(c_ref.shape[0]):
            c_ref[d, j] = both[d * share : (d + 1) * share, 8 * j : 8 * (j + 1)]


def make_local(mesh):
    n_blk, n_smp = mesh.shape["blk"], mesh.shape["smp"]
    if n_smp != 8:
        raise NotImplementedError(n_smp)

    def pairs(bit, sends):
        out = []
        for b in range(n_blk):
            for s in range(n_smp):
                role = s ^ (7 if b & 1 else 0)
                if sends(role & 1, role >> 1 & 1, role >> 2):
                    out.append((b * n_smp + s, b * n_smp + (s ^ bit)))
        return out

    def move(x, bit, sends):
        return lax.ppermute(x, ("blk", "smp"), pairs(bit, sends))

    def local(x, traits, folds, lambdas, guesses):
        rows = x.shape[0]
        total = rows * n_smp
        bound = BOUND * total
        yt = traits.T
        f_row = folds.reshape(1, rows)
        prior = jnp.transpose(guesses[0], (1, 2, 0)).reshape(-1, guesses.shape[1])

        def call(kernel, outs, specs, scratch, *args, mib=12, flops=0, **static):
            import functools

            return pl.pallas_call(
                functools.partial(kernel, **static),
                out_shape=outs,
                in_specs=specs,
                out_specs=jax.tree.map(lambda _: VMEM, outs),
                scratch_shapes=scratch,
                compiler_params=pltpu.CompilerParams(vmem_limit_bytes=mib * MIB),
                cost_estimate=pl.CostEstimate(flops=flops, bytes_accessed=4 * MIB, transcendentals=0),
            )(*args)

        def packed(*lead):
            return jax.ShapeDtypeStruct((*lead, PACKED, BLOCK), f32)

        def wire(*lead):
            return jax.ShapeDtypeStruct((*lead, WIRE, BLOCK), jnp.int16)

        def roles():
            mirror = 7 * (lax.axis_index("blk") & 1)
            role = lax.axis_index("smp") ^ mirror
            b0, b1, b2 = role & 1, role >> 1 & 1, role >> 2
            return [2 - 2 * b0, 1, 2 * b0, 4 - b1, 3 + b1, jnp.where(b0 == b1, 1, 0), b2] + [o ^ mirror for o in OWNERS]

        work = pltpu.VMEM((PACKED, BLOCK), f32)
        xt = pltpu.VMEM((BLOCK, rows), bf16)
        chunks = 4
        gram_flops = 2 * rows * BLOCK * BLOCK
        m0, x_near, yt_near, f_near = call(
            gram_first_kernel,
            (
                wire(),
                jax.ShapeDtypeStruct(x.shape, bf16),
                jax.ShapeDtypeStruct((16, rows), bf16),
                jax.ShapeDtypeStruct((1, rows), jnp.int32),
            ),
            [HBM] * 3,
            [work, xt, pltpu.VMEM(yt.shape, bf16), pltpu.SemaphoreType.DMA((chunks + 2,))],
            *(pltpu.with_memory_space_constraint(v, pltpu.HBM) for v in (x, yt, f_row)),
            bound=bound,
            roles=roles,
            chunks=chunks,
            mib=14,
            flops=gram_flops,
        )
        p1 = move(m0, 1, lambda u, v, w: True)
        m1, m3, k1 = call(
            gram_send_kernel,
            (wire(), wire(), packed()),
            [VMEM, VMEM, VMEM],
            [work, xt],
            x_near,
            yt_near,
            f_near,
            bound=bound,
            roles=roles,
            mib=14,
            flops=2 * gram_flops,
        )
        p3 = move(m3, 2, lambda u, v, w: True)
        p2 = move(m1, 1, lambda u, v, w: u == 1)
        k2, k4 = call(
            gram_keep_kernel, (packed(), packed()), [VMEM] * 3, [xt], x_near, yt_near, f_near, roles=roles, mib=14, flops=2 * gram_flops
        )
        ma, mb, ka, kb = call(
            second_kernel,
            (wire(), wire(), packed(), packed()),
            [VMEM] * 6,
            [work, work],
            k1,
            k2,
            k4,
            p1,
            p2,
            p3,
            bound=bound,
            roles=roles,
        )
        early, ma, mb = lax.optimization_barrier((prior, ma, mb))
        p4 = move(ma, 2, lambda u, v, w: (u, v) != (1, 1))
        p5 = move(mb, 1, lambda u, v, w: u == 1)
        prior_all = lax.all_gather(early, "blk", axis=0)
        prior_all, p4 = lax.optimization_barrier((prior_all, p4))
        msg, keep = call(
            third_kernel, (wire(), packed()), [VMEM] * 4, [work, work], ka, kb, p4, p5, bound=bound, roles=roles
        )
        p6 = move(msg, 4, lambda u, v, w: u == 0 or (u, v, w) == (1, 1, 1))
        beta = call(
            solve_kernel,
            jax.ShapeDtypeStruct((n_smp, 16, BLOCK), bf16),
            [SMEM, VMEM, VMEM],
            [pltpu.VMEM((BLOCK + 8, 2 * BLOCK), f32), pltpu.VMEM((BLOCK + 8, 2 * BLOCK), f32), pltpu.VMEM((8, 2 * BLOCK), f32)],
            lambdas,
            keep,
            p6,
            bound=bound,
            total=float(total),
        )
        betas = lax.all_to_all(beta, "smp", 0, 0)
        oof = call(
            predict_kernel,
            jax.ShapeDtypeStruct((16, rows), bf16),
            [VMEM, VMEM, VMEM],
            [],
            x_near,
            betas,
            f_near,
            scale=math.sqrt(total / BLOCK),
            roles=roles,
        )
        oof_all = lax.all_gather(oof, "blk", axis=0, tiled=True)
        n_cross = prior.shape[0] // 8 + 2 * n_blk
        part = call(
            cross_kernel,
            jax.ShapeDtypeStruct((n_smp, 2, n_cross // n_smp, 8), f32),
            [VMEM] * 3,
            [],
            oof,
            oof_all,
            prior_all,
            scale=1.0 / total,
        )
        cross = jnp.sum(lax.all_to_all(part, "smp", 0, 0), axis=0)
        return (
            jnp.transpose(oof.reshape(2, 8, rows), (2, 1, 0)),
            jnp.transpose(cross, (2, 0, 1)),
        )

    return local


def solution(mesh):
    return jax.shard_map(
        make_local(mesh),
        mesh=mesh,
        in_specs=(P("smp", "blk"), P("smp", None), P("smp"), P(), P("smp", "blk", None, None)),
        out_specs=(P("smp", None, "blk"), P(None, "blk", "smp")),
        check_vma=False,
    )
```

```python
import math

import jax
import jax.numpy as jnp
from jax import lax
from jax.experimental import pallas as pl
from jax.experimental.pallas import tpu as pltpu
from jax.sharding import PartitionSpec as P

BLOCK = 512
FOLDS = 5

LANES = 128
TILE = 8
HALF = 64
PACKED = 272
WIRE = 272
DIGIT = 32766.0
BOUND = 36.0
OWNERS = (0, 2, 3, 4, 6)

f32 = jnp.float32
bf16 = jnp.bfloat16
VMEM = pl.BlockSpec(memory_space=pltpu.VMEM)
HBM = pl.BlockSpec(memory_space=pltpu.HBM)
MIB = 1024 * 1024


def nt(a, b, precision=None):
    return lax.dot_general(a, b, (((1,), (1,)), ((), ())), precision=precision, preferred_element_type=f32)


def iota(shape, dim):
    return lax.broadcasted_iota(jnp.int32, shape, dim)


def square_masks():
    row, col = iota((LANES, LANES), 0), iota((LANES, LANES), 1)
    return row == col, col < row


def column(row_vector, eye):
    return jnp.sum(jnp.where(eye, jnp.broadcast_to(row_vector, (LANES, LANES)), 0.0), axis=1, keepdims=True)


LAYOUT = (((0, 1), (1, 0), (2, 3), (3, 2)), ((2, 0), (2, 1), (3, 0), (3, 1)))


def place(r, c):
    return slice(r * LANES, (r + 1) * LANES), slice(c * LANES, (c + 1) * LANES)


def pair_scale(r, c, rows, cols, low):
    i, j = LAYOUT[r][c]
    if (r, c) in ((0, 0), (0, 2)):
        return jnp.where(low, cols[i] * rows[i], cols[j] * rows[j])
    return cols[i] * rows[j]


def split(vector):
    return [vector[:, i * LANES : (i + 1) * LANES] for i in range(BLOCK // LANES)]


def to_int(x):
    return jnp.floor(x + 0.5).astype(jnp.int32).astype(jnp.int16)


def digits(value, bound):
    u = value * (DIGIT / bound)
    high = jnp.floor(u)
    return high, (u - high) * DIGIT


def undigits(high, low, bound):
    return (high + low * (1.0 / DIGIT)) * (bound / DIGIT)


def encode(get, msg_ref, bound, eye, low):
    diag = get(slice(264, 265), slice(0, BLOCK))
    dh, dl = digits(diag, bound)
    dl = jnp.floor(dl + 0.5)
    scale = lax.rsqrt(undigits(dh, dl, bound) + 1e-3)
    rows = split(scale)
    cols = [column(r, eye) for r in rows]
    for r in range(2):
        for c in range(4):
            rs, cs = place(r, c)
            msg_ref[rs, cs] = to_int(get(rs, cs) * (pair_scale(r, c, rows, cols, low) * DIGIT))
    xy = get(slice(256, 264), slice(0, BLOCK)) * scale
    mh, ml = digits(jnp.max(jnp.abs(xy), axis=1, keepdims=True), bound)
    ml = jnp.floor(ml + 0.5)
    xy = xy * (DIGIT / (undigits(mh, ml, bound) + 1e-2))
    wide = [jnp.broadcast_to(v, (TILE, LANES)) for v in (mh, ml)]
    deep = [jnp.concatenate([*split(v), jnp.zeros((4, LANES), f32)], axis=0) for v in (dh, dl)]
    msg_ref[256:272, :] = to_int(jnp.concatenate([xy, jnp.concatenate(wide + deep, axis=1)], axis=0))


def decode(msg_ref, bound, eye, low):
    tail = msg_ref[256:272, :].astype(f32)
    top = undigits(tail[8:16, 0:LANES], tail[8:16, LANES : 2 * LANES], bound)
    deep = undigits(tail[8:12, 2 * LANES : 3 * LANES], tail[8:12, 3 * LANES : 4 * LANES], bound)
    diag = jnp.concatenate([deep[i : i + 1] for i in range(4)], axis=1)
    scale = jnp.sqrt(diag + 1e-3)
    rows = split(scale)
    cols = [column(r, eye) for r in rows]

    def matrix(r, c):
        rs, cs = place(r, c)
        return msg_ref[rs, cs].astype(f32) * (pair_scale(r, c, rows, cols, low) * (1.0 / DIGIT))

    def rest():
        return tail[0:8] * ((top[:, 0:1] + 1e-2) * (1.0 / DIGIT)) * scale, diag

    return matrix, rest


def add_message(dst_ref, src_ref, msg_ref, bound, eye, low):
    matrix, rest = decode(msg_ref, bound, eye, low)
    for r in range(2):
        for c in range(4):
            rs, cs = place(r, c)
            dst_ref[rs, cs] = src_ref[rs, cs] + matrix(r, c)
    xy, diag = rest()
    dst_ref[256:264, :] = src_ref[256:264, :] + xy
    dst_ref[264:272, :] = src_ref[264:272, :] + jnp.concatenate([diag, jnp.zeros((7, BLOCK), f32)], axis=0)


def reader(ref):
    return lambda rows, cols: ref[rows, cols]


def gram_one(fold, x_ref, xt_ref, yt_ref, f_ref, out_ref, eye, low):
    mask = jnp.where(f_ref[...] != fold, 1.0, 0.0).astype(bf16)
    g0 = jnp.dot(xt_ref[0:256, :] * mask, x_ref[:, 0:256], preferred_element_type=f32)
    lower = jnp.concatenate([xt_ref[256:BLOCK, :], yt_ref[...]], axis=0)
    g1 = jnp.dot(lower * mask, x_ref[...], preferred_element_type=f32)

    def block(i, j):
        rs, cs = place(i, j)
        return g0[rs, cs] if i < 2 else g1[(i - 2) * LANES : (i - 1) * LANES, cs]

    for r in range(2):
        for c in range(4):
            i, j = LAYOUT[r][c]
            rs, cs = place(r, c)
            if (r, c) in ((0, 0), (0, 2)):
                out_ref[rs, cs] = jnp.where(low, block(i, i), jnp.where(eye, 0.0, block(j, j)))
            else:
                out_ref[rs, cs] = block(i, j)
    diag = [jnp.sum(jnp.where(eye, block(i, i), 0.0), axis=0, keepdims=True) for i in range(4)]
    out_ref[256:264, :] = g1[256:264, :]
    out_ref[264:272, :] = jnp.concatenate([jnp.concatenate(diag, axis=1), jnp.zeros((7, BLOCK), f32)], axis=0)


def gram_first_kernel(
    x_hbm, yt_hbm, f_hbm, msg_ref, x_ref, yt_ref, f_ref, work_ref, xt_ref, in_ref, sems, *, bound, roles, chunks
):
    rows = x_ref.shape[0] // chunks
    small = [pltpu.make_async_copy(yt_hbm, in_ref, sems.at[chunks]), pltpu.make_async_copy(f_hbm, f_ref, sems.at[chunks + 1])]
    loads = []
    for c in range(chunks):
        part = pl.ds(c * rows, rows)
        loads.append(pltpu.make_async_copy(x_hbm.at[part], x_ref.at[part], sems.at[c]))
    for copy in loads + small:
        copy.start()
    eye, low = square_masks()
    for c, copy in enumerate(loads):
        copy.wait()
        part = slice(c * rows, (c + 1) * rows)
        xt_ref[:, part] = x_ref[part, :].T
    for copy in small:
        copy.wait()
    yt_ref[...] = jnp.concatenate([in_ref[...], jnp.zeros_like(in_ref[...])], axis=0)
    gram_one(roles()[0], x_ref, xt_ref, yt_ref, f_ref, work_ref, eye, low)
    encode(reader(work_ref), msg_ref, bound, eye, low)


def gram_send_kernel(x_ref, yt_ref, f_ref, m1_ref, m3_ref, keep_ref, work_ref, xt_ref, *, bound, roles):
    eye, low = square_masks()
    info = roles()
    xt_ref[...] = x_ref[...].T
    for slot, dst, msg_ref in ((3, work_ref, m3_ref), (1, keep_ref, m1_ref)):
        gram_one(info[slot], x_ref, xt_ref, yt_ref, f_ref, dst, eye, low)
        encode(reader(dst), msg_ref, bound, eye, low)


def gram_keep_kernel(x_ref, yt_ref, f_ref, k2_ref, k4_ref, xt_ref, *, roles):
    eye, low = square_masks()
    info = roles()
    xt_ref[...] = x_ref[...].T
    for slot, dst in ((2, k2_ref), (4, k4_ref)):
        gram_one(info[slot], x_ref, xt_ref, yt_ref, f_ref, dst, eye, low)


def second_kernel(
    k1_ref, k2_ref, k4_ref, p1_ref, p2_ref, p3_ref, ma_ref, mb_ref, ka_ref, kb_ref, s1_ref, s2_ref, *, bound, roles
):
    eye, low = square_masks()
    add_message(s2_ref, k2_ref, p1_ref, bound, eye, low)
    add_message(s1_ref, k1_ref, p2_ref, bound, eye, low)
    add_message(kb_ref, k4_ref, p3_ref, bound, eye, low)
    first = roles()[5] == 1
    encode(lambda r, c: jnp.where(first, s1_ref[r, c], s2_ref[r, c]), ma_ref, bound, eye, low)
    encode(reader(kb_ref), mb_ref, bound, eye, low)
    ka_ref[...] = jnp.where(first, s2_ref[...], s1_ref[...])


def third_kernel(ka_ref, kb_ref, p4_ref, p5_ref, msg_ref, keep_ref, sa_ref, sb_ref, *, bound, roles):
    eye, low = square_masks()
    add_message(sa_ref, ka_ref, p4_ref, bound, eye, low)
    add_message(sb_ref, kb_ref, p5_ref, bound, eye, low)
    upper = roles()[6] == 1
    encode(lambda r, c: jnp.where(upper, sa_ref[r, c], sb_ref[r, c]), msg_ref, bound, eye, low)
    keep_ref[...] = jnp.where(upper, sb_ref[...], sa_ref[...])


def sublane(x, p):
    return jnp.broadcast_to(x[p : p + 1, :], (TILE, LANES))


def tree(terms):
    terms = list(terms)
    while len(terms) > 1:
        terms = [terms[i] + terms[i + 1] if i + 1 < len(terms) else terms[i] for i in range(0, len(terms), 2)]
    return terms[0]


def invert_pair(tiles):
    lane, sub = iota((TILE, LANES), 1), iota((TILE, LANES), 0)
    col = lane % HALF
    half = lane - col
    here = [sub == p for p in range(TILE)]
    count = len(tiles)
    for g in range(count):
        inside = (col >= g * TILE) & (col < (g + 1) * TILE)
        index = [half + (g * TILE + q) for q in range(TILE)]

        def spread(t, q):
            return jnp.take_along_axis(t, index[q], axis=1)

        others = [(g + 1) % count] + [i for i in range(count) if i != g and i != (g + 1) % count]
        lanes = [[None] * TILE for _ in range(count)]
        for q in range(TILE):
            for i in [g] + others:
                lanes[i][q] = spread(tiles[i], q)
        c = list(lanes[g])
        r = jnp.where(inside, jnp.where(col - g * TILE == sub, 1.0, 0.0), tiles[g])
        for p in range(0, TILE, 2):
            cp, cn = c[p], c[p + 1]
            a, b, d = sublane(cp, p), sublane(cp, p + 1), sublane(cn, p + 1)
            inv = 1.0 / (a * d - b * b)

            def eliminate(x):
                e0, e1 = sublane(x, p), sublane(x, p + 1)
                f0, f1 = d * e0 - b * e1, a * e1 - b * e0
                return jnp.where(here[p], f0 * inv, jnp.where(here[p + 1], f1 * inv, x - (cp * f0 + cn * f1) * inv))

            for q in range(p + 2, TILE):
                c[q] = eliminate(c[q])
            r = eliminate(r)
        rows = [sublane(r, p) for p in range(TILE)]
        for i in others:
            tiles[i] = jnp.where(inside, 0.0, tiles[i]) - tree([lanes[i][p] * rows[p] for p in range(TILE)])
        tiles[g] = r
        yield


def block_diagonal(t):
    left = iota(t.shape, 1) < HALF
    zero = jnp.zeros_like(t)
    return jnp.concatenate([jnp.where(left, t, zero), jnp.where(left, zero, t)], axis=0)


def parts(x):
    high = x.astype(bf16)
    return high, (x - high.astype(f32)).astype(bf16)


def left4(p):
    return jnp.concatenate(p, axis=1)


def rows4(p):
    return jnp.concatenate([jnp.concatenate([q, q], axis=1) for q in p], axis=0)


def cols4(p):
    return jnp.concatenate([jnp.concatenate([q, q], axis=0) for q in p], axis=1)


def fold_halves(r):
    half = r.shape[1] // 2
    return r[:, :half] + r[:, half:]


def mm4(a, b):
    return fold_halves(lax.dot_general(a, b, (((1,), (0,)), ((), ())), preferred_element_type=f32))


def nt4(a, b):
    return fold_halves(nt(a, b))


def factor_solve(n, shift, m_ref, w_ref, x_ref):
    blocks, groups = n // HALF, HALF // TILE

    def begin(b):
        top = m_ref[b * HALF : (b + 1) * HALF, b * LANES : (b + 1) * LANES] + shift
        tiles = [top[i * TILE : (i + 1) * TILE] for i in range(groups)]
        return tiles, invert_pair(tiles)

    def run(steps, work):
        done = 0
        for g in range(groups):
            next(steps)
            todo = len(work) * (g + 1) // groups
            for k in range(done, todo):
                work[k]()
            done = todo
        for _ in steps:
            pass

    tiles, steps = begin(0)
    run(steps, [])
    for b in range(blocks):
        cs, nx = slice(b * LANES, (b + 1) * LANES), (b + 1) * HALF
        inverse = cols4(parts(block_diagonal(jnp.concatenate(tiles, axis=0))))
        panel = parts(m_ref[nx:, cs])
        left = left4(panel)
        first = HALF if nx < n else 8
        w0 = mm4(left[:first], inverse)
        w_ref[nx : nx + first, cs] = w0
        if nx >= n:
            break

        def right(j):
            lo = (j - b - 1) * HALF
            return rows4([block_diagonal(p[lo : lo + HALF]) for p in panel])

        js = slice((b + 1) * LANES, (b + 2) * LANES)
        m_ref[nx : nx + HALF, js] = m_ref[nx : nx + HALF, js] - nt4(left4(parts(w0)), right(b + 1))
        tiles, steps = begin(b + 1)
        kept = {}

        def rest():
            w = mm4(left[HALF:], inverse)
            w_ref[nx + HALF :, cs] = w
            kept["w"] = left4(parts(w))

        def trail(j):
            def go():
                jc, r0 = slice(j * LANES, (j + 1) * LANES), max(j * HALF, nx + HALF)
                m_ref[r0:, jc] = m_ref[r0:, jc] - nt4(kept["w"][r0 - nx - HALF :], right(j))

            return go

        run(steps, [rest] + [trail(j) for j in range(b + 1, blocks)])
    for b in reversed(range(blocks)):
        cs = slice(b * LANES, (b + 1) * LANES)
        x = w_ref[n:, cs]
        if b + 1 < blocks:
            below = [
                jnp.concatenate([block_diagonal(p[i * HALF : (i + 1) * HALF]) for i in range(blocks - b - 1)], axis=0)
                for p in parts(w_ref[(b + 1) * HALF : n, cs])
            ]
            x = x - mm4(left4(parts(x_ref[:, (b + 1) * LANES :])), cols4(below))
        x_ref[:, cs] = x


def solve_kernel(lambda_ref, k_ref, p_ref, o_ref, m_ref, w_ref, x_ref, *, bound, total):
    eye, low = square_masks()
    matrix, rest = decode(p_ref, bound, eye, low)
    n = BLOCK

    def put(rows, t, c):
        u = pltpu.roll(t, HALF, 1)
        left = iota(t.shape, 1) < HALF
        m_ref[rows, 2 * c * LANES : (2 * c + 1) * LANES] = jnp.where(left, t, u)
        m_ref[rows, (2 * c + 1) * LANES : (2 * c + 2) * LANES] = jnp.where(left, u, t)

    xy, extra = rest()
    diag = split(k_ref[264:265, :] + extra)
    for r in range(2):
        for c in range(4):
            i, j = LAYOUT[r][c]
            t = k_ref[place(r, c)] + matrix(r, c)
            if (r, c) in ((0, 0), (0, 2)):
                u = t.T
                put(place(i, 0)[0], jnp.where(eye, diag[i], jnp.where(low, t, u)), i)
                put(place(j, 0)[0], jnp.where(eye, diag[j], jnp.where(low, u, t)), j)
            else:
                put(place(i, 0)[0], t, j)
    right = k_ref[256:264, :] + xy
    for c in range(4):
        put(slice(n, n + 8), right[:, c * LANES : (c + 1) * LANES], c)

    lane, sub = iota((HALF, LANES), 1), iota((HALF, LANES), 0)
    shift = jnp.where(lane % HALF == sub, jnp.where(lane < HALF, lambda_ref[0:1, 0:1] * total, lambda_ref[0:1, 1:2] * total), 0.0)
    factor_solve(n, shift, m_ref, w_ref, x_ref)
    left = iota((8, LANES), 1) < HALF
    for c in range(4):
        even, odd = x_ref[:, 2 * c * LANES : (2 * c + 1) * LANES], x_ref[:, (2 * c + 1) * LANES : (2 * c + 2) * LANES]
        first = jnp.where(left, even, pltpu.roll(odd, HALF, 1))
        second = jnp.where(left, pltpu.roll(even, HALF, 1), odd)
        both = jnp.concatenate([first, second], axis=0).astype(bf16)
        for d in range(o_ref.shape[0]):
            o_ref[d, :, c * LANES : (c + 1) * LANES] = both


def predict_kernel(x_ref, b_ref, f_ref, o_ref, *, scale, roles):
    info = roles()
    weights = jnp.concatenate([b_ref[info[7 + k]] for k in range(FOLDS)], axis=0)
    fitted = nt(weights, x_ref[...])
    folds = f_ref[...]
    total = jnp.zeros((16, folds.shape[1]), f32)
    for k in range(FOLDS):
        total = jnp.where(folds == k, fitted[16 * k : 16 * (k + 1)], total)
    o_ref[...] = (total * scale).astype(bf16)


def cross_kernel(o_ref, j_ref, g_ref, c_ref, *, scale):
    own = o_ref[...]
    count, width = g_ref.shape[0], g_ref.shape[2]
    prior = g_ref.shape[1] // 8
    old = tree([nt(own[:, b * width : (b + 1) * width], g_ref[b]) for b in range(count)])
    new = nt(own, j_ref[...])
    t_row, t_old = iota(old.shape, 0) % 8, iota(old.shape, 1) // prior
    t_new = iota(new.shape, 1) % 8
    old = jnp.where(t_row == t_old, old, 0.0)
    new = jnp.where(iota(new.shape, 0) % 8 == t_new, new, 0.0)
    pick_old = jnp.where(iota((prior, old.shape[1]), 1) % prior == iota((prior, old.shape[1]), 0), 1.0, 0.0)
    features = new.shape[1] // 8
    pick_new = jnp.where(iota((features, new.shape[1]), 1) // 8 == iota((features, new.shape[1]), 0), 1.0, 0.0)
    high = lax.Precision.HIGHEST
    both = jnp.concatenate([nt(pick_old, old, high), nt(pick_new, new, high)], axis=0) * scale
    share = (prior + features) // c_ref.shape[0]
    for j in range(2):
        for d in range(c_ref.shape[0]):
            c_ref[d, j] = both[d * share : (d + 1) * share, 8 * j : 8 * (j + 1)]


def make_local(mesh):
    n_blk, n_smp = mesh.shape["blk"], mesh.shape["smp"]
    if n_smp != 8:
        raise NotImplementedError(n_smp)

    def pairs(bit, sends):
        out = []
        for b in range(n_blk):
            for s in range(n_smp):
                role = s ^ (7 if b & 1 else 0)
                if sends(role & 1, role >> 1 & 1, role >> 2):
                    out.append((b * n_smp + s, b * n_smp + (s ^ bit)))
        return out

    def move(x, bit, sends):
        return lax.ppermute(x, ("blk", "smp"), pairs(bit, sends))

    def local(x, traits, folds, lambdas, guesses):
        rows = x.shape[0]
        total = rows * n_smp
        bound = BOUND * total
        yt = traits.T
        f_row = folds.reshape(1, rows)
        prior = jnp.transpose(guesses[0], (1, 2, 0)).reshape(-1, guesses.shape[1])

        def call(kernel, outs, specs, scratch, *args, mib=12, flops=0, **static):
            import functools

            return pl.pallas_call(
                functools.partial(kernel, **static),
                out_shape=outs,
                in_specs=specs,
                out_specs=jax.tree.map(lambda _: VMEM, outs),
                scratch_shapes=scratch,
                compiler_params=pltpu.CompilerParams(vmem_limit_bytes=mib * MIB),
                cost_estimate=pl.CostEstimate(flops=flops, bytes_accessed=4 * MIB, transcendentals=0),
            )(*args)

        def packed(*lead):
            return jax.ShapeDtypeStruct((*lead, PACKED, BLOCK), f32)

        def wire(*lead):
            return jax.ShapeDtypeStruct((*lead, WIRE, BLOCK), jnp.int16)

        def roles():
            mirror = 7 * (lax.axis_index("blk") & 1)
            role = lax.axis_index("smp") ^ mirror
            b0, b1, b2 = role & 1, role >> 1 & 1, role >> 2
            return [2 - 2 * b0, 1, 2 * b0, 4 - b1, 3 + b1, jnp.where(b0 == b1, 1, 0), b2] + [o ^ mirror for o in OWNERS]

        work = pltpu.VMEM((PACKED, BLOCK), f32)
        xt = pltpu.VMEM((BLOCK, rows), bf16)
        chunks = 4
        gram_flops = 2 * rows * BLOCK * BLOCK
        m0, x_near, yt_near, f_near = call(
            gram_first_kernel,
            (
                wire(),
                jax.ShapeDtypeStruct(x.shape, bf16),
                jax.ShapeDtypeStruct((16, rows), bf16),
                jax.ShapeDtypeStruct((1, rows), jnp.int32),
            ),
            [HBM] * 3,
            [work, xt, pltpu.VMEM(yt.shape, bf16), pltpu.SemaphoreType.DMA((chunks + 2,))],
            *(pltpu.with_memory_space_constraint(v, pltpu.HBM) for v in (x, yt, f_row)),
            bound=bound,
            roles=roles,
            chunks=chunks,
            mib=14,
            flops=gram_flops,
        )
        p1 = move(m0, 1, lambda u, v, w: True)
        m1, m3, k1 = call(
            gram_send_kernel,
            (wire(), wire(), packed()),
            [VMEM, VMEM, VMEM],
            [work, xt],
            x_near,
            yt_near,
            f_near,
            bound=bound,
            roles=roles,
            mib=14,
            flops=2 * gram_flops,
        )
        p3 = move(m3, 2, lambda u, v, w: True)
        p2 = move(m1, 1, lambda u, v, w: u == 1)
        k2, k4 = call(
            gram_keep_kernel, (packed(), packed()), [VMEM] * 3, [xt], x_near, yt_near, f_near, roles=roles, mib=14, flops=2 * gram_flops
        )
        ma, mb, ka, kb = call(
            second_kernel,
            (wire(), wire(), packed(), packed()),
            [VMEM] * 6,
            [work, work],
            k1,
            k2,
            k4,
            p1,
            p2,
            p3,
            bound=bound,
            roles=roles,
        )
        early, ma, mb = lax.optimization_barrier((prior, ma, mb))
        p4 = move(ma, 2, lambda u, v, w: (u, v) != (1, 1))
        p5 = move(mb, 1, lambda u, v, w: u == 1)
        prior_all = lax.all_gather(early, "blk", axis=0)
        prior_all, p4 = lax.optimization_barrier((prior_all, p4))
        msg, keep = call(
            third_kernel, (wire(), packed()), [VMEM] * 4, [work, work], ka, kb, p4, p5, bound=bound, roles=roles
        )
        p6 = move(msg, 4, lambda u, v, w: u == 0 or (u, v, w) == (1, 1, 1))
        beta = call(
            solve_kernel,
            jax.ShapeDtypeStruct((n_smp, 16, BLOCK), bf16),
            [VMEM, VMEM, VMEM],
            [pltpu.VMEM((BLOCK + 8, 2 * BLOCK), f32), pltpu.VMEM((BLOCK + 8, 2 * BLOCK), f32), pltpu.VMEM((8, 2 * BLOCK), f32)],
            lambdas.reshape(1, -1),
            keep,
            p6,
            bound=bound,
            total=float(total),
        )
        betas = lax.all_to_all(beta, "smp", 0, 0)
        oof = call(
            predict_kernel,
            jax.ShapeDtypeStruct((16, rows), bf16),
            [VMEM, VMEM, VMEM],
            [],
            x_near,
            betas,
            f_near,
            scale=math.sqrt(total / BLOCK),
            roles=roles,
        )
        oof_all = lax.all_gather(oof, "blk", axis=0, tiled=True)
        n_cross = prior.shape[0] // 8 + 2 * n_blk
        part = call(
            cross_kernel,
            jax.ShapeDtypeStruct((n_smp, 2, n_cross // n_smp, 8), f32),
            [VMEM] * 3,
            [],
            oof,
            oof_all,
            prior_all,
            scale=1.0 / total,
        )
        cross = jnp.sum(lax.all_to_all(part, "smp", 0, 0), axis=0)
        return (
            jnp.transpose(oof.reshape(2, 8, rows), (2, 1, 0)),
            jnp.transpose(cross, (2, 0, 1)),
        )

    return local


def solution(mesh):
    return jax.shard_map(
        make_local(mesh),
        mesh=mesh,
        in_specs=(P("smp", "blk"), P("smp", None), P("smp"), P(), P("smp", "blk", None, None)),
        out_specs=(P("smp", None, "blk"), P(None, "blk", "smp")),
        check_vma=False,
    )
```

```python
import math

import jax
import jax.numpy as jnp
from jax import lax
from jax.experimental import pallas as pl
from jax.experimental.pallas import tpu as pltpu
from jax.sharding import PartitionSpec as P

BLOCK = 512
FOLDS = 5

LANES = 128
TILE = 8
HALF = 64
PACKED = 272
WIRE = 272
DIGIT = 32766.0
BOUND = 36.0
OWNERS = (0, 2, 3, 4, 6)

f32 = jnp.float32
bf16 = jnp.bfloat16
VMEM = pl.BlockSpec(memory_space=pltpu.VMEM)
HBM = pl.BlockSpec(memory_space=pltpu.HBM)
MIB = 1024 * 1024


def nt(a, b, precision=None):
    return lax.dot_general(a, b, (((1,), (1,)), ((), ())), precision=precision, preferred_element_type=f32)


def iota(shape, dim):
    return lax.broadcasted_iota(jnp.int32, shape, dim)


def square_masks():
    row, col = iota((LANES, LANES), 0), iota((LANES, LANES), 1)
    return row == col, col < row


def column(row_vector, eye):
    return jnp.sum(jnp.where(eye, jnp.broadcast_to(row_vector, (LANES, LANES)), 0.0), axis=1, keepdims=True)


LAYOUT = (((0, 1), (1, 0), (2, 3), (3, 2)), ((2, 0), (2, 1), (3, 0), (3, 1)))


def place(r, c):
    return slice(r * LANES, (r + 1) * LANES), slice(c * LANES, (c + 1) * LANES)


def pair_scale(r, c, rows, cols, low):
    i, j = LAYOUT[r][c]
    if (r, c) in ((0, 0), (0, 2)):
        return jnp.where(low, cols[i] * rows[i], cols[j] * rows[j])
    return cols[i] * rows[j]


def split(vector):
    return [vector[:, i * LANES : (i + 1) * LANES] for i in range(BLOCK // LANES)]


def to_int(x):
    return jnp.floor(x + 0.5).astype(jnp.int32).astype(jnp.int16)


def digits(value, bound):
    u = value * (DIGIT / bound)
    high = jnp.floor(u)
    return high, (u - high) * DIGIT


def undigits(high, low, bound):
    return (high + low * (1.0 / DIGIT)) * (bound / DIGIT)


def encode(get, msg_ref, bound, eye, low):
    diag = get(slice(264, 265), slice(0, BLOCK))
    dh, dl = digits(diag, bound)
    dl = jnp.floor(dl + 0.5)
    scale = lax.rsqrt(undigits(dh, dl, bound) + 1e-3)
    rows = split(scale)
    cols = [column(r, eye) for r in rows]
    for r in range(2):
        for c in range(4):
            rs, cs = place(r, c)
            msg_ref[rs, cs] = to_int(get(rs, cs) * (pair_scale(r, c, rows, cols, low) * DIGIT))
    xy = get(slice(256, 264), slice(0, BLOCK)) * scale
    mh, ml = digits(jnp.max(jnp.abs(xy), axis=1, keepdims=True), bound)
    ml = jnp.floor(ml + 0.5)
    xy = xy * (DIGIT / (undigits(mh, ml, bound) + 1e-2))
    wide = [jnp.broadcast_to(v, (TILE, LANES)) for v in (mh, ml)]
    deep = [jnp.concatenate([*split(v), jnp.zeros((4, LANES), f32)], axis=0) for v in (dh, dl)]
    msg_ref[256:272, :] = to_int(jnp.concatenate([xy, jnp.concatenate(wide + deep, axis=1)], axis=0))


def decode(msg_ref, bound, eye, low):
    tail = msg_ref[256:272, :].astype(f32)
    top = undigits(tail[8:16, 0:LANES], tail[8:16, LANES : 2 * LANES], bound)
    deep = undigits(tail[8:12, 2 * LANES : 3 * LANES], tail[8:12, 3 * LANES : 4 * LANES], bound)
    diag = jnp.concatenate([deep[i : i + 1] for i in range(4)], axis=1)
    scale = jnp.sqrt(diag + 1e-3)
    rows = split(scale)
    cols = [column(r, eye) for r in rows]

    def matrix(r, c):
        rs, cs = place(r, c)
        return msg_ref[rs, cs].astype(f32) * (pair_scale(r, c, rows, cols, low) * (1.0 / DIGIT))

    def rest():
        return tail[0:8] * ((top[:, 0:1] + 1e-2) * (1.0 / DIGIT)) * scale, diag

    return matrix, rest


def add_message(dst_ref, src_ref, msg_ref, bound, eye, low):
    matrix, rest = decode(msg_ref, bound, eye, low)
    for r in range(2):
        for c in range(4):
            rs, cs = place(r, c)
            dst_ref[rs, cs] = src_ref[rs, cs] + matrix(r, c)
    xy, diag = rest()
    dst_ref[256:264, :] = src_ref[256:264, :] + xy
    dst_ref[264:272, :] = src_ref[264:272, :] + jnp.concatenate([diag, jnp.zeros((7, BLOCK), f32)], axis=0)


def reader(ref):
    return lambda rows, cols: ref[rows, cols]


def gram_one(fold, x_ref, xt_ref, yt_ref, f_ref, out_ref, eye, low):
    mask = jnp.where(f_ref[...] != fold, 1.0, 0.0).astype(bf16)
    g0 = jnp.dot(xt_ref[0:256, :] * mask, x_ref[:, 0:256], preferred_element_type=f32)
    lower = jnp.concatenate([xt_ref[256:BLOCK, :], yt_ref[...]], axis=0)
    g1 = jnp.dot(lower * mask, x_ref[...], preferred_element_type=f32)

    def block(i, j):
        rs, cs = place(i, j)
        return g0[rs, cs] if i < 2 else g1[(i - 2) * LANES : (i - 1) * LANES, cs]

    for r in range(2):
        for c in range(4):
            i, j = LAYOUT[r][c]
            rs, cs = place(r, c)
            if (r, c) in ((0, 0), (0, 2)):
                out_ref[rs, cs] = jnp.where(low, block(i, i), jnp.where(eye, 0.0, block(j, j)))
            else:
                out_ref[rs, cs] = block(i, j)
    diag = [jnp.sum(jnp.where(eye, block(i, i), 0.0), axis=0, keepdims=True) for i in range(4)]
    out_ref[256:264, :] = g1[256:264, :]
    out_ref[264:272, :] = jnp.concatenate([jnp.concatenate(diag, axis=1), jnp.zeros((7, BLOCK), f32)], axis=0)


def gram_first_kernel(
    x_hbm, yt_hbm, f_hbm, msg_ref, x_ref, yt_ref, f_ref, work_ref, xt_ref, in_ref, sems, *, bound, roles, chunks
):
    rows = x_ref.shape[0] // chunks
    small = [pltpu.make_async_copy(yt_hbm, in_ref, sems.at[chunks]), pltpu.make_async_copy(f_hbm, f_ref, sems.at[chunks + 1])]
    loads = []
    for c in range(chunks):
        part = pl.ds(c * rows, rows)
        loads.append(pltpu.make_async_copy(x_hbm.at[part], x_ref.at[part], sems.at[c]))
    for copy in loads + small:
        copy.start()
    eye, low = square_masks()
    for c, copy in enumerate(loads):
        copy.wait()
        part = slice(c * rows, (c + 1) * rows)
        xt_ref[:, part] = x_ref[part, :].T
    for copy in small:
        copy.wait()
    yt_ref[...] = jnp.concatenate([in_ref[...], jnp.zeros_like(in_ref[...])], axis=0)
    gram_one(roles()[0], x_ref, xt_ref, yt_ref, f_ref, work_ref, eye, low)
    encode(reader(work_ref), msg_ref, bound, eye, low)


def gram_send_kernel(x_ref, yt_ref, f_ref, m1_ref, m3_ref, keep_ref, work_ref, xt_ref, *, bound, roles):
    eye, low = square_masks()
    info = roles()
    xt_ref[...] = x_ref[...].T
    for slot, dst, msg_ref in ((3, work_ref, m3_ref), (1, keep_ref, m1_ref)):
        gram_one(info[slot], x_ref, xt_ref, yt_ref, f_ref, dst, eye, low)
        encode(reader(dst), msg_ref, bound, eye, low)


def gram_keep_kernel(x_ref, yt_ref, f_ref, k2_ref, k4_ref, xt_ref, *, roles):
    eye, low = square_masks()
    info = roles()
    xt_ref[...] = x_ref[...].T
    for slot, dst in ((2, k2_ref), (4, k4_ref)):
        gram_one(info[slot], x_ref, xt_ref, yt_ref, f_ref, dst, eye, low)


def second_kernel(
    k1_ref, k2_ref, k4_ref, p1_ref, p2_ref, p3_ref, ma_ref, mb_ref, ka_ref, kb_ref, s1_ref, s2_ref, *, bound, roles
):
    eye, low = square_masks()
    add_message(s2_ref, k2_ref, p1_ref, bound, eye, low)
    add_message(s1_ref, k1_ref, p2_ref, bound, eye, low)
    add_message(kb_ref, k4_ref, p3_ref, bound, eye, low)
    first = roles()[5] == 1
    encode(lambda r, c: jnp.where(first, s1_ref[r, c], s2_ref[r, c]), ma_ref, bound, eye, low)
    encode(reader(kb_ref), mb_ref, bound, eye, low)
    ka_ref[...] = jnp.where(first, s2_ref[...], s1_ref[...])


def third_kernel(ka_ref, kb_ref, p4_ref, p5_ref, msg_ref, keep_ref, sa_ref, sb_ref, *, bound, roles):
    eye, low = square_masks()
    add_message(sa_ref, ka_ref, p4_ref, bound, eye, low)
    add_message(sb_ref, kb_ref, p5_ref, bound, eye, low)
    upper = roles()[6] == 1
    encode(lambda r, c: jnp.where(upper, sa_ref[r, c], sb_ref[r, c]), msg_ref, bound, eye, low)
    keep_ref[...] = jnp.where(upper, sb_ref[...], sa_ref[...])


def sublane(x, p):
    return jnp.broadcast_to(x[p : p + 1, :], (TILE, LANES))


def tree(terms):
    terms = list(terms)
    while len(terms) > 1:
        terms = [terms[i] + terms[i + 1] if i + 1 < len(terms) else terms[i] for i in range(0, len(terms), 2)]
    return terms[0]


def invert_pair(tiles):
    lane, sub = iota((TILE, LANES), 1), iota((TILE, LANES), 0)
    col = lane % HALF
    half = lane - col
    here = [sub == p for p in range(TILE)]
    count = len(tiles)
    for g in range(count):
        inside = (col >= g * TILE) & (col < (g + 1) * TILE)
        index = [half + (g * TILE + q) for q in range(TILE)]

        def spread(t, q):
            return jnp.take_along_axis(t, index[q], axis=1)

        others = [(g + 1) % count] + [i for i in range(count) if i != g and i != (g + 1) % count]
        lanes = [[None] * TILE for _ in range(count)]
        for q in range(TILE):
            for i in [g] + others:
                lanes[i][q] = spread(tiles[i], q)
        c = list(lanes[g])
        r = jnp.where(inside, jnp.where(col - g * TILE == sub, 1.0, 0.0), tiles[g])
        for p in range(0, TILE, 2):
            cp, cn = c[p], c[p + 1]
            a, b, d = sublane(cp, p), sublane(cp, p + 1), sublane(cn, p + 1)
            inv = 1.0 / (a * d - b * b)

            def eliminate(x):
                e0, e1 = sublane(x, p), sublane(x, p + 1)
                f0, f1 = d * e0 - b * e1, a * e1 - b * e0
                return jnp.where(here[p], f0 * inv, jnp.where(here[p + 1], f1 * inv, x - (cp * f0 + cn * f1) * inv))

            for q in range(p + 2, TILE):
                c[q] = eliminate(c[q])
            r = eliminate(r)
        rows = [sublane(r, p) for p in range(TILE)]
        for i in others:
            tiles[i] = jnp.where(inside, 0.0, tiles[i]) - tree([lanes[i][p] * rows[p] for p in range(TILE)])
        tiles[g] = r
        yield


def block_diagonal(t):
    left = iota(t.shape, 1) < HALF
    zero = jnp.zeros_like(t)
    return jnp.concatenate([jnp.where(left, t, zero), jnp.where(left, zero, t)], axis=0)


def parts(x):
    high = x.astype(bf16)
    return high, (x - high.astype(f32)).astype(bf16)


def left4(p):
    return jnp.concatenate(p, axis=1)


def rows4(p):
    return jnp.concatenate([jnp.concatenate([q, q], axis=1) for q in p], axis=0)


def cols4(p):
    return jnp.concatenate([jnp.concatenate([q, q], axis=0) for q in p], axis=1)


def fold_halves(r):
    half = r.shape[1] // 2
    return r[:, :half] + r[:, half:]


def mm4(a, b):
    return fold_halves(lax.dot_general(a, b, (((1,), (0,)), ((), ())), preferred_element_type=f32))


def nt4(a, b):
    return fold_halves(nt(a, b))


def factor_solve(n, shift, m_ref, w_ref, x_ref):
    blocks, groups = n // HALF, HALF // TILE

    def begin(b):
        top = m_ref[b * HALF : (b + 1) * HALF, b * LANES : (b + 1) * LANES] + shift
        tiles = [top[i * TILE : (i + 1) * TILE] for i in range(groups)]
        return tiles, invert_pair(tiles)

    def run(steps, work):
        done = 0
        for g in range(groups):
            next(steps)
            todo = len(work) * (g + 1) // groups
            for k in range(done, todo):
                work[k]()
            done = todo
        for _ in steps:
            pass

    tiles, steps = begin(0)
    run(steps, [])
    for b in range(blocks):
        cs, nx = slice(b * LANES, (b + 1) * LANES), (b + 1) * HALF
        inverse = cols4(parts(block_diagonal(jnp.concatenate(tiles, axis=0))))
        panel = parts(m_ref[nx:, cs])
        left = left4(panel)
        first = HALF if nx < n else 8
        w0 = mm4(left[:first], inverse)
        w_ref[nx : nx + first, cs] = w0
        if nx >= n:
            break

        def right(j):
            lo = (j - b - 1) * HALF
            return rows4([block_diagonal(p[lo : lo + HALF]) for p in panel])

        js = slice((b + 1) * LANES, (b + 2) * LANES)
        m_ref[nx : nx + HALF, js] = m_ref[nx : nx + HALF, js] - nt4(left4(parts(w0)), right(b + 1))
        tiles, steps = begin(b + 1)
        kept = {}

        def rest():
            w = mm4(left[HALF:], inverse)
            w_ref[nx + HALF :, cs] = w
            kept["w"] = left4(parts(w))

        def trail(j):
            def go():
                jc, r0 = slice(j * LANES, (j + 1) * LANES), max(j * HALF, nx + HALF)
                m_ref[r0:, jc] = m_ref[r0:, jc] - nt4(kept["w"][r0 - nx - HALF :], right(j))

            return go

        run(steps, [rest] + [trail(j) for j in range(b + 1, blocks)])
    for b in reversed(range(blocks)):
        cs = slice(b * LANES, (b + 1) * LANES)
        x = w_ref[n:, cs]
        if b + 1 < blocks:
            below = [
                jnp.concatenate([block_diagonal(p[i * HALF : (i + 1) * HALF]) for i in range(blocks - b - 1)], axis=0)
                for p in parts(w_ref[(b + 1) * HALF : n, cs])
            ]
            x = x - mm4(left4(parts(x_ref[:, (b + 1) * LANES :])), cols4(below))
        x_ref[:, cs] = x


def solve_kernel(lambda_ref, k_ref, p_ref, o_ref, m_ref, w_ref, x_ref, *, bound, total):
    eye, low = square_masks()
    matrix, rest = decode(p_ref, bound, eye, low)
    n = BLOCK

    def put(rows, t, c):
        u = pltpu.roll(t, HALF, 1)
        left = iota(t.shape, 1) < HALF
        m_ref[rows, 2 * c * LANES : (2 * c + 1) * LANES] = jnp.where(left, t, u)
        m_ref[rows, (2 * c + 1) * LANES : (2 * c + 2) * LANES] = jnp.where(left, u, t)

    xy, extra = rest()
    diag = split(k_ref[264:265, :] + extra)
    for r in range(2):
        for c in range(4):
            i, j = LAYOUT[r][c]
            t = k_ref[place(r, c)] + matrix(r, c)
            if (r, c) in ((0, 0), (0, 2)):
                u = t.T
                put(place(i, 0)[0], jnp.where(eye, diag[i], jnp.where(low, t, u)), i)
                put(place(j, 0)[0], jnp.where(eye, diag[j], jnp.where(low, u, t)), j)
            else:
                put(place(i, 0)[0], t, j)
    right = k_ref[256:264, :] + xy
    for c in range(4):
        put(slice(n, n + 8), right[:, c * LANES : (c + 1) * LANES], c)

    lane, sub = iota((HALF, LANES), 1), iota((HALF, LANES), 0)
    shift = jnp.where(lane % HALF == sub, jnp.where(lane < HALF, lambda_ref[0:1, 0:1] * total, lambda_ref[0:1, 1:2] * total), 0.0)
    factor_solve(n, shift, m_ref, w_ref, x_ref)
    left = iota((8, LANES), 1) < HALF
    for c in range(4):
        even, odd = x_ref[:, 2 * c * LANES : (2 * c + 1) * LANES], x_ref[:, (2 * c + 1) * LANES : (2 * c + 2) * LANES]
        first = jnp.where(left, even, pltpu.roll(odd, HALF, 1))
        second = jnp.where(left, pltpu.roll(even, HALF, 1), odd)
        both = jnp.concatenate([first, second], axis=0).astype(bf16)
        for d in range(o_ref.shape[0]):
            o_ref[d, :, c * LANES : (c + 1) * LANES] = both


def predict_kernel(x_ref, b_ref, f_ref, o_ref, *, scale, roles):
    info = roles()
    weights = jnp.concatenate([b_ref[info[7 + k]] for k in range(FOLDS)], axis=0)
    fitted = nt(weights, x_ref[...])
    folds = f_ref[...]
    total = jnp.zeros((16, folds.shape[1]), f32)
    for k in range(FOLDS):
        total = jnp.where(folds == k, fitted[16 * k : 16 * (k + 1)], total)
    o_ref[...] = (total * scale).astype(bf16)


def cross_kernel(o_ref, j_ref, g_ref, c_ref, *, scale):
    own = o_ref[...]
    count, width = g_ref.shape[0], g_ref.shape[2]
    prior = g_ref.shape[1] // 8
    old = tree([nt(own[:, b * width : (b + 1) * width], g_ref[b]) for b in range(count)])
    new = nt(own, j_ref[...])
    t_row, t_old = iota(old.shape, 0) % 8, iota(old.shape, 1) // prior
    t_new = iota(new.shape, 1) % 8
    old = jnp.where(t_row == t_old, old, 0.0)
    new = jnp.where(iota(new.shape, 0) % 8 == t_new, new, 0.0)
    features = new.shape[1] // 8
    picked = jnp.concatenate([old, new], axis=1)
    row, col = (iota((prior + features, picked.shape[1]), d) for d in (0, 1))
    wanted = jnp.where(col < old.shape[1], col % prior, prior + (col - old.shape[1]) // 8)
    both = nt(jnp.where(row == wanted, 1.0, 0.0), picked, lax.Precision.HIGHEST) * scale
    share = (prior + features) // c_ref.shape[0]
    for j in range(2):
        for d in range(c_ref.shape[0]):
            c_ref[d, j] = both[d * share : (d + 1) * share, 8 * j : 8 * (j + 1)]


def make_local(mesh):
    n_blk, n_smp = mesh.shape["blk"], mesh.shape["smp"]
    if n_smp != 8:
        raise NotImplementedError(n_smp)

    def pairs(bit, sends):
        out = []
        for b in range(n_blk):
            for s in range(n_smp):
                role = s ^ (7 if b & 1 else 0)
                if sends(role & 1, role >> 1 & 1, role >> 2):
                    out.append((b * n_smp + s, b * n_smp + (s ^ bit)))
        return out

    def move(x, bit, sends):
        return lax.ppermute(x, ("blk", "smp"), pairs(bit, sends))

    def local(x, traits, folds, lambdas, guesses):
        rows = x.shape[0]
        total = rows * n_smp
        bound = BOUND * total
        yt = traits.T
        f_row = folds.reshape(1, rows)
        prior = jnp.transpose(guesses[0], (1, 2, 0)).reshape(-1, guesses.shape[1])

        def call(kernel, outs, specs, scratch, *args, mib=12, flops=0, **static):
            import functools

            return pl.pallas_call(
                functools.partial(kernel, **static),
                out_shape=outs,
                in_specs=specs,
                out_specs=jax.tree.map(lambda _: VMEM, outs),
                scratch_shapes=scratch,
                compiler_params=pltpu.CompilerParams(vmem_limit_bytes=mib * MIB),
                cost_estimate=pl.CostEstimate(flops=flops, bytes_accessed=4 * MIB, transcendentals=0),
            )(*args)

        def packed(*lead):
            return jax.ShapeDtypeStruct((*lead, PACKED, BLOCK), f32)

        def wire(*lead):
            return jax.ShapeDtypeStruct((*lead, WIRE, BLOCK), jnp.int16)

        def roles():
            mirror = 7 * (lax.axis_index("blk") & 1)
            role = lax.axis_index("smp") ^ mirror
            b0, b1, b2 = role & 1, role >> 1 & 1, role >> 2
            return [2 - 2 * b0, 1, 2 * b0, 4 - b1, 3 + b1, jnp.where(b0 == b1, 1, 0), b2] + [o ^ mirror for o in OWNERS]

        work = pltpu.VMEM((PACKED, BLOCK), f32)
        xt = pltpu.VMEM((BLOCK, rows), bf16)
        chunks = 8
        gram_flops = 2 * rows * BLOCK * BLOCK
        m0, x_near, yt_near, f_near = call(
            gram_first_kernel,
            (
                wire(),
                jax.ShapeDtypeStruct(x.shape, bf16),
                jax.ShapeDtypeStruct((16, rows), bf16),
                jax.ShapeDtypeStruct((1, rows), jnp.int32),
            ),
            [HBM] * 3,
            [work, xt, pltpu.VMEM(yt.shape, bf16), pltpu.SemaphoreType.DMA((chunks + 2,))],
            *(pltpu.with_memory_space_constraint(v, pltpu.HBM) for v in (x, yt, f_row)),
            bound=bound,
            roles=roles,
            chunks=chunks,
            mib=14,
            flops=gram_flops,
        )
        p1 = move(m0, 1, lambda u, v, w: True)
        m1, m3, k1 = call(
            gram_send_kernel,
            (wire(), wire(), packed()),
            [VMEM, VMEM, VMEM],
            [work, xt],
            x_near,
            yt_near,
            f_near,
            bound=bound,
            roles=roles,
            mib=14,
            flops=2 * gram_flops,
        )
        p3 = move(m3, 2, lambda u, v, w: True)
        p2 = move(m1, 1, lambda u, v, w: u == 1)
        k2, k4 = call(
            gram_keep_kernel, (packed(), packed()), [VMEM] * 3, [xt], x_near, yt_near, f_near, roles=roles, mib=14, flops=2 * gram_flops
        )
        ma, mb, ka, kb = call(
            second_kernel,
            (wire(), wire(), packed(), packed()),
            [VMEM] * 6,
            [work, work],
            k1,
            k2,
            k4,
            p1,
            p2,
            p3,
            bound=bound,
            roles=roles,
        )
        early, ma, mb = lax.optimization_barrier((prior, ma, mb))
        p4 = move(ma, 2, lambda u, v, w: (u, v) != (1, 1))
        p5 = move(mb, 1, lambda u, v, w: u == 1)
        prior_all = lax.all_gather(early, "blk", axis=0)
        prior_all, p4 = lax.optimization_barrier((prior_all, p4))
        msg, keep = call(
            third_kernel, (wire(), packed()), [VMEM] * 4, [work, work], ka, kb, p4, p5, bound=bound, roles=roles
        )
        p6 = move(msg, 4, lambda u, v, w: u == 0 or (u, v, w) == (1, 1, 1))
        beta = call(
            solve_kernel,
            jax.ShapeDtypeStruct((n_smp, 16, BLOCK), bf16),
            [VMEM, VMEM, VMEM],
            [pltpu.VMEM((BLOCK + 8, 2 * BLOCK), f32), pltpu.VMEM((BLOCK + 8, 2 * BLOCK), f32), pltpu.VMEM((8, 2 * BLOCK), f32)],
            lambdas.reshape(1, -1),
            keep,
            p6,
            bound=bound,
            total=float(total),
        )
        betas = lax.all_to_all(beta, "smp", 0, 0)
        oof = call(
            predict_kernel,
            jax.ShapeDtypeStruct((16, rows), bf16),
            [VMEM, VMEM, VMEM],
            [],
            x_near,
            betas,
            f_near,
            scale=math.sqrt(total / BLOCK),
            roles=roles,
        )
        oof_all = lax.all_gather(oof, "blk", axis=0, tiled=True)
        n_cross = prior.shape[0] // 8 + 2 * n_blk
        part = call(
            cross_kernel,
            jax.ShapeDtypeStruct((n_smp, 2, n_cross // n_smp, 8), f32),
            [VMEM] * 3,
            [],
            oof,
            oof_all,
            prior_all,
            scale=1.0 / total,
        )
        cross = jnp.sum(lax.all_to_all(part, "smp", 0, 0), axis=0)
        return (
            jnp.transpose(oof.reshape(2, 8, rows), (2, 1, 0)),
            jnp.transpose(cross, (2, 0, 1)),
        )

    return local


def solution(mesh):
    return jax.shard_map(
        make_local(mesh),
        mesh=mesh,
        in_specs=(P("smp", "blk"), P("smp", None), P("smp"), P(), P("smp", "blk", None, None)),
        out_specs=(P("smp", None, "blk"), P(None, "blk", "smp")),
        check_vma=False,
    )
```
